32 devices in a mesh: grp: 2 (over y), depth: 4 (over z), shot: 2 (over x), lat: 2 (over core).
Axes of the slice: x: 2, y: 2, z: 4, core: 2. Of those that a mesh axis runs over, the one named last changes fastest.
Arguments:
- fwd_prev: float32 [8, 8, 128, 128], P(('grp', 'shot'), 'depth', 'lat'), parts along dimension 0, may hold values from -6 to 6
- fwd_now: float32 [8, 8, 128, 128], P(('grp', 'shot'), 'depth', 'lat'), parts along dimension 0, may hold values from -6 to 6
- adj_late: float32 [8, 8, 128, 128], P(('grp', 'shot'), 'depth', 'lat'), parts along dimension 0, may hold values from -6 to 6
- adj_last: float32 [8, 8, 128, 128], P(('grp', 'shot'), 'depth', 'lat'), parts along dimension 0, may hold values from -6 to 6
- velocity: float32 [16, 128, 128], P(('grp', 'depth'), 'lat', 'shot'), parts along dimension 0, may hold values from 1.5 to 4.5
- density: float32 [16, 128, 128], P(('grp', 'depth'), 'lat'), parts along dimension 0, may hold values from 1.5 to 2.5
- wavelet: float32 [8, 2], P(('grp', 'shot')), parts along dimension 0, may hold values from -48 to 48
- source_cell: int32 [8], P(('grp', 'shot')), parts along dimension 0, may hold values from 0 to 131071
- receiver_cell: int32 [8, 2048], P(('grp', 'shot')), parts along dimension 0, may hold values from 0 to 131071
- observed: float32 [8, 2, 2048], P(('grp', 'shot')), parts along dimension 0, may hold values from -18 to 18
Outputs:
- updated_velocity: float32 [16, 128, 128], P(('grp', 'depth'), 'lat', 'shot'), parts along dimension 0
- update_direction: float32 [16, 128, 128], P(('grp', 'depth'), 'lat', 'shot'), parts along dimension 0
The draws below stay inside these ranges and needn't reach their ends.
There are 2 independent parts, one for each index of `grp`. The reference program is written for one: setup_inputs(seed, part) draws one part's arguments, and reference() takes and returns one part's arrays. A program takes and returns all parts, laid end to end along the dimension named above; each array names one. Nothing has to cross between parts.
Inputs may be any that keep to these rules, and one draw needn't show every extreme that they name: `source_cell`: a flattened cell index depth * 128 * 128 + x * 128 + y. `receiver_cell`: flattened cell indices depth * 128 * 128 + x * 128 + y; a cell may repeat.
All inputs are finite; a program needn't handle non-finite values. Where the reference program divides by a largest or mean magnitude, that divisor is 1e-20 or more.
Results may differ from the reference program's by a relative error of at most 0.00002.
Values sent between devices are 32-bit elements; how exact they have to be, the bound alone decides.
No kernel may reach another device: no remote copies, remote signals or barrier semaphores. Data moves between devices by JAX's collectives and lax.ppermute only.
A program may use at most 64 MiB of HBM per device.

```python
import jax
import jax.numpy as jnp
from jax import lax

NY = 128
NREC = 2048
STEPS = 2
ITERS = 2
NZ = 8
NX = 128
SHOTS = 4


def place_ends(drawn, own_key, low, high):
    index_at = [jax.random.randint(jax.random.fold_in(own_key, axis), (), 0, length) for axis, length in enumerate(drawn.shape)]
    longest = drawn.shape.index(max(drawn.shape))
    neighbour = index_at[:longest] + [(index_at[longest] + 1) % drawn.shape[longest]] + index_at[longest + 1:]
    return drawn.at[tuple(index_at)].set(low).at[tuple(neighbour)].set(high)


def level_of(own_key, dims, shards, low, top_value):
    gain, own = 1.0, jax.random.fold_in(own_key, 6)
    for position, blocks in shards:
        heights = jnp.exp(jax.random.uniform(jax.random.fold_in(own, position), (blocks,), jnp.float32, low / len(shards), top_value / len(shards)))
        gain = gain * jnp.repeat(heights, dims[position] // blocks).reshape([-1 if axis == position else 1 for axis in range(len(dims))])
    return gain


def normal_values(stream_key, dims, scale, most, pieces=(), kind=jnp.bfloat16):
    array = scale * jax.random.normal(stream_key, dims, jnp.float32)
    if pieces:
        array = array * level_of(stream_key, dims, pieces, -0.22, 0.18)
    return jnp.clip(array, -most, most).astype(kind)


def setup_inputs(seed: int = 0, part: int = 0) -> dict:
    seeds = jax.random.split(jax.random.key(seed), 11)
    part_keys = jax.random.split(jax.random.fold_in(seeds[10], part), 11)
    fwd_prev = normal_values(part_keys[0], (SHOTS, NZ, NX, NY), 1.0, 6.0, ((0, 2), (1, 4), (2, 2)), jnp.float32)
    fwd_now = normal_values(part_keys[1], (SHOTS, NZ, NX, NY), 1.0, 6.0, ((0, 2), (1, 4), (2, 2)), jnp.float32)
    adj_late = normal_values(part_keys[2], (SHOTS, NZ, NX, NY), 1.0, 6.0, ((0, 2), (1, 4), (2, 2)), jnp.float32)
    adj_last = normal_values(part_keys[3], (SHOTS, NZ, NX, NY), 1.0, 6.0, ((0, 2), (1, 4), (2, 2)), jnp.float32)
    velocity = jnp.clip(1.5 + 3.0 * jax.random.uniform(part_keys[4], (NZ, NX, NY), jnp.float32) ** level_of(part_keys[4], (NZ, NX, NY), ((0, 4), (1, 2), (2, 2)), -0.2, 0.2), 1.5, 4.5)
    density = jnp.clip(1.5 + 1.0 * jax.random.uniform(part_keys[5], (NZ, NX, NY), jnp.float32) ** level_of(part_keys[5], (NZ, NX, NY), ((0, 4), (1, 2)), -0.2, 0.2), 1.5, 2.5)
    wavelet = normal_values(part_keys[6], (SHOTS, STEPS), 8.0, 48.0, ((0, 2),), jnp.float32)
    source_cell = place_ends(jax.random.randint(part_keys[7], (SHOTS,), 0, NZ * NX * NY), jax.random.fold_in(part_keys[7], 1), 0, (NZ * NX * NY) - 1).astype(jnp.int32)
    receiver_cell = place_ends(jax.random.randint(part_keys[8], (SHOTS, NREC), 0, NZ * NX * NY), jax.random.fold_in(part_keys[8], 1), 0, (NZ * NX * NY) - 1).astype(jnp.int32)
    observed = normal_values(part_keys[9], (SHOTS, STEPS, NREC), 3.0, 18.0, ((0, 2),), jnp.float32)
    return {"fwd_prev": fwd_prev, "fwd_now": fwd_now, "adj_late": adj_late, "adj_last": adj_last, "velocity": velocity, "density": density, "wavelet": wavelet, "source_cell": source_cell, "receiver_cell": receiver_cell, "observed": observed}


COURANT = 0.1
STEP_SIZE = 0.1
EPSILON = 1e-6
NEIGHBOURS = ((1, 0, 0), (-1, 0, 0), (0, 1, 0), (0, -1, 0), (0, 0, 1), (0, 0, -1))


def pad_cells(cells_array):
    widths = [(0, 0)] * (cells_array.ndim - 3) + [(1, 1)] * 3
    return jnp.pad(cells_array, widths)


def laplace(padded, buoy_pad):
    depth_cells = padded.shape[-3] - 2
    row_cells = padded.shape[-2] - 2
    col_cells = padded.shape[-1] - 2
    center_field = padded[..., 1:-1, 1:-1, 1:-1]
    center_buoy = buoy_pad[1:-1, 1:-1, 1:-1]
    summed = jnp.zeros(center_field.shape, jnp.float32)
    for shift_depth, shift_row, shift_col in NEIGHBOURS:
        near_buoy = buoy_pad[1 + shift_depth:1 + shift_depth + depth_cells, 1 + shift_row:1 + shift_row + row_cells, 1 + shift_col:1 + shift_col + col_cells]
        near_field = padded[..., 1 + shift_depth:1 + shift_depth + depth_cells, 1 + shift_row:1 + shift_row + row_cells, 1 + shift_col:1 + shift_col + col_cells]
        summed = summed + 0.5 * (center_buoy + near_buoy) * (near_field - center_field)
    return summed


def imaging(stiffness, buoy_pad, fwd_prev, fwd_now, adj_late, adj_last, wavelet, source_cell, receiver_cell, observed):
    def per_shot(gradient, shot_inputs):
        wave_prev, wave_now, late_adj, last_adj, amplitude, source_index, receiver_index, recorded = shot_inputs
        laplacians = []
        misfits = []
        for step_index in range(STEPS):
            laplacian = laplace(pad_cells(wave_now), buoy_pad)
            laplacians.append(laplacian)
            wave_next = 2.0 * wave_now - wave_prev + stiffness * laplacian
            flattened = wave_next.reshape(-1).at[source_index].add(amplitude[step_index])
            misfits.append(flattened[receiver_index] - recorded[step_index])
            wave_prev, wave_now = wave_now, flattened.reshape(wave_now.shape)
        for step_index in reversed(range(STEPS)):
            scaled = stiffness * last_adj
            adj_next = 2.0 * last_adj - late_adj + laplace(pad_cells(scaled), buoy_pad)
            adj_next = adj_next.reshape(-1).at[receiver_index].add(misfits[step_index]).reshape(last_adj.shape)
            gradient = gradient + adj_next * stiffness * laplacians[step_index]
            late_adj, last_adj = last_adj, adj_next
        return gradient, None

    start = jnp.zeros(stiffness.shape, jnp.float32)
    gradient, unused = lax.scan(per_shot, start, (fwd_prev, fwd_now, adj_late, adj_last, wavelet, source_cell, receiver_cell, observed))
    return gradient


def reference(fwd_prev, fwd_now, adj_late, adj_last, velocity, density, wavelet, source_cell, receiver_cell, observed):
    buoy_pad = pad_cells(1.0 / density)
    velocity_now = velocity
    direction = jnp.zeros(velocity.shape, jnp.float32)
    for update_index in range(ITERS):
        stiffness = (velocity_now * COURANT) ** 2 * density
        gradient = imaging(stiffness, buoy_pad, fwd_prev, fwd_now, adj_late, adj_last, wavelet, source_cell, receiver_cell, observed)
        largest = jnp.max(jnp.abs(gradient))
        direction = gradient / (largest + EPSILON)
        velocity_now = velocity_now * jnp.exp(-STEP_SIZE * direction)
    return velocity_now, direction
```

```python
import functools

import jax
import jax.numpy as jnp
from jax import lax
from jax.experimental import pallas as pl
from jax.experimental.pallas import tpu as pltpu
from jax.sharding import PartitionSpec as P

ITERS = 2

COURANT = 0.1
STEP_SIZE = 0.1
EPSILON = 1e-06
PAD = 8


def even_pairs(count):
    return [(i, i ^ 1) for i in range(count) if i ^ 1 < count]


def odd_pairs(count):
    ups = [(i, i + 1) for i in range(1, count - 1, 2)]
    return ups + [(b, a) for a, b in ups]


def two_pairs(count, first):
    ups = [(i, i + 2) for i in range(count - 2) if (i % 4 < 2) == first]
    return ups + [(b, a) for a, b in ups]


def send(block, axis, pairs):
    if not pairs:
        return jnp.zeros_like(block)
    return lax.ppermute(block, axis, pairs)


def pack(arrays):
    return jnp.concatenate([a.reshape(-1, a.shape[-1]) for a in arrays], axis=0)


def unpack(packed, shapes):
    out = []
    start = 0
    for shape in shapes:
        rows = 1
        for size in shape[:-1]:
            rows *= size
        out.append(packed[start : start + rows].reshape(shape))
        start += rows
    return out


def split_three(values):
    high = values.astype(jnp.bfloat16)
    rest = values - high.astype(jnp.float32)
    middle = rest.astype(jnp.bfloat16)
    low = (rest - middle.astype(jnp.float32)).astype(jnp.bfloat16)
    return high, middle, low


def spread_kernel(rows, cols, row_ref, col_ref, obs_ref, out_ref):
    nrec = row_ref.shape[-1]
    steps = obs_ref.shape[1]
    row_iota = lax.broadcasted_iota(jnp.int32, (rows, nrec), 0)
    col_iota = lax.broadcasted_iota(jnp.int32, (cols, nrec), 0)
    dims = (((1,), (1,)), ((), ()))
    for shot in range(row_ref.shape[0]):
        at_row = (row_ref[shot] == row_iota).astype(jnp.float32).astype(jnp.bfloat16)
        at_col = col_ref[shot] == col_iota
        ones = at_col.astype(jnp.float32).astype(jnp.bfloat16)
        out_ref[shot, 0] = lax.dot_general(
            at_row, ones, dims, preferred_element_type=jnp.float32
        )
        for step in range(steps):
            obs = obs_ref[shot, step : step + 1, :]
            high = obs.astype(jnp.bfloat16).astype(jnp.float32)
            rest = obs - high
            middle = rest.astype(jnp.bfloat16).astype(jnp.float32)
            low = rest - middle
            total = None
            for part in (high, middle, low):
                term = lax.dot_general(
                    at_row,
                    jnp.where(at_col, part, 0.0).astype(jnp.bfloat16),
                    dims,
                    preferred_element_type=jnp.float32,
                )
                total = term if total is None else total + term
            out_ref[shot, 1 + step] = total


def spread(row_id, col_id, observed, rows, cols):
    shots, nrec = row_id.shape
    steps = observed.shape[1]
    return pl.pallas_call(
        functools.partial(spread_kernel, rows, cols),
        out_shape=jax.ShapeDtypeStruct((shots, 1 + steps, rows, cols), jnp.float32),
        in_specs=[pl.BlockSpec(memory_space=pltpu.VMEM)] * 3,
        out_specs=pl.BlockSpec(memory_space=pltpu.VMEM),
        cost_estimate=pl.CostEstimate(
            flops=2 * shots * (1 + 3 * steps) * rows * cols * nrec,
            bytes_accessed=4 * shots * (1 + steps) * rows * cols,
            transcendentals=0,
        ),
        name="spread",
    )(row_id[:, None, :], col_id[:, None, :], observed)


def laplace(field, buoy):
    planes = field.shape[-3] - 2
    rows, cols = field.shape[-2:]
    wide = [(0, 0)] * (field.ndim - 2) + [(1, 1), (1, 1)]
    field = jnp.pad(field, wide)
    buoy = jnp.pad(buoy, [(0, 0), (1, 1), (1, 1)])
    center_field = field[..., 1:-1, 1:-1, 1:-1]
    center_buoy = buoy[1:-1, 1:-1, 1:-1]
    summed = None
    for dz, dx, dy in ((1, 0, 0), (-1, 0, 0), (0, 1, 0), (0, -1, 0), (0, 0, 1), (0, 0, -1)):
        near_buoy = buoy[1 + dz : 1 + dz + planes, 1 + dx : 1 + dx + rows, 1 + dy : 1 + dy + cols]
        near = field[..., 1 + dz : 1 + dz + planes, 1 + dx : 1 + dx + rows, 1 + dy : 1 + dy + cols]
        term = 0.5 * (center_buoy + near_buoy) * (near - center_field)
        summed = term if summed is None else summed + term
    return summed


def inner(block, cut):
    return block[..., cut : block.shape[-3] - cut, :, :]


def shards(
    fwd_prev,
    fwd_now,
    adj_late,
    adj_last,
    velocity,
    density,
    wavelet,
    source_cell,
    receiver_cell,
    observed,
):
    shots, planes, rows, cols = fwd_now.shape
    depth_count = lax.axis_size("depth")
    shot_count = lax.axis_size("shot")
    lat_count = lax.axis_size("lat")
    if planes != 2 or wavelet.shape[1] != 2 or lat_count != 2:
        raise ValueError("unsupported split")
    depth_at = lax.axis_index("depth")
    lat_at = lax.axis_index("lat")
    shot_at = lax.axis_index("shot")
    even = depth_at % 2 == 0
    front = depth_at % 4 < 2
    own_width = velocity.shape[2]
    evens = even_pairs(depth_count)
    odds = odd_pairs(depth_count)
    swap = [(0, 1), (1, 0)]

    def shot_sum(block):
        if shot_count == 2:
            return block + lax.ppermute(block, "shot", swap)
        return lax.psum(block, "shot")

    def depth_max(value):
        if depth_count & (depth_count - 1):
            return lax.pmax(value, "depth")
        step = 1
        while step < depth_count:
            pairs = [(i, i ^ step) for i in range(depth_count)]
            value = jnp.maximum(value, lax.ppermute(value, "depth", pairs))
            step *= 2
        return value

    if shot_count == 2:
        other = lax.ppermute(velocity, "shot", swap)
        full_velocity = jnp.where(
            shot_at == 0,
            jnp.concatenate([velocity, other], axis=2),
            jnp.concatenate([other, velocity], axis=2),
        )
    else:
        full_velocity = lax.all_gather(velocity, "shot", axis=2, tiled=True)

    near_shapes = [fwd_now.shape, fwd_prev.shape, adj_last.shape, density.shape, (shots, 1, rows, cols)]
    top_late = adj_late[:, planes - 1 :]
    low_late = adj_late[:, :1]
    common = [fwd_now, fwd_prev, adj_last, density]
    by_even = send(pack(common + [jnp.where(even, top_late, low_late)]), "depth", evens)
    by_odd = send(pack(common + [jnp.where(even, low_late, top_late)]), "depth", odds)
    up = unpack(jnp.where(even, by_even, by_odd), near_shapes)
    low = unpack(jnp.where(even, by_odd, by_even), near_shapes)
    far_shapes = [(shots, 1, rows, cols), (1, rows, cols)]
    top_far = pack([fwd_now[:, planes - 1 :], density[planes - 1 :]])
    low_far = pack([fwd_now[:, :1], density[:1]])
    by_first = send(jnp.where(front, top_far, low_far), "depth", two_pairs(depth_count, True))
    by_second = send(jnp.where(front, low_far, top_far), "depth", two_pairs(depth_count, False))
    far_up = unpack(jnp.where(front, by_first, by_second), far_shapes)
    far_low = unpack(jnp.where(front, by_second, by_first), far_shapes)
    vel_even = send(full_velocity, "depth", evens)
    vel_odd = send(full_velocity, "depth", odds)
    vel_up = jnp.where(even, vel_even, vel_odd)
    vel_low = jnp.where(even, vel_odd, vel_even)

    now = jnp.concatenate([far_low[0], low[0], fwd_now, up[0], far_up[0]], axis=1)
    prev = jnp.concatenate([low[1], fwd_prev, up[1]], axis=1)
    last = jnp.concatenate([low[2], adj_last, up[2]], axis=1)
    late = jnp.concatenate([low[4], adj_late, up[4]], axis=1)
    dens = jnp.concatenate([far_low[1], low[3], density, up[3], far_up[1]], axis=0)
    vel = jnp.concatenate([vel_low, full_velocity, vel_up], axis=0)

    def add_rows(blocks, extra=None):
        edges = pack([jnp.where(lat_at == 0, b[..., rows - PAD :, :], b[..., :PAD, :]) for b in blocks])
        if extra is not None:
            edges = jnp.concatenate([edges, extra], axis=0)
        got = lax.ppermute(edges, "lat", swap)
        parts = unpack(got, [b.shape[:-2] + (PAD, cols) for b in blocks])
        wide = [
            jnp.concatenate(
                [jnp.where(lat_at == 1, part, 0.0), block, jnp.where(lat_at == 0, part, 0.0)],
                axis=-2,
            )
            for part, block in zip(parts, blocks)
        ]
        if extra is None:
            return wide
        return wide, got[got.shape[0] - extra.shape[0] :]

    now, prev, last, late, dens, vel = add_rows([now, prev, last, late, dens, vel])
    buoy = jnp.where(dens > 0.0, 1.0 / jnp.where(dens > 0.0, dens, 1.0), 0.0)

    wide_rows = rows + 2 * PAD
    full_rows = rows * lat_count
    depth_start = depth_at * planes
    row_start = lat_at * rows

    def place(cells, margin):
        plane_at = cells // (full_rows * cols) - depth_start + margin
        row_at = cells // cols % full_rows - row_start + PAD
        inside = (
            (plane_at >= 0)
            & (plane_at < planes + 2 * margin)
            & (row_at >= 0)
            & (row_at < wide_rows)
        )
        return jnp.where(inside, plane_at * wide_rows + row_at, -1), cells % cols

    row_id, col_id = place(receiver_cell, 1)
    dense = spread(row_id, col_id, observed, (planes + 2) * wide_rows, cols)
    dense = dense.reshape(shots, 3, planes + 2, wide_rows, cols)
    hits, sums = dense[:, 0], [dense[:, 1], dense[:, 2]]

    def source(step, margin):
        at_row, at_col = place(source_cell, margin)
        shape = (shots, planes + 2 * margin, wide_rows, cols)
        line = lax.broadcasted_iota(jnp.int32, shape, 1) * wide_rows
        line = line + lax.broadcasted_iota(jnp.int32, shape, 2)
        column = lax.broadcasted_iota(jnp.int32, shape, 3)
        here = (line == at_row[:, None, None, None]) & (column == at_col[:, None, None, None])
        return jnp.where(here, wavelet[:, step][:, None, None, None], 0.0)

    lap_first = laplace(now, buoy)
    base = 2.0 * inner(now, 1) - prev + source(0, 2)

    def gradient_of(stiff):
        second = base + stiff * lap_first
        lap_second = laplace(second, inner(buoy, 1))
        third = (
            2.0 * inner(second, 1)
            - inner(now, 2)
            + inner(stiff, 1) * lap_second
            + source(1, 1)
        )
        upper = (
            2.0 * inner(last, 1)
            - late
            + laplace(stiff * last, inner(buoy, 1))
            + (hits * third - sums[1])
        )
        lower = (
            2.0 * inner(upper, 1)
            - inner(last, 2)
            + laplace(inner(stiff, 1) * upper, inner(buoy, 2))
            + (inner(hits, 1) * inner(second, 2) - inner(sums[0], 1))
        )
        shared = upper[:, 1:-1] * lap_second[:, 1:-1] + lower * lap_first[:, 2:-2]
        return (inner(stiff, 2) * jnp.sum(shared, axis=0))[:, PAD:-PAD, :]

    def own_lines(block):
        return lax.dynamic_slice_in_dim(block, shot_at * own_width, own_width, 2)

    stiff = (vel * COURANT) ** 2 * inner(dens, 1)
    own_velocity = velocity
    direction = None
    for update_index in range(ITERS):
        summed = shot_sum(gradient_of(stiff))
        largest = jnp.broadcast_to(jnp.max(jnp.abs(summed)), (1, cols))
        if update_index + 1 == ITERS:
            largest = jnp.maximum(largest, lax.ppermute(largest, "lat", swap))
            largest = depth_max(largest)
            direction = own_lines(summed) / (largest[0, 0] + EPSILON)
            own_velocity = own_velocity * jnp.exp(-STEP_SIZE * direction)
            break
        (summed,), got = add_rows([summed], largest)
        largest = jnp.maximum(largest, got)
        by_even = send(summed, "depth", evens)
        by_odd = send(summed, "depth", odds)
        largest = depth_max(largest)
        up_sum = jnp.where(even, by_even, by_odd)
        low_sum = jnp.where(even, by_odd, by_even)
        whole = jnp.concatenate([low_sum, summed, up_sum], axis=0) / (largest[0, 0] + EPSILON)
        stiff = stiff * jnp.exp(-2.0 * STEP_SIZE * whole)
        own_velocity = own_velocity * jnp.exp(
            -STEP_SIZE * own_lines(inner(whole, 2)[:, PAD:-PAD, :])
        )
    return (own_velocity, direction)


def solution(mesh):
    fields = P(("grp", "shot"), "depth", "lat", None)
    model = P(("grp", "depth"), "lat", "shot")
    placed = (
        fields,
        fields,
        fields,
        fields,
        model,
        P(("grp", "depth"), "lat", None),
        P(("grp", "shot"), None),
        P(("grp", "shot")),
        P(("grp", "shot"), None),
        P(("grp", "shot"), None, None),
    )
    return jax.shard_map(
        shards,
        mesh=mesh,
        in_specs=placed,
        out_specs=(model, model),
        check_vma=False,
    )
```

```python
import functools

import jax
import jax.numpy as jnp
from jax import lax
from jax.experimental import pallas as pl
from jax.experimental.pallas import tpu as pltpu
from jax.sharding import PartitionSpec as P

ITERS = 2

COURANT = 0.1
STEP_SIZE = 0.1
EPSILON = 1e-06
PAD = 8
WIDE = 3


def even_pairs(count):
    return [(i, i ^ 1) for i in range(count) if i ^ 1 < count]


def odd_pairs(count):
    ups = [(i, i + 1) for i in range(1, count - 1, 2)]
    return ups + [(b, a) for a, b in ups]


def two_pairs(count, first):
    ups = [(i, i + 2) for i in range(count - 2) if (i % 4 < 2) == first]
    return ups + [(b, a) for a, b in ups]


def send(block, axis, pairs):
    if not pairs:
        return jnp.zeros_like(block)
    return lax.ppermute(block, axis, pairs)


def on_chip(kernel, out_shapes, args, scratch=(), flops=0, limit=8, name=None):
    spec = pl.BlockSpec(memory_space=pltpu.VMEM)
    outs = tuple(pltpu.VMEM(shape, jnp.float32) for shape in out_shapes)
    moved = sum(a.size * 4 for a in args)
    return pl.pallas_call(
        kernel,
        out_shape=outs,
        in_specs=[spec] * len(args),
        out_specs=tuple(spec for _ in outs),
        scratch_shapes=[pltpu.VMEM(shape, jnp.float32) for shape in scratch],
        compiler_params=pltpu.CompilerParams(vmem_limit_bytes=limit << 20),
        cost_estimate=pl.CostEstimate(flops=flops, bytes_accessed=moved, transcendentals=0),
        name=name,
    )(*[pltpu.with_memory_space_constraint(a, pltpu.VMEM) for a in args])


def pack_kernel(now, prev, last, dens, late, to_even, to_odd, to_far):
    depth_at = lax.axis_index("depth")
    even = depth_at % 2 == 0
    front = depth_at % 4 < 2
    shots, planes, rows, cols = now.shape
    block = planes * rows
    start = 0
    for field in (now, prev, last):
        for shot in range(shots):
            value = field[shot].reshape(block, cols)
            to_even[start : start + block] = value
            to_odd[start : start + block] = value
            start += block
    value = dens[...].reshape(block, cols)
    to_even[start : start + block] = value
    to_odd[start : start + block] = value
    start += block
    for shot in range(shots):
        low, top = late[shot, 0], late[shot, planes - 1]
        to_even[start : start + rows] = jnp.where(even, top, low)
        to_odd[start : start + rows] = jnp.where(even, low, top)
        start += rows
        to_far[0, shot * rows : (shot + 1) * rows] = jnp.where(
            front, now[shot, planes - 1], now[shot, 0]
        )
        to_far[1, shot * rows : (shot + 1) * rows] = jnp.where(
            front, now[shot, 0], now[shot, planes - 1]
        )
    end = shots * rows
    to_far[0, end:] = jnp.where(front, dens[planes - 1], dens[0])
    to_far[1, end:] = jnp.where(front, dens[0], dens[planes - 1])


def spread_kernel(row_ref, col_ref, obs_ref, out_ref):
    shots, nrec = row_ref.shape
    rows, cols = out_ref.shape[2:]
    steps = obs_ref.shape[1]
    row_iota = lax.broadcasted_iota(jnp.int32, (rows, nrec), 0)
    col_iota = lax.broadcasted_iota(jnp.int32, (cols, nrec), 0)
    dims = (((1,), (1,)), ((), ()))
    for shot in range(shots):
        at_row = (row_ref[shot : shot + 1, :] == row_iota).astype(jnp.float32)
        at_row = at_row.astype(jnp.bfloat16)
        at_col = col_ref[shot : shot + 1, :] == col_iota
        ones = at_col.astype(jnp.float32).astype(jnp.bfloat16)
        out_ref[shot, 0] = lax.dot_general(
            at_row, ones, dims, preferred_element_type=jnp.float32
        )
        for step in range(steps):
            obs = obs_ref[shot, step : step + 1, :]
            high = obs.astype(jnp.bfloat16).astype(jnp.float32)
            rest = obs - high
            middle = rest.astype(jnp.bfloat16).astype(jnp.float32)
            low = rest - middle
            total = None
            for part in (high, middle, low):
                term = lax.dot_general(
                    at_row,
                    jnp.where(at_col, part, 0.0).astype(jnp.bfloat16),
                    dims,
                    preferred_element_type=jnp.float32,
                )
                total = term if total is None else total + term
            out_ref[shot, 1 + step] = total


class Halo:
    def __init__(self, own, near_even, near_odd, far_first, far_second, vel_own, vel_even, vel_odd):
        depth_at = lax.axis_index("depth")
        self.even = depth_at % 2 == 0
        self.front = depth_at % 4 < 2
        self.own = own
        self.near = (near_even, near_odd)
        self.far = (far_first, far_second)
        self.vel = (vel_own, vel_even, vel_odd)
        self.shots, self.planes, self.rows, self.cols = own[0].shape

    def near_rows(self, start, upper, rows):
        first, second = self.near if upper else self.near[::-1]
        return jnp.where(self.even, first[start : start + rows], second[start : start + rows])

    def far_rows(self, start, upper, rows):
        first, second = self.far if upper else self.far[::-1]
        return jnp.where(self.front, first[start : start + rows], second[start : start + rows])

    def field(self, which, shot, at):
        rows, planes = self.rows, self.planes
        if 0 <= at < planes:
            return self.own[which][shot, at]
        upper = at >= planes
        step = at - planes if upper else planes + at
        if which == 4:
            start = (3 * self.shots * planes + planes + shot) * rows
            return self.near_rows(start, upper, rows)
        if 0 <= step < planes:
            start = ((which * self.shots + shot) * planes + step) * rows
            return self.near_rows(start, upper, rows)
        return self.far_rows(shot * rows, upper, rows)

    def dens(self, at):
        rows, planes = self.rows, self.planes
        if 0 <= at < planes:
            return self.own[3][at]
        upper = at >= planes
        step = at - planes if upper else planes + at
        if 0 <= step < planes:
            return self.near_rows((3 * self.shots * planes + step) * rows, upper, rows)
        return self.far_rows(self.shots * rows, upper, rows)

    def velocity(self, at):
        planes = self.planes
        if 0 <= at < planes:
            return self.vel[0][at]
        upper = at >= planes
        step = at - planes if upper else planes + at
        first, second = self.vel[1:] if upper else self.vel[:0:-1]
        return jnp.where(self.even, first[step], second[step])

    def plane_list(self):
        out = []
        planes = self.planes
        for which, margin in ((0, 3), (1, 2), (2, 2), (4, 1)):
            for shot in range(self.shots):
                for at in range(-margin, planes + margin):
                    out.append((which, shot, at))
        for at in range(-3, planes + 3):
            out.append((3, 0, at))
        for at in range(-2, planes + 2):
            out.append((5, 0, at))
        return out

    def plane(self, item):
        which, shot, at = item
        if which == 3:
            return self.dens(at)
        if which == 5:
            return self.velocity(at)
        return self.field(which, shot, at)


def edge_kernel(now, prev, last, dens, late, near_even, near_odd, far_first, far_second, vel, vel_even, vel_odd, out):
    halo = Halo((now, prev, last, dens, late), near_even, near_odd, far_first, far_second, vel, vel_even, vel_odd)
    first = lax.axis_index("lat") == 0
    rows = halo.rows
    for index, item in enumerate(halo.plane_list()):
        value = halo.plane(item)
        out[index * PAD : (index + 1) * PAD] = jnp.where(first, value[rows - PAD :], value[:PAD])


def near_cols(value):
    lane = lax.broadcasted_iota(jnp.int32, value.shape, 1)
    cols = value.shape[1]
    above = jnp.where(lane == cols - 1, 0.0, pltpu.roll(value, cols - 1, 1))
    below = jnp.where(lane == 0, 0.0, pltpu.roll(value, 1, 1))
    return above, below


def laplace(field, at, cz, cx, cp, cm):
    middle = field(at)
    rows = middle.shape[0]
    flux = cx(at) * (pltpu.roll(middle, rows - 1, 0) - middle)
    total = flux - pltpu.roll(flux, 1, 0)
    above, below = near_cols(middle)
    total = total + (cp(at) * (above - middle) + cm(at) * (below - middle))
    return total + (cz(at) * (field(at + 1) - middle) + cz(at - 1) * (field(at - 1) - middle))


def prepare_kernel(
    now,
    prev,
    last,
    dens,
    late,
    near_even,
    near_odd,
    far_first,
    far_second,
    vel,
    vel_even,
    vel_odd,
    edges,
    dense,
    source_at,
    wavelet,
    lap_out,
    base_out,
    turn_out,
    late_out,
    last_out,
    low_out,
    stiff_out,
    cz_out,
    cx_out,
    cp_out,
    cm_out,
    now_buf,
    buoy_buf,
):
    halo = Halo((now, prev, last, dens, late), near_even, near_odd, far_first, far_second, vel, vel_even, vel_odd)
    lat_at = lax.axis_index("lat")
    rows, cols, shots, planes = halo.rows, halo.cols, halo.shots, halo.planes
    wide = rows + 2 * PAD
    where_is = {item: index for index, item in enumerate(halo.plane_list())}

    def whole(item):
        index = where_is[item]
        part = edges[index * PAD : (index + 1) * PAD]
        low = jnp.where(lat_at == 1, part, 0.0)
        high = jnp.where(lat_at == 0, part, 0.0)
        return jnp.concatenate([low, halo.plane(item), high], axis=0)

    for at in range(-3, planes + 3):
        density = whole((3, 0, at))
        inside = density > 0.0
        buoy_buf[at + 3] = jnp.where(inside, 1.0 / jnp.where(inside, density, 1.0), 0.0)
        if -2 <= at < planes + 2:
            speed = whole((5, 0, at)) * COURANT
            stiff_out[at + 2] = speed * speed * density
        for shot in range(shots):
            now_buf[shot, at + 3] = whole((0, shot, at))
    for at in range(-3, planes + 2):
        cz_out[at + 3] = 0.5 * (buoy_buf[at + 3] + buoy_buf[at + 4])
    for at in range(-2, planes + 2):
        buoy = buoy_buf[at + 3]
        cx_out[at + 2] = 0.5 * (buoy + pltpu.roll(buoy, wide - 1, 0))
        above, below = near_cols(buoy)
        cp_out[at + 2] = 0.5 * (buoy + above)
        cm_out[at + 2] = 0.5 * (buoy + below)
    line = lax.broadcasted_iota(jnp.int32, (wide, cols), 0)
    column = lax.broadcasted_iota(jnp.int32, (wide, cols), 1)
    for shot in range(shots):
        for at in range(-2, planes + 2):
            here = (line + (at + 2) * wide == source_at[shot, 0]) & (column == source_at[shot, 1])
            middle = now_buf[shot, at + 3]
            lap_out[shot, at + 2] = laplace(
                lambda k: now_buf[shot, k + 3],
                at,
                lambda k: cz_out[k + 3],
                lambda k: cx_out[k + 2],
                lambda k: cp_out[k + 2],
                lambda k: cm_out[k + 2],
            )
            base_out[shot, at + 2] = (
                2.0 * middle - whole((1, shot, at)) + jnp.where(here, wavelet[shot, 0], 0.0)
            )
            newest = whole((2, shot, at))
            last_out[shot, at + 2] = newest
            if -1 <= at < planes + 1:
                turn_out[shot, at + 1] = jnp.where(here, wavelet[shot, 1], 0.0) - middle
                late_out[shot, at + 1] = (
                    2.0 * newest
                    - whole((4, shot, at))
                    - dense[shot, 2, (at + 1) * wide : (at + 2) * wide]
                )
            if 0 <= at < planes:
                low_out[shot, at] = newest + dense[shot, 1, (at + 1) * wide : (at + 2) * wide]


def update_kernel(
    stiff,
    lap,
    base,
    turn,
    late,
    last,
    low,
    dense,
    cz_ref,
    cx_ref,
    cp_ref,
    cm_ref,
    out,
    second,
    scaled,
    upper,
    lap_second,
):
    shots, planes = low.shape[:2]
    wide, cols = low.shape[2:]
    cz = lambda k: cz_ref[k + 1]
    cx = lambda k: cx_ref[k]
    cp = lambda k: cp_ref[k]
    cm = lambda k: cm_ref[k]
    for at in range(planes + 4):
        rigid = stiff[at]
        for shot in range(shots):
            second[shot, at] = base[shot, at] + rigid * lap[shot, at]
            scaled[shot, at] = rigid * last[shot, at]
    for at in range(1, planes + 3):
        rigid = stiff[at]
        for shot in range(shots):
            hits = dense[shot, 0, (at - 1) * wide : at * wide]
            lap_now = laplace(lambda k: second[shot, k], at, cz, cx, cp, cm)
            third = 2.0 * second[shot, at] + turn[shot, at - 1] + rigid * lap_now
            adj = late[shot, at - 1] + hits * third
            adj = adj + laplace(lambda k: scaled[shot, k], at, cz, cx, cp, cm)
            upper[shot, at - 1] = adj
            if 2 <= at < planes + 2:
                lap_second[shot, at - 2] = lap_now
    for at in range(1, planes + 3):
        for shot in range(shots):
            scaled[shot, at] = stiff[at] * upper[shot, at - 1]
    for at in range(2, planes + 2):
        total = None
        for shot in range(shots):
            hits = dense[shot, 0, (at - 1) * wide : at * wide]
            lower = 2.0 * upper[shot, at - 1] - low[shot, at - 2] + hits * second[shot, at]
            lower = lower + laplace(lambda k: scaled[shot, k], at, cz, cx, cp, cm)
            term = upper[shot, at - 1] * lap_second[shot, at - 2] + lower * lap[shot, at]
            total = term if total is None else total + term
        out[at - 2] = (stiff[at] * total)[PAD : wide - PAD]


def tile_max(value):
    planes, rows, cols = value.shape
    return jnp.max(jnp.abs(value).reshape(planes * rows // 8, 8, cols), axis=0)


def sum_kernel(mine, other, total, edges):
    value = mine[...] + other[...]
    total[...] = value
    first = lax.axis_index("lat") == 0
    planes, rows, cols = value.shape
    for at in range(planes):
        edges[at * PAD : (at + 1) * PAD] = jnp.where(
            first, value[at, rows - PAD :], value[at, :PAD]
        )
    edges[planes * PAD :] = tile_max(value)


def last_sum_kernel(mine, other, total, largest):
    value = mine[...] + other[...]
    total[...] = value
    largest[...] = tile_max(value)


def widen_kernel(total, mine, got, out):
    planes, rows, cols = total.shape
    wide = rows + 2 * PAD
    lat_at = lax.axis_index("lat")
    for at in range(planes):
        part = got[at * PAD : (at + 1) * PAD]
        start = at * wide
        out[start : start + PAD] = jnp.where(lat_at == 1, part, 0.0)
        out[start + PAD : start + PAD + rows] = total[at]
        out[start + PAD + rows : start + wide] = jnp.where(lat_at == 0, part, 0.0)
    out[planes * wide :] = jnp.maximum(mine[planes * PAD :], got[planes * PAD :])


def restiff_kernel(stiff, mine, by_even, by_odd, largest, velocity, stiff_out, vel_out):
    planes, rows, own = velocity.shape
    wide = rows + 2 * PAD
    even = lax.axis_index("depth") % 2 == 0
    shot_at = lax.axis_index("shot")
    cols = mine.shape[1]
    scale = jnp.max(jnp.max(largest[...], axis=1, keepdims=True), axis=0, keepdims=True) + EPSILON
    for at in range(-2, planes + 2):
        if 0 <= at < planes:
            value = mine[at * wide : (at + 1) * wide]
        else:
            upper = at >= planes
            step = at - planes if upper else planes + at
            first, second = (by_even, by_odd) if upper else (by_odd, by_even)
            value = jnp.where(
                even, first[step * wide : (step + 1) * wide], second[step * wide : (step + 1) * wide]
            )
        value = value / scale
        stiff_out[at + 2] = stiff[at + 2] * jnp.exp(-2.0 * STEP_SIZE * value)
        if 0 <= at < planes:
            shifted = pltpu.roll(value[PAD : PAD + rows], (cols - shot_at * own) % cols, 1)
            vel_out[at] = velocity[at] * jnp.exp(-STEP_SIZE * shifted[:, :own])


def finish_kernel(total, largest, velocity, vel_out, dir_out):
    planes, rows, own = velocity.shape
    shot_at = lax.axis_index("shot")
    cols = total.shape[2]
    scale = jnp.max(jnp.max(largest[...], axis=1, keepdims=True), axis=0, keepdims=True) + EPSILON
    for at in range(planes):
        value = total[at] / scale
        shifted = pltpu.roll(value, (cols - shot_at * own) % cols, 1)[:, :own]
        dir_out[at] = shifted
        vel_out[at] = velocity[at] * jnp.exp(-STEP_SIZE * shifted)


def shards(
    fwd_prev,
    fwd_now,
    adj_late,
    adj_last,
    velocity,
    density,
    wavelet,
    source_cell,
    receiver_cell,
    observed,
):
    shots, planes, rows, cols = fwd_now.shape
    depth_count = lax.axis_size("depth")
    shot_count = lax.axis_size("shot")
    lat_count = lax.axis_size("lat")
    if planes != 2 or wavelet.shape[1] != 2 or lat_count != 2:
        raise ValueError("unsupported split")
    depth_at = lax.axis_index("depth")
    lat_at = lax.axis_index("lat")
    shot_at = lax.axis_index("shot")
    evens = even_pairs(depth_count)
    odds = odd_pairs(depth_count)
    swap = [(0, 1), (1, 0)]
    wide = rows + 2 * PAD

    def shot_terms(block):
        if shot_count == 2:
            return block, lax.ppermute(block, "shot", swap)
        return lax.psum(block, "shot"), jnp.zeros_like(block)

    def depth_max(value, from_pair=None):
        if depth_count & (depth_count - 1):
            return lax.pmax(value, "depth")
        first = 1 if from_pair is None else 2
        if depth_count <= 4:
            parts = [
                lax.ppermute(value, "depth", [(i, i ^ k) for i in range(depth_count)])
                for k in range(first, depth_count)
            ]
            if from_pair is not None:
                parts.append(from_pair)
            for part in parts:
                value = jnp.maximum(value, part)
            return value
        if from_pair is not None:
            value = jnp.maximum(value, from_pair)
        step = first
        while step < depth_count:
            pairs = [(i, i ^ step) for i in range(depth_count)]
            value = jnp.maximum(value, lax.ppermute(value, "depth", pairs))
            step *= 2
        return value

    if shot_count == 2:
        other = lax.ppermute(velocity, "shot", swap)
        full_velocity = jnp.where(
            shot_at == 0,
            jnp.concatenate([velocity, other], axis=2),
            jnp.concatenate([other, velocity], axis=2),
        )
    else:
        full_velocity = lax.all_gather(velocity, "shot", axis=2, tiled=True)

    own = (fwd_now, fwd_prev, adj_last, density, adj_late)
    near_rows = (3 * shots * planes + planes + shots) * rows
    far_rows = (shots + 1) * rows
    to_even, to_odd, to_far = on_chip(
        pack_kernel,
        [(near_rows, cols), (near_rows, cols), (2, far_rows, cols)],
        own,
        name="pack",
    )
    near_even = send(to_even, "depth", evens)
    near_odd = send(to_odd, "depth", odds)
    far_first = send(to_far[0], "depth", two_pairs(depth_count, True))
    far_second = send(to_far[1], "depth", two_pairs(depth_count, False))

    full_rows = rows * lat_count
    depth_start = depth_at * planes
    row_start = lat_at * rows

    def place(cells, margin):
        plane_at = cells // (full_rows * cols) - depth_start + margin
        row_at = cells // cols % full_rows - row_start + PAD
        inside = (
            (plane_at >= 0)
            & (plane_at < planes + 2 * margin)
            & (row_at >= 0)
            & (row_at < wide)
        )
        return jnp.where(inside, plane_at * wide + row_at, -1), cells % cols

    row_id, col_id = place(receiver_cell, 1)
    row_id, full_velocity = lax.optimization_barrier((row_id, full_velocity))
    vel_even = send(full_velocity, "depth", evens)
    vel_odd = send(full_velocity, "depth", odds)
    spread_shape = (shots, 3, (planes + 2) * wide, cols)
    (dense,) = on_chip(
        spread_kernel,
        [spread_shape],
        (row_id, col_id, observed),
        flops=14 * shots * spread_shape[2] * cols * row_id.shape[1],
        limit=24,
        name="spread",
    )
    source_at = jnp.stack(place(source_cell, 2), axis=1)

    halos = own + (near_even, near_odd, far_first, far_second, full_velocity, vel_even, vel_odd)
    strips = shots * (4 * planes + 16) + 2 * planes + 10
    (edges,) = on_chip(edge_kernel, [(strips * PAD, cols)], halos, name="edge")
    edges = lax.ppermute(edges, "lat", swap)

    deep, deeper = planes + 4, planes + 6
    model = (wide, cols)
    spec = pl.BlockSpec(memory_space=pltpu.VMEM)
    scalars = pl.BlockSpec(memory_space=pltpu.SMEM)
    prepared_shapes = [
        (shots, deep) + model,
        (shots, deep) + model,
        (shots, planes + 2) + model,
        (shots, planes + 2) + model,
        (shots, deep) + model,
        (shots, planes) + model,
        (deep,) + model,
        (planes + 5,) + model,
        (deep,) + model,
        (deep,) + model,
        (deep,) + model,
    ]
    vectors = halos + (edges, dense)
    prepared = pl.pallas_call(
        prepare_kernel,
        out_shape=tuple(pltpu.VMEM(shape, jnp.float32) for shape in prepared_shapes),
        in_specs=[spec] * len(vectors) + [scalars, scalars],
        out_specs=tuple(spec for _ in prepared_shapes),
        scratch_shapes=[
            pltpu.VMEM((shots, deeper) + model, jnp.float32),
            pltpu.VMEM((deeper,) + model, jnp.float32),
        ],
        compiler_params=pltpu.CompilerParams(vmem_limit_bytes=8 << 20),
        name="prepare",
    )(
        *[pltpu.with_memory_space_constraint(a, pltpu.VMEM) for a in vectors],
        source_at,
        wavelet,
    )
    lap, base, turn, late, last, low, stiff, cz, cx, cp, cm = prepared

    def gradient_of(stiff):
        (out,) = on_chip(
            update_kernel,
            [(planes, rows, cols)],
            (stiff, lap, base, turn, late, last, low, dense, cz, cx, cp, cm),
            scratch=[
                (shots, deep) + model,
                (shots, deep) + model,
                (shots, planes + 2) + model,
                (shots, planes) + model,
            ],
            name="update",
        )
        return out

    own_velocity = velocity
    for update_index in range(ITERS):
        mine, other = shot_terms(gradient_of(stiff))
        if update_index + 1 == ITERS:
            summed, largest = on_chip(
                last_sum_kernel, [(planes, rows, cols), (8, cols)], (mine, other), name="last_sum"
            )
            largest = jnp.maximum(largest, lax.ppermute(largest, "lat", swap))
            largest = depth_max(largest)
            return tuple(
                on_chip(
                    finish_kernel,
                    [velocity.shape, velocity.shape],
                    (summed, largest, own_velocity),
                    name="finish",
                )
            )
        edge_rows = planes * PAD + 8
        summed, tail = on_chip(
            sum_kernel, [(planes, rows, cols), (edge_rows, cols)], (mine, other), name="sum"
        )
        got = lax.ppermute(tail, "lat", swap)
        (widened,) = on_chip(
            widen_kernel, [(planes * wide + 8, cols)], (summed, tail, got), name="widen"
        )
        by_even = send(widened, "depth", evens)
        by_odd = send(widened, "depth", odds)
        largest = depth_max(widened[planes * wide :], by_even[planes * wide :])
        stiff, own_velocity = on_chip(
            restiff_kernel,
            [stiff.shape, velocity.shape],
            (stiff, widened, by_even, by_odd, largest, own_velocity),
            name="restiff",
        )


def solution(mesh):
    fields = P(("grp", "shot"), "depth", "lat", None)
    model = P(("grp", "depth"), "lat", "shot")
    placed = (
        fields,
        fields,
        fields,
        fields,
        model,
        P(("grp", "depth"), "lat", None),
        P(("grp", "shot"), None),
        P(("grp", "shot")),
        P(("grp", "shot"), None),
        P(("grp", "shot"), None, None),
    )
    return jax.shard_map(
        shards,
        mesh=mesh,
        in_specs=placed,
        out_specs=(model, model),
        check_vma=False,
    )
```

```python
import jax
import jax.numpy as jnp
from jax import lax
from jax.experimental import pallas as pl
from jax.experimental.pallas import tpu as pltpu
from jax.sharding import PartitionSpec as P


ITERS = 2

COURANT = 0.1
STEP_SIZE = 0.1
EPSILON = 1e-06
PAD = 8


def even_pairs(count):
    return [(i, i ^ 1) for i in range(count) if i ^ 1 < count]


def odd_pairs(count):
    ups = [(i, i + 1) for i in range(1, count - 1, 2)]
    return ups + [(b, a) for a, b in ups]


def two_pairs(count, first):
    ups = [(i, i + 2) for i in range(count - 2) if (i % 4 < 2) == first]
    return ups + [(b, a) for a, b in ups]


def send(block, axis, pairs):
    if not pairs:
        return jnp.zeros_like(block)
    return lax.ppermute(block, axis, pairs)


def on_chip(kernel, out_shapes, args, scratch=(), flops=0, limit=8, keep=True):
    spec = pl.BlockSpec(memory_space=pltpu.VMEM)
    place = pltpu.VMEM if keep else jax.ShapeDtypeStruct
    outs = tuple(place(shape, jnp.float32) for shape in out_shapes)
    moved = sum(a.size * 4 for a in args)
    return pl.pallas_call(
        kernel,
        out_shape=outs,
        in_specs=[spec] * len(args),
        out_specs=tuple(spec for _ in outs),
        scratch_shapes=[pltpu.VMEM(shape, jnp.float32) for shape in scratch],
        compiler_params=pltpu.CompilerParams(vmem_limit_bytes=limit << 20),
        cost_estimate=pl.CostEstimate(flops=flops, bytes_accessed=moved, transcendentals=0),
    )(*[pltpu.with_memory_space_constraint(a, pltpu.VMEM) for a in args])


def pack_kernel(now, prev, last, dens, late, to_even, to_odd, to_far, late_out, sems):
    depth_at = lax.axis_index("depth")
    even = depth_at % 2 == 0
    front = depth_at % 4 < 2
    shots, planes, _, _ = now.shape
    copies = []
    start = 0
    for field in (now, prev, last):
        for shot in range(shots):
            copies.append((field.at[shot], to_even.at[start : start + planes]))
            start += planes
    copies.append((dens, to_even.at[start : start + planes]))
    start += planes
    copies.append((late, late_out))
    copies = [
        pltpu.make_async_copy(source, target, sems.at[index])
        for index, (source, target) in enumerate(copies)
    ]
    for copy in copies:
        copy.start()
    for copy in copies:
        copy.wait()
    to_odd[:start] = to_even[:start]
    for shot in range(shots):
        low, top = late_out[shot, 0], late_out[shot, planes - 1]
        to_even[start + shot] = jnp.where(even, top, low)
        to_odd[start + shot] = jnp.where(even, low, top)
        low, top = to_even[shot * planes], to_even[shot * planes + planes - 1]
        to_far[0, shot] = jnp.where(front, top, low)
        to_far[1, shot] = jnp.where(front, low, top)
    low, top = to_even[start - planes], to_even[start - 1]
    to_far[0, shots] = jnp.where(front, top, low)
    to_far[1, shots] = jnp.where(front, low, top)


def spread_kernel(row_ref, col_ref, obs_ref, out_ref):
    shots, nrec = row_ref.shape
    rows, cols = out_ref.shape[2:]
    steps = obs_ref.shape[1]
    row_iota = lax.broadcasted_iota(jnp.int32, (rows, nrec), 0)
    col_iota = lax.broadcasted_iota(jnp.int32, (cols, nrec), 0)
    dims = (((1,), (1,)), ((), ()))
    for shot in range(shots):
        at_row = (row_ref[shot : shot + 1, :] == row_iota).astype(jnp.float32)
        at_row = at_row.astype(jnp.bfloat16)
        at_col = col_ref[shot : shot + 1, :] == col_iota
        ones = at_col.astype(jnp.float32).astype(jnp.bfloat16)
        out_ref[shot, 0] = lax.dot_general(
            at_row, ones, dims, preferred_element_type=jnp.float32
        )
        for step in range(steps):
            obs = obs_ref[shot, step : step + 1, :]
            high = obs.astype(jnp.bfloat16).astype(jnp.float32)
            rest = obs - high
            middle = rest.astype(jnp.bfloat16).astype(jnp.float32)
            low = rest - middle
            total = None
            for part in (high, middle, low):
                term = lax.dot_general(
                    at_row,
                    jnp.where(at_col, part, 0.0).astype(jnp.bfloat16),
                    dims,
                    preferred_element_type=jnp.float32,
                )
                total = term if total is None else total + term
            out_ref[shot, 1 + step] = total


class Halo:
    def __init__(self, own, late, near_even, near_odd, far_first, far_second, vel_own, vel_even, vel_odd):
        depth_at = lax.axis_index("depth")
        self.even = depth_at % 2 == 0
        self.front = depth_at % 4 < 2
        self.own, self.late = own, late
        self.near = (near_even, near_odd)
        self.far = (far_first, far_second)
        self.vel = (vel_own, vel_even, vel_odd)
        self.shots, self.planes, self.rows, self.cols = late.shape

    def pick(self, pair, flag, upper, index):
        first, second = pair if upper else pair[::-1]
        return jnp.where(flag, first[index], second[index])

    def plane(self, item):
        which, shot, at = item
        planes, shots = self.planes, self.shots
        inside = 0 <= at < planes
        upper = at >= planes
        step = at if inside else (at - planes if upper else planes + at)
        if which == 5:
            if inside:
                return self.vel[0][at]
            return self.pick(self.vel[1:], self.even, upper, step)
        if which == 4:
            if inside:
                return self.late[shot, at]
            return self.pick(self.near, self.even, upper, (3 * shots + 1) * planes + shot)
        if 0 <= step < planes:
            index = (which * shots + shot) * planes + step
            return self.own[index] if inside else self.pick(self.near, self.even, upper, index)
        return self.pick(self.far, self.front, upper, shots if which == 3 else shot)

    def plane_list(self):
        out = []
        planes = self.planes
        for which, margin in ((0, 3), (1, 2), (2, 2), (4, 1)):
            for shot in range(self.shots):
                for at in range(-margin, planes + margin):
                    out.append((which, shot, at))
        for at in range(-3, planes + 3):
            out.append((3, 0, at))
        for at in range(-2, planes + 2):
            out.append((5, 0, at))
        return out


def edge_kernel(*refs):
    halo = Halo(*refs[:-1])
    out = refs[-1]
    first = lax.axis_index("lat") == 0
    rows = halo.rows
    for index, item in enumerate(halo.plane_list()):
        value = halo.plane(item)
        out[index * PAD : (index + 1) * PAD] = jnp.where(first, value[rows - PAD :], value[:PAD])


def near_cols(value):
    lane = lax.broadcasted_iota(jnp.int32, value.shape, 1)
    cols = value.shape[1]
    above = jnp.where(lane == cols - 1, 0.0, pltpu.roll(value, cols - 1, 1))
    below = jnp.where(lane == 0, 0.0, pltpu.roll(value, 1, 1))
    return above, below


def laplace(field, at, cz, cx, cp, cm):
    middle = field(at)
    rows = middle.shape[0]
    flux = cx(at) * (pltpu.roll(middle, rows - 1, 0) - middle)
    total = flux - pltpu.roll(flux, 1, 0)
    above, below = near_cols(middle)
    total = total + (cp(at) * (above - middle) + cm(at) * (below - middle))
    return total + (cz(at) * (field(at + 1) - middle) + cz(at - 1) * (field(at - 1) - middle))


def prepare_kernel(
    own,
    late,
    near_even,
    near_odd,
    far_first,
    far_second,
    vel,
    vel_even,
    vel_odd,
    edges,
    dense,
    source_at,
    wavelet,
    lap_out,
    base_out,
    turn_out,
    late_out,
    last_out,
    low_out,
    stiff_out,
    cz_out,
    cx_out,
    cp_out,
    cm_out,
    now_buf,
    buoy_buf,
):
    halo = Halo(own, late, near_even, near_odd, far_first, far_second, vel, vel_even, vel_odd)
    lat_at = lax.axis_index("lat")
    rows, cols, shots, planes = halo.rows, halo.cols, halo.shots, halo.planes
    wide = rows + 2 * PAD
    where_is = {item: index for index, item in enumerate(halo.plane_list())}

    def whole(item):
        index = where_is[item]
        part = edges[index * PAD : (index + 1) * PAD]
        low = jnp.where(lat_at == 1, part, 0.0)
        high = jnp.where(lat_at == 0, part, 0.0)
        return jnp.concatenate([low, halo.plane(item), high], axis=0)

    for at in range(-3, planes + 3):
        density = whole((3, 0, at))
        inside = density > 0.0
        buoy_buf[at + 3] = jnp.where(inside, 1.0 / jnp.where(inside, density, 1.0), 0.0)
        if -2 <= at < planes + 2:
            speed = whole((5, 0, at)) * COURANT
            stiff_out[at + 2] = speed * speed * density
        for shot in range(shots):
            now_buf[shot, at + 3] = whole((0, shot, at))
    for at in range(-3, planes + 2):
        cz_out[at + 3] = 0.5 * (buoy_buf[at + 3] + buoy_buf[at + 4])
    for at in range(-2, planes + 2):
        buoy = buoy_buf[at + 3]
        cx_out[at + 2] = 0.5 * (buoy + pltpu.roll(buoy, wide - 1, 0))
        above, below = near_cols(buoy)
        cp_out[at + 2] = 0.5 * (buoy + above)
        cm_out[at + 2] = 0.5 * (buoy + below)
    line = lax.broadcasted_iota(jnp.int32, (wide, cols), 0)
    column = lax.broadcasted_iota(jnp.int32, (wide, cols), 1)
    for shot in range(shots):
        for at in range(-2, planes + 2):
            here = (line + (at + 2) * wide == source_at[shot, 0]) & (column == source_at[shot, 1])
            middle = now_buf[shot, at + 3]
            lap_out[shot, at + 2] = laplace(
                lambda k: now_buf[shot, k + 3],
                at,
                lambda k: cz_out[k + 3],
                lambda k: cx_out[k + 2],
                lambda k: cp_out[k + 2],
                lambda k: cm_out[k + 2],
            )
            base_out[shot, at + 2] = (
                2.0 * middle - whole((1, shot, at)) + jnp.where(here, wavelet[shot, 0], 0.0)
            )
            newest = whole((2, shot, at))
            last_out[shot, at + 2] = newest
            if -1 <= at < planes + 1:
                turn_out[shot, at + 1] = jnp.where(here, wavelet[shot, 1], 0.0) - middle
                late_out[shot, at + 1] = (
                    2.0 * newest
                    - whole((4, shot, at))
                    - dense[shot, 2, (at + 1) * wide : (at + 2) * wide]
                )
            if 0 <= at < planes:
                low_out[shot, at] = newest + dense[shot, 1, (at + 1) * wide : (at + 2) * wide]


def update_kernel(
    stiff,
    lap,
    base,
    turn,
    late,
    last,
    low,
    dense,
    cz_ref,
    cx_ref,
    cp_ref,
    cm_ref,
    out,
    second,
    scaled,
    upper,
    lap_second,
):
    shots, planes = low.shape[:2]
    wide, _ = low.shape[2:]
    cz = lambda k: cz_ref[k + 1]
    cx = lambda k: cx_ref[k]
    cp = lambda k: cp_ref[k]
    cm = lambda k: cm_ref[k]
    for at in range(planes + 4):
        rigid = stiff[at]
        for shot in range(shots):
            second[shot, at] = base[shot, at] + rigid * lap[shot, at]
            scaled[shot, at] = rigid * last[shot, at]
    for at in range(1, planes + 3):
        rigid = stiff[at]
        for shot in range(shots):
            hits = dense[shot, 0, (at - 1) * wide : at * wide]
            lap_now = laplace(lambda k: second[shot, k], at, cz, cx, cp, cm)
            third = 2.0 * second[shot, at] + turn[shot, at - 1] + rigid * lap_now
            adj = late[shot, at - 1] + hits * third
            adj = adj + laplace(lambda k: scaled[shot, k], at, cz, cx, cp, cm)
            upper[shot, at - 1] = adj
            if 2 <= at < planes + 2:
                lap_second[shot, at - 2] = lap_now
    for at in range(1, planes + 3):
        for shot in range(shots):
            scaled[shot, at] = stiff[at] * upper[shot, at - 1]
    for at in range(2, planes + 2):
        total = None
        for shot in range(shots):
            hits = dense[shot, 0, (at - 1) * wide : at * wide]
            lower = 2.0 * upper[shot, at - 1] - low[shot, at - 2] + hits * second[shot, at]
            lower = lower + laplace(lambda k: scaled[shot, k], at, cz, cx, cp, cm)
            term = upper[shot, at - 1] * lap_second[shot, at - 2] + lower * lap[shot, at]
            total = term if total is None else total + term
        out[at - 2] = (stiff[at] * total)[PAD : wide - PAD]


def tile_max(value):
    planes, rows, cols = value.shape
    return jnp.max(jnp.abs(value).reshape(planes * rows // 8, 8, cols), axis=0)


def sum_kernel(mine, other, total, edges):
    value = mine[...] + other[...]
    total[...] = value
    first = lax.axis_index("lat") == 0
    planes, rows, _ = value.shape
    for at in range(planes):
        edges[at * PAD : (at + 1) * PAD] = jnp.where(
            first, value[at, rows - PAD :], value[at, :PAD]
        )
    edges[planes * PAD :] = tile_max(value)


def last_sum_kernel(mine, other, total, largest):
    value = mine[...] + other[...]
    total[...] = value
    largest[...] = tile_max(value)


def widen_kernel(total, mine, got, out):
    planes, rows, _ = total.shape
    wide = rows + 2 * PAD
    lat_at = lax.axis_index("lat")
    for at in range(planes):
        part = got[at * PAD : (at + 1) * PAD]
        start = at * wide
        out[start : start + PAD] = jnp.where(lat_at == 1, part, 0.0)
        out[start + PAD : start + PAD + rows] = total[at]
        out[start + PAD + rows : start + wide] = jnp.where(lat_at == 0, part, 0.0)
    out[planes * wide :] = jnp.maximum(mine[planes * PAD :], got[planes * PAD :])


def restiff_kernel(stiff, mine, by_even, by_odd, largest, velocity, stiff_out, vel_out):
    planes, rows, own = velocity.shape
    wide = rows + 2 * PAD
    even = lax.axis_index("depth") % 2 == 0
    shot_at = lax.axis_index("shot")
    cols = mine.shape[1]
    scale = jnp.max(jnp.max(largest[...], axis=1, keepdims=True), axis=0, keepdims=True) + EPSILON
    for at in range(-2, planes + 2):
        if 0 <= at < planes:
            value = mine[at * wide : (at + 1) * wide]
        else:
            upper = at >= planes
            step = at - planes if upper else planes + at
            first, second = (by_even, by_odd) if upper else (by_odd, by_even)
            value = jnp.where(
                even, first[step * wide : (step + 1) * wide], second[step * wide : (step + 1) * wide]
            )
        value = value / scale
        stiff_out[at + 2] = stiff[at + 2] * jnp.exp(-2.0 * STEP_SIZE * value)
        if 0 <= at < planes:
            shifted = pltpu.roll(value[PAD : PAD + rows], (cols - shot_at * own) % cols, 1)
            vel_out[at] = velocity[at] * jnp.exp(-STEP_SIZE * shifted[:, :own])


def finish_kernel(total, largest, velocity, vel_out, dir_out):
    planes, _, own = velocity.shape
    shot_at = lax.axis_index("shot")
    cols = total.shape[2]
    scale = jnp.max(jnp.max(largest[...], axis=1, keepdims=True), axis=0, keepdims=True) + EPSILON
    for at in range(planes):
        value = total[at] / scale
        shifted = pltpu.roll(value, (cols - shot_at * own) % cols, 1)[:, :own]
        dir_out[at] = shifted
        vel_out[at] = velocity[at] * jnp.exp(-STEP_SIZE * shifted)


def shards(
    fwd_prev,
    fwd_now,
    adj_late,
    adj_last,
    velocity,
    density,
    wavelet,
    source_cell,
    receiver_cell,
    observed,
):
    shots, planes, rows, cols = fwd_now.shape
    depth_count = lax.axis_size("depth")
    shot_count = lax.axis_size("shot")
    lat_count = lax.axis_size("lat")
    if planes != 2 or wavelet.shape[1] != 2 or lat_count != 2:
        raise ValueError("unsupported split")
    depth_at = lax.axis_index("depth")
    lat_at = lax.axis_index("lat")
    shot_at = lax.axis_index("shot")
    evens = even_pairs(depth_count)
    odds = odd_pairs(depth_count)
    swap = [(0, 1), (1, 0)]
    wide = rows + 2 * PAD

    def shot_terms(block):
        if shot_count == 2:
            return block, lax.ppermute(block, "shot", swap)
        return lax.psum(block, "shot"), jnp.zeros_like(block)

    def depth_max(value, from_pair=None):
        if depth_count & (depth_count - 1):
            return lax.pmax(value, "depth")
        first = 1 if from_pair is None else 2
        if depth_count <= 4 and from_pair is None:
            parts = [
                lax.ppermute(value, "depth", [(i, i ^ k) for i in range(depth_count)])
                for k in range(1, depth_count)
            ]
            for part in parts:
                value = jnp.maximum(value, part)
            return value
        if from_pair is not None:
            value = jnp.maximum(value, from_pair)
        step = first
        while step < depth_count:
            pairs = [(i, i ^ step) for i in range(depth_count)]
            value = jnp.maximum(value, lax.ppermute(value, "depth", pairs))
            step *= 2
        return value

    if shot_count == 2:
        other = send(velocity, "shot", swap)
        full_velocity = jnp.where(
            shot_at == 0,
            jnp.concatenate([velocity, other], axis=2),
            jnp.concatenate([other, velocity], axis=2),
        )
    else:
        full_velocity = lax.all_gather(velocity, "shot", axis=2, tiled=True)

    near_planes = (3 * shots + 1) * planes + shots
    hbm = pl.BlockSpec(memory_space=pl.ANY)
    spec = pl.BlockSpec(memory_space=pltpu.VMEM)
    to_even, to_odd, to_far, own_late = pl.pallas_call(
        pack_kernel,
        out_shape=(
            pltpu.VMEM((near_planes, rows, cols), jnp.float32),
            pltpu.VMEM((near_planes, rows, cols), jnp.float32),
            pltpu.VMEM((2, shots + 1, rows, cols), jnp.float32),
            pltpu.VMEM(adj_late.shape, jnp.float32),
        ),
        in_specs=[hbm] * 5,
        out_specs=(spec, spec, spec, spec),
        scratch_shapes=[pltpu.SemaphoreType.DMA((3 * shots + 2,))],
        compiler_params=pltpu.CompilerParams(vmem_limit_bytes=8 << 20),
        name="pack",
    )(fwd_now, fwd_prev, adj_last, density, adj_late)
    near_odd = send(to_odd, "depth", odds)
    far_first = send(to_far[0], "depth", two_pairs(depth_count, True))
    far_second = send(to_far[1], "depth", two_pairs(depth_count, False))
    near_even = send(to_even, "depth", evens)

    full_rows = rows * lat_count
    depth_start = depth_at * planes
    row_start = lat_at * rows

    def place(cells, margin):
        plane_at = cells // (full_rows * cols) - depth_start + margin
        row_at = cells // cols % full_rows - row_start + PAD
        inside = (
            (plane_at >= 0)
            & (plane_at < planes + 2 * margin)
            & (row_at >= 0)
            & (row_at < wide)
        )
        return jnp.where(inside, plane_at * wide + row_at, -1), cells % cols

    row_id, col_id = place(receiver_cell, 1)
    row_id, full_velocity = lax.optimization_barrier((row_id, full_velocity))
    vel_odd = send(full_velocity, "depth", odds)
    vel_even = send(full_velocity, "depth", evens)
    spread_shape = (shots, 3, (planes + 2) * wide, cols)
    (dense,) = on_chip(
        spread_kernel,
        [spread_shape],
        (row_id, col_id, observed),
        flops=14 * shots * spread_shape[2] * cols * row_id.shape[1],
        limit=24,
    )
    source_at = jnp.stack(place(source_cell, 2), axis=1)

    halos = (to_even, own_late) + (near_even, near_odd, far_first, far_second, full_velocity, vel_even, vel_odd)
    strips = shots * (4 * planes + 16) + 2 * planes + 10
    (edges,) = on_chip(edge_kernel, [(strips * PAD, cols)], halos)
    edges = send(edges, "lat", swap)

    deep, deeper = planes + 4, planes + 6
    model = (wide, cols)
    scalars = pl.BlockSpec(memory_space=pltpu.SMEM)
    prepared_shapes = [
        (shots, deep) + model,
        (shots, deep) + model,
        (shots, planes + 2) + model,
        (shots, planes + 2) + model,
        (shots, deep) + model,
        (shots, planes) + model,
        (deep,) + model,
        (planes + 5,) + model,
        (deep,) + model,
        (deep,) + model,
        (deep,) + model,
    ]
    vectors = halos + (edges, dense)
    prepared = pl.pallas_call(
        prepare_kernel,
        out_shape=tuple(pltpu.VMEM(shape, jnp.float32) for shape in prepared_shapes),
        in_specs=[spec] * len(vectors) + [scalars, scalars],
        out_specs=tuple(spec for _ in prepared_shapes),
        scratch_shapes=[
            pltpu.VMEM((shots, deeper) + model, jnp.float32),
            pltpu.VMEM((deeper,) + model, jnp.float32),
        ],
        compiler_params=pltpu.CompilerParams(vmem_limit_bytes=8 << 20),
        name="prepare",
    )(
        *[pltpu.with_memory_space_constraint(a, pltpu.VMEM) for a in vectors],
        source_at,
        wavelet,
    )
    lap, base, turn, late, last, low, stiff, cz, cx, cp, cm = prepared

    def gradient_of(stiff):
        (out,) = on_chip(
            update_kernel,
            [(planes, rows, cols)],
            (stiff, lap, base, turn, late, last, low, dense, cz, cx, cp, cm),
            scratch=[
                (shots, deep) + model,
                (shots, deep) + model,
                (shots, planes + 2) + model,
                (shots, planes) + model,
            ],
        )
        return out

    own_velocity = velocity
    for update_index in range(ITERS):
        mine, other = shot_terms(gradient_of(stiff))
        if update_index + 1 == ITERS:
            summed, largest = on_chip(
                last_sum_kernel, [(planes, rows, cols), (8, cols)], (mine, other)
            )
            largest = jnp.maximum(largest, lax.ppermute(largest, "lat", swap))
            largest = depth_max(largest)
            return tuple(
                on_chip(
                    finish_kernel,
                    [velocity.shape, velocity.shape],
                    (summed, largest, own_velocity),
                    keep=False,
                )
            )
        edge_rows = planes * PAD + 8
        summed, tail = on_chip(sum_kernel, [(planes, rows, cols), (edge_rows, cols)], (mine, other))
        got = lax.ppermute(tail, "lat", swap)
        (widened,) = on_chip(widen_kernel, [(planes * wide + 8, cols)], (summed, tail, got))
        by_even = send(widened, "depth", evens)
        by_odd = send(widened[: planes * wide], "depth", odds)
        largest = depth_max(widened[planes * wide :], by_even[planes * wide :])
        stiff, own_velocity = on_chip(
            restiff_kernel,
            [stiff.shape, velocity.shape],
            (stiff, widened, by_even, by_odd, largest, own_velocity),
        )


def solution(mesh):
    fields = P(("grp", "shot"), "depth", "lat", None)
    model = P(("grp", "depth"), "lat", "shot")
    placed = (
        fields,
        fields,
        fields,
        fields,
        model,
        P(("grp", "depth"), "lat", None),
        P(("grp", "shot"), None),
        P(("grp", "shot")),
        P(("grp", "shot"), None),
        P(("grp", "shot"), None, None),
    )

    return jax.shard_map(
        shards,
        mesh=mesh,
        in_specs=placed,
        out_specs=(model, model),
        check_vma=False,
    )
```

```python
import jax
import jax.numpy as jnp
from jax import lax
from jax.experimental import pallas as pl
from jax.experimental.pallas import tpu as pltpu
from jax.sharding import PartitionSpec as P


ITERS = 2

COURANT = 0.1
STEP_SIZE = 0.1
EPSILON = 1e-06
PAD = 8
NOW, PREV, LAST, LATE, DENS, VEL, LAP = range(7)


def even_pairs(count):
    return [(i, i ^ 1) for i in range(count) if i ^ 1 < count]


def odd_pairs(count):
    ups = [(i, i + 1) for i in range(1, count - 1, 2)]
    return ups + [(b, a) for a, b in ups]


def send(block, axis, pairs):
    if not pairs:
        return jnp.zeros_like(block)
    return lax.ppermute(block, axis, pairs)


def on_chip(kernel, out_shapes, args, scratch=(), flops=0, limit=8, keep=True):
    spec = pl.BlockSpec(memory_space=pltpu.VMEM)
    place = pltpu.VMEM if keep else jax.ShapeDtypeStruct
    outs = tuple(place(shape, jnp.float32) for shape in out_shapes)
    moved = sum(a.size * 4 for a in args)
    return pl.pallas_call(
        kernel,
        out_shape=outs,
        in_specs=[spec] * len(args),
        out_specs=tuple(spec for _ in outs),
        scratch_shapes=[pltpu.VMEM(shape, jnp.float32) for shape in scratch],
        compiler_params=pltpu.CompilerParams(vmem_limit_bytes=limit << 20),
        cost_estimate=pl.CostEstimate(flops=flops, bytes_accessed=moved, transcendentals=0),
    )(*[pltpu.with_memory_space_constraint(a, pltpu.VMEM) for a in args])


def copy_all(copies, sems):
    copies = [
        pltpu.make_async_copy(source, target, sems.at[index])
        for index, (source, target) in enumerate(copies)
    ]
    for copy in copies:
        copy.start()
    for copy in copies:
        copy.wait()


def first_kernel(now, dens, vel, out, edges, vel_buf, sems):
    shots, planes, rows, cols = now.shape
    count = shots * planes
    copies = [
        (now.at[shot], out.at[shot * planes : (shot + 1) * planes]) for shot in range(shots)
    ]
    copies += [(dens, out.at[count : count + planes]), (vel, vel_buf)]
    copy_all(copies, sems)
    lines = [vel_buf[at] for at in range(planes)]
    spare = cols - planes * vel.shape[2]
    if spare:
        lines.append(jnp.zeros((rows, spare), jnp.float32))
    out[count + planes] = jnp.concatenate(lines, axis=1)
    first = lax.axis_index("lat") == 0
    for at in range(count + planes):
        edges[at * PAD : (at + 1) * PAD] = jnp.where(
            first, out[at, rows - PAD :], out[at, :PAD]
        )


def second_kernel(prev, last, late, out, late_out, sems):
    shots, planes, _, _ = prev.shape
    copies = []
    start = 0
    for field in (prev, last):
        for shot in range(shots):
            copies.append((field.at[shot], out.at[start : start + planes]))
            start += planes
    copy_all(copies + [(late, late_out)], sems)


def spread_kernel(row_ref, col_ref, obs_ref, out_ref):
    shots, nrec = row_ref.shape
    rows, cols = out_ref.shape[2:]
    steps = obs_ref.shape[1]
    row_iota = lax.broadcasted_iota(jnp.int32, (rows, nrec), 0)
    col_iota = lax.broadcasted_iota(jnp.int32, (cols, nrec), 0)
    dims = (((1,), (1,)), ((), ()))
    for shot in range(shots):
        at_row = (row_ref[shot : shot + 1, :] == row_iota).astype(jnp.float32)
        at_row = at_row.astype(jnp.bfloat16)
        at_col = col_ref[shot : shot + 1, :] == col_iota
        ones = at_col.astype(jnp.float32).astype(jnp.bfloat16)
        out_ref[shot, 0] = lax.dot_general(
            at_row, ones, dims, preferred_element_type=jnp.float32
        )
        for step in range(steps):
            obs = obs_ref[shot, step : step + 1, :]
            high = obs.astype(jnp.bfloat16).astype(jnp.float32)
            rest = obs - high
            middle = rest.astype(jnp.bfloat16).astype(jnp.float32)
            low = rest - middle
            total = None
            for part in (high, middle, low):
                term = lax.dot_general(
                    at_row,
                    jnp.where(at_col, part, 0.0).astype(jnp.bfloat16),
                    dims,
                    preferred_element_type=jnp.float32,
                )
                total = term if total is None else total + term
            out_ref[shot, 1 + step] = total


class Halo:
    def __init__(self, first, second, late, first_by, second_by, third_by, vel):
        self.even = lax.axis_index("depth") % 2 == 0
        self.first, self.second, self.late, self.vel = first, second, late, vel
        self.first_by, self.second_by, self.third_by = first_by, second_by, third_by
        self.shots, self.planes, self.rows, self.cols = late.shape

    def pick(self, pair, upper, index):
        a, b = pair if upper else pair[::-1]
        return jnp.where(self.even, a[index], b[index])

    def plane(self, item):
        which, shot, at = item
        planes, shots = self.planes, self.shots
        inside = 0 <= at < planes
        upper = at >= planes
        step = at if inside else (at - planes if upper else planes + at)
        if which == VEL:
            return self.vel[at + 2]
        if which == LAP:
            return self.pick(self.third_by, upper, shots + shot)
        if which == LATE:
            return self.late[shot, at] if inside else self.pick(self.third_by, upper, shot)
        if which in (NOW, DENS):
            index = (shot if which == NOW else shots) * planes + step
            return self.first[index] if inside else self.pick(self.first_by, upper, index)
        index = ((0 if which == PREV else shots) + shot) * planes + step
        return self.second[index] if inside else self.pick(self.second_by, upper, index)

    def plane_list(self):
        planes = self.planes
        out = []
        for which, margin in ((NOW, 2), (PREV, 2), (LAST, 2), (LATE, 1)):
            for shot in range(self.shots):
                for at in range(-margin, planes + margin):
                    out.append((which, shot, at))
        for shot in range(self.shots):
            out += [(LAP, shot, -2), (LAP, shot, planes + 1)]
        for which in (DENS, VEL):
            for at in range(-2, planes + 2):
                out.append((which, 0, at))
        return out


def halo_of(refs):
    first, second, late, fe, fo, se, so, te, to, vel = refs
    return Halo(first, second, late, (fe, fo), (se, so), (te, to), vel)


def edge_kernel(*refs):
    halo = halo_of(refs[:-1])
    out = refs[-1]
    first = lax.axis_index("lat") == 0
    rows = halo.rows
    for index, item in enumerate(halo.plane_list()):
        value = halo.plane(item)
        out[index * PAD : (index + 1) * PAD] = jnp.where(first, value[rows - PAD :], value[:PAD])


def near_cols(value):
    lane = lax.broadcasted_iota(jnp.int32, value.shape, 1)
    cols = value.shape[1]
    above = jnp.where(lane == cols - 1, 0.0, pltpu.roll(value, cols - 1, 1))
    below = jnp.where(lane == 0, 0.0, pltpu.roll(value, 1, 1))
    return above, below


def laplace(field, at, cz, cx, cp, cm):
    middle = field(at)
    rows = middle.shape[0]
    flux = cx(at) * (pltpu.roll(middle, rows - 1, 0) - middle)
    total = flux - pltpu.roll(flux, 1, 0)
    above, below = near_cols(middle)
    total = total + (cp(at) * (above - middle) + cm(at) * (below - middle))
    return total + (cz(at) * (field(at + 1) - middle) + cz(at - 1) * (field(at - 1) - middle))


def inverse(density):
    inside = density > 0.0
    return jnp.where(inside, 1.0 / jnp.where(inside, density, 1.0), 0.0)


def with_rows(part, value, lat_at):
    low = jnp.where(lat_at == 1, part, 0.0)
    high = jnp.where(lat_at == 0, part, 0.0)
    return jnp.concatenate([low, value, high], axis=0)


def couple(buoy, at, cz, cx, cp, cm):
    plane = buoy(at)
    cz(at, 0.5 * (plane + buoy(at + 1)))
    cx(at, 0.5 * (plane + pltpu.roll(plane, plane.shape[0] - 1, 0)))
    above, below = near_cols(plane)
    cp(at, 0.5 * (plane + above))
    cm(at, 0.5 * (plane + below))


def third_kernel(first, by_even, by_odd, edges, late, to_even, to_odd, now_buf, buoy_buf, cz, cx, cp, cm):
    even = lax.axis_index("depth") % 2 == 0
    lat_at = lax.axis_index("lat")
    shots, planes, rows, cols = late.shape

    def whole(index, at):
        if 0 <= at < planes:
            place = index * planes + at
            return with_rows(edges[place * PAD : (place + 1) * PAD], first[place], lat_at)
        upper = at >= planes
        a, b = (by_even, by_odd) if upper else (by_odd, by_even)
        place = index * planes + (0 if upper else planes - 1)
        empty = jnp.zeros((PAD, cols), jnp.float32)
        return jnp.concatenate([empty, jnp.where(even, a[place], b[place]), empty], axis=0)

    for at in range(-1, planes + 1):
        buoy_buf[at + 1] = inverse(whole(shots, at))
        for shot in range(shots):
            now_buf[shot, at + 1] = whole(shot, at)

    def put(ref):
        def store(at, value):
            ref[at + 1] = value

        return store

    for at in range(-1, planes):
        couple(lambda k: buoy_buf[k + 1], at, put(cz), put(cx), put(cp), put(cm))
    for shot in range(shots):
        ends = [
            laplace(
                lambda k: now_buf[shot, k + 1],
                at,
                lambda k: cz[k + 1],
                lambda k: cx[k + 1],
                lambda k: cp[k + 1],
                lambda k: cm[k + 1],
            )[PAD : PAD + rows]
            for at in (planes - 2, 1)
        ]
        low, top = late[shot, 0], late[shot, planes - 1]
        to_even[shot] = jnp.where(even, top, low)
        to_odd[shot] = jnp.where(even, low, top)
        to_even[shots + shot] = jnp.where(even, ends[0], ends[1])
        to_odd[shots + shot] = jnp.where(even, ends[1], ends[0])


def prepare_kernel(
    first,
    second,
    late,
    first_even,
    first_odd,
    second_even,
    second_odd,
    third_even,
    third_odd,
    vel,
    edges,
    dense,
    source_at,
    wavelet,
    lap_out,
    base_out,
    turn_out,
    late_out,
    last_out,
    low_out,
    stiff_out,
    cz,
    cx,
    cp,
    cm,
    now_buf,
    buoy_buf,
):
    halo = Halo(
        first,
        second,
        late,
        (first_even, first_odd),
        (second_even, second_odd),
        (third_even, third_odd),
        vel,
    )
    lat_at = lax.axis_index("lat")
    rows, cols, shots, planes = halo.rows, halo.cols, halo.shots, halo.planes
    wide = rows + 2 * PAD
    where_is = {item: index for index, item in enumerate(halo.plane_list())}

    def whole(which, shot, at):
        item = (which, shot, at)
        index = where_is[item]
        return with_rows(edges[index * PAD : (index + 1) * PAD], halo.plane(item), lat_at)

    for at in range(-2, planes + 2):
        density = whole(DENS, 0, at)
        buoy_buf[at + 2] = inverse(density)
        speed = whole(VEL, 0, at) * COURANT
        stiff_out[at + 2] = speed * speed * density
        for shot in range(shots):
            now_buf[shot, at + 2] = whole(NOW, shot, at)

    def put(ref):
        def store(at, value):
            ref[at + 2] = value

        return store

    for at in range(-2, planes + 1):
        couple(lambda k: buoy_buf[k + 2], at, put(cz), put(cx), put(cp), put(cm))
    line = lax.broadcasted_iota(jnp.int32, (wide, cols), 0)
    column = lax.broadcasted_iota(jnp.int32, (wide, cols), 1)
    for shot in range(shots):
        for at in range(-2, planes + 2):
            here = (line + (at + 2) * wide == source_at[shot, 0]) & (column == source_at[shot, 1])
            middle = now_buf[shot, at + 2]
            if -1 <= at < planes + 1:
                lap_out[shot, at + 2] = laplace(
                    lambda k: now_buf[shot, k + 2],
                    at,
                    lambda k: cz[k + 2],
                    lambda k: cx[k + 2],
                    lambda k: cp[k + 2],
                    lambda k: cm[k + 2],
                )
            else:
                lap_out[shot, at + 2] = whole(LAP, shot, at)
            base_out[shot, at + 2] = (
                2.0 * middle - whole(PREV, shot, at) + jnp.where(here, wavelet[shot, 0], 0.0)
            )
            newest = whole(LAST, shot, at)
            last_out[shot, at + 2] = newest
            if -1 <= at < planes + 1:
                turn_out[shot, at + 1] = jnp.where(here, wavelet[shot, 1], 0.0) - middle
                late_out[shot, at + 1] = (
                    2.0 * newest
                    - whole(LATE, shot, at)
                    - dense[shot, 2, (at + 1) * wide : (at + 2) * wide]
                )
            if 0 <= at < planes:
                low_out[shot, at] = newest + dense[shot, 1, (at + 1) * wide : (at + 2) * wide]


def update_kernel(
    stiff,
    lap,
    base,
    turn,
    late,
    last,
    low,
    dense,
    cz_ref,
    cx_ref,
    cp_ref,
    cm_ref,
    out,
    second,
    scaled,
    upper,
    lap_second,
):
    shots, planes = low.shape[:2]
    wide, _ = low.shape[2:]
    cz = lambda k: cz_ref[k]
    cx = lambda k: cx_ref[k]
    cp = lambda k: cp_ref[k]
    cm = lambda k: cm_ref[k]
    for at in range(planes + 4):
        rigid = stiff[at]
        for shot in range(shots):
            second[shot, at] = base[shot, at] + rigid * lap[shot, at]
            scaled[shot, at] = rigid * last[shot, at]
    for at in range(1, planes + 3):
        rigid = stiff[at]
        for shot in range(shots):
            hits = dense[shot, 0, (at - 1) * wide : at * wide]
            lap_now = laplace(lambda k: second[shot, k], at, cz, cx, cp, cm)
            third = 2.0 * second[shot, at] + turn[shot, at - 1] + rigid * lap_now
            adj = late[shot, at - 1] + hits * third
            adj = adj + laplace(lambda k: scaled[shot, k], at, cz, cx, cp, cm)
            upper[shot, at - 1] = adj
            if 2 <= at < planes + 2:
                lap_second[shot, at - 2] = lap_now
    for at in range(1, planes + 3):
        for shot in range(shots):
            scaled[shot, at] = stiff[at] * upper[shot, at - 1]
    for at in range(2, planes + 2):
        total = None
        for shot in range(shots):
            hits = dense[shot, 0, (at - 1) * wide : at * wide]
            lower = 2.0 * upper[shot, at - 1] - low[shot, at - 2] + hits * second[shot, at]
            lower = lower + laplace(lambda k: scaled[shot, k], at, cz, cx, cp, cm)
            term = upper[shot, at - 1] * lap_second[shot, at - 2] + lower * lap[shot, at]
            total = term if total is None else total + term
        out[at - 2] = (stiff[at] * total)[PAD : wide - PAD]


def tile_max(value):
    planes, rows, cols = value.shape
    return jnp.max(jnp.abs(value).reshape(planes * rows // 8, 8, cols), axis=0)


def sum_kernel(mine, other, total, edges):
    value = mine[...] + other[...]
    total[...] = value
    first = lax.axis_index("lat") == 0
    planes, rows, _ = value.shape
    for at in range(planes):
        edges[at * PAD : (at + 1) * PAD] = jnp.where(
            first, value[at, rows - PAD :], value[at, :PAD]
        )
    edges[planes * PAD :] = tile_max(value)


def last_sum_kernel(mine, other, total, largest):
    value = mine[...] + other[...]
    total[...] = value
    largest[...] = tile_max(value)


def widen_kernel(total, mine, got, out):
    planes, rows, _ = total.shape
    wide = rows + 2 * PAD
    lat_at = lax.axis_index("lat")
    for at in range(planes):
        part = got[at * PAD : (at + 1) * PAD]
        start = at * wide
        out[start : start + PAD] = jnp.where(lat_at == 1, part, 0.0)
        out[start + PAD : start + PAD + rows] = total[at]
        out[start + PAD + rows : start + wide] = jnp.where(lat_at == 0, part, 0.0)
    out[planes * wide :] = jnp.maximum(mine[planes * PAD :], got[planes * PAD :])


def restiff_kernel(stiff, mine, by_even, by_odd, largest, velocity, stiff_out, vel_out):
    planes, rows, own = velocity.shape
    wide = rows + 2 * PAD
    even = lax.axis_index("depth") % 2 == 0
    shot_at = lax.axis_index("shot")
    cols = mine.shape[1]
    scale = jnp.max(jnp.max(largest[...], axis=1, keepdims=True), axis=0, keepdims=True) + EPSILON
    for at in range(-2, planes + 2):
        if 0 <= at < planes:
            value = mine[at * wide : (at + 1) * wide]
        else:
            upper = at >= planes
            step = at - planes if upper else planes + at
            first, second = (by_even, by_odd) if upper else (by_odd, by_even)
            value = jnp.where(
                even, first[step * wide : (step + 1) * wide], second[step * wide : (step + 1) * wide]
            )
        value = value / scale
        stiff_out[at + 2] = stiff[at + 2] * jnp.exp(-2.0 * STEP_SIZE * value)
        if 0 <= at < planes:
            shifted = pltpu.roll(value[PAD : PAD + rows], (cols - shot_at * own) % cols, 1)
            vel_out[at] = velocity[at] * jnp.exp(-STEP_SIZE * shifted[:, :own])


def finish_kernel(total, largest, velocity, vel_out, dir_out):
    planes, _, own = velocity.shape
    shot_at = lax.axis_index("shot")
    cols = total.shape[2]
    scale = jnp.max(jnp.max(largest[...], axis=1, keepdims=True), axis=0, keepdims=True) + EPSILON
    for at in range(planes):
        value = total[at] / scale
        shifted = pltpu.roll(value, (cols - shot_at * own) % cols, 1)[:, :own]
        dir_out[at] = shifted
        vel_out[at] = velocity[at] * jnp.exp(-STEP_SIZE * shifted)


def shards(
    fwd_prev,
    fwd_now,
    adj_late,
    adj_last,
    velocity,
    density,
    wavelet,
    source_cell,
    receiver_cell,
    observed,
):
    shots, planes, rows, cols = fwd_now.shape
    depth_count = lax.axis_size("depth")
    shot_count = lax.axis_size("shot")
    lat_count = lax.axis_size("lat")
    if planes != 2 or wavelet.shape[1] != 2 or lat_count != 2:
        raise ValueError("unsupported split")
    depth_at = lax.axis_index("depth")
    lat_at = lax.axis_index("lat")
    shot_at = lax.axis_index("shot")
    evens = even_pairs(depth_count)
    odds = odd_pairs(depth_count)
    swap = [(0, 1), (1, 0)]
    own_width = velocity.shape[2]
    wide = rows + 2 * PAD

    def shot_terms(block):
        if shot_count == 2:
            return block, lax.ppermute(block, "shot", swap)
        return lax.psum(block, "shot"), jnp.zeros_like(block)

    def depth_max(value, from_pair=None):
        if depth_count & (depth_count - 1):
            return lax.pmax(value, "depth")
        first = 1 if from_pair is None else 2
        if depth_count <= 4 and from_pair is None:
            parts = [
                lax.ppermute(value, "depth", [(i, i ^ k) for i in range(depth_count)])
                for k in range(1, depth_count)
            ]
            for part in parts:
                value = jnp.maximum(value, part)
            return value
        if from_pair is not None:
            value = jnp.maximum(value, from_pair)
        step = first
        while step < depth_count:
            pairs = [(i, i ^ step) for i in range(depth_count)]
            value = jnp.maximum(value, lax.ppermute(value, "depth", pairs))
            step *= 2
        return value

    hbm = pl.BlockSpec(memory_space=pltpu.HBM)
    spec = pl.BlockSpec(memory_space=pltpu.VMEM)

    def load(kernel, shapes, args, scratch, count):
        return pl.pallas_call(
            kernel,
            out_shape=tuple(pltpu.VMEM(shape, jnp.float32) for shape in shapes),
            in_specs=[hbm] * len(args),
            out_specs=tuple(spec for _ in shapes),
            scratch_shapes=scratch + [pltpu.SemaphoreType.DMA((count,))],
            compiler_params=pltpu.CompilerParams(vmem_limit_bytes=4 << 20),
        )(*[pltpu.with_memory_space_constraint(a, pltpu.HBM) for a in args])

    own_planes = (shots + 1) * planes
    first, first_edges = load(
        first_kernel,
        [(own_planes + 1, rows, cols), (own_planes * PAD, cols)],
        (fwd_now, density, velocity),
        [pltpu.VMEM(velocity.shape, jnp.float32)],
        shots + 2,
    )
    first_odd = send(first, "depth", odds)
    first_even = send(first, "depth", evens)
    first_edges = send(first_edges, "lat", swap)
    second, late = load(
        second_kernel,
        [(2 * shots * planes, rows, cols), adj_late.shape],
        (fwd_prev, adj_last, adj_late),
        [],
        2 * shots + 1,
    )
    second_odd = send(second, "depth", odds)
    second_even = send(second, "depth", evens)

    even = depth_at % 2 == 0
    lines = jnp.stack(
        [
            jnp.where(even, first_odd[own_planes], first_even[own_planes]),
            first[own_planes],
            jnp.where(even, first_even[own_planes], first_odd[own_planes]),
        ]
    )
    if shot_count == 2:
        other = send(lines, "shot", swap)
        parts = [jnp.where(shot_at == 0, lines, other), jnp.where(shot_at == 0, other, lines)]
    else:
        gathered = lax.all_gather(lines, "shot")
        parts = [gathered[k] for k in range(shot_count)]
    full_velocity = jnp.stack(
        [
            jnp.concatenate([p[block, :, k * own_width : (k + 1) * own_width] for p in parts], axis=1)
            for block in range(3)
            for k in range(planes)
        ]
    )
    small = (planes + 1, wide, cols)
    to_even, to_odd = on_chip(
        third_kernel,
        [(2 * shots, rows, cols)] * 2,
        (first, first_even, first_odd, first_edges, late),
        scratch=[(shots, planes + 2, wide, cols), (planes + 2, wide, cols)] + [small] * 4,
    )
    third_odd = send(to_odd, "depth", odds)
    third_even = send(to_even, "depth", evens)

    full_rows = rows * lat_count
    depth_start = depth_at * planes
    row_start = lat_at * rows

    def place(cells, margin):
        plane_at = cells // (full_rows * cols) - depth_start + margin
        row_at = cells // cols % full_rows - row_start + PAD
        inside = (
            (plane_at >= 0)
            & (plane_at < planes + 2 * margin)
            & (row_at >= 0)
            & (row_at < wide)
        )
        return jnp.where(inside, plane_at * wide + row_at, -1), cells % cols

    row_id, col_id = place(receiver_cell, 1)
    spread_shape = (shots, 3, (planes + 2) * wide, cols)
    (dense,) = on_chip(
        spread_kernel,
        [spread_shape],
        (row_id, col_id, observed),
        flops=14 * shots * spread_shape[2] * cols * row_id.shape[1],
        limit=24,
    )
    source_at = jnp.stack(place(source_cell, 2), axis=1)

    halos = (first, second, late, first_even, first_odd, second_even, second_odd)
    halos += (third_even, third_odd, full_velocity)
    strips = shots * (4 * planes + 16) + 2 * (planes + 4)
    (edges,) = on_chip(edge_kernel, [(strips * PAD, cols)], halos)
    edges = send(edges, "lat", swap)

    deep = planes + 4
    model = (wide, cols)
    scalars = pl.BlockSpec(memory_space=pltpu.SMEM)
    prepared_shapes = [
        (shots, deep) + model,
        (shots, deep) + model,
        (shots, planes + 2) + model,
        (shots, planes + 2) + model,
        (shots, deep) + model,
        (shots, planes) + model,
        (deep,) + model,
        (planes + 3,) + model,
        (planes + 3,) + model,
        (planes + 3,) + model,
        (planes + 3,) + model,
    ]
    vectors = halos + (edges, dense)
    prepared = pl.pallas_call(
        prepare_kernel,
        out_shape=tuple(pltpu.VMEM(shape, jnp.float32) for shape in prepared_shapes),
        in_specs=[spec] * len(vectors) + [scalars, scalars],
        out_specs=tuple(spec for _ in prepared_shapes),
        scratch_shapes=[
            pltpu.VMEM((shots, deep) + model, jnp.float32),
            pltpu.VMEM((deep,) + model, jnp.float32),
        ],
        compiler_params=pltpu.CompilerParams(vmem_limit_bytes=8 << 20),
        name="prepare",
    )(
        *[pltpu.with_memory_space_constraint(a, pltpu.VMEM) for a in vectors],
        source_at,
        wavelet,
    )
    lap, base, turn, late, last, low, stiff, cz, cx, cp, cm = prepared

    def gradient_of(stiff):
        (out,) = on_chip(
            update_kernel,
            [(planes, rows, cols)],
            (stiff, lap, base, turn, late, last, low, dense, cz, cx, cp, cm),
            scratch=[
                (shots, deep) + model,
                (shots, deep) + model,
                (shots, planes + 2) + model,
                (shots, planes) + model,
            ],
        )
        return out

    own_velocity = velocity
    for update_index in range(ITERS):
        mine, other = shot_terms(gradient_of(stiff))
        if update_index + 1 == ITERS:
            summed, largest = on_chip(
                last_sum_kernel, [(planes, rows, cols), (8, cols)], (mine, other)
            )
            largest = jnp.maximum(largest, lax.ppermute(largest, "lat", swap))
            largest = depth_max(largest)
            return tuple(
                on_chip(
                    finish_kernel,
                    [velocity.shape, velocity.shape],
                    (summed, largest, own_velocity),
                    keep=False,
                )
            )
        edge_rows = planes * PAD + 8
        summed, tail = on_chip(sum_kernel, [(planes, rows, cols), (edge_rows, cols)], (mine, other))
        got = lax.ppermute(tail, "lat", swap)
        (widened,) = on_chip(widen_kernel, [(planes * wide + 8, cols)], (summed, tail, got))
        by_even = send(widened, "depth", evens)
        by_odd = send(widened[: planes * wide], "depth", odds)
        largest = depth_max(widened[planes * wide :], by_even[planes * wide :])
        stiff, own_velocity = on_chip(
            restiff_kernel,
            [stiff.shape, velocity.shape],
            (stiff, widened, by_even, by_odd, largest, own_velocity),
        )


def solution(mesh):
    fields = P(("grp", "shot"), "depth", "lat", None)
    model = P(("grp", "depth"), "lat", "shot")
    placed = (
        fields,
        fields,
        fields,
        fields,
        model,
        P(("grp", "depth"), "lat", None),
        P(("grp", "shot"), None),
        P(("grp", "shot")),
        P(("grp", "shot"), None),
        P(("grp", "shot"), None, None),
    )

    return jax.shard_map(
        shards,
        mesh=mesh,
        in_specs=placed,
        out_specs=(model, model),
        check_vma=False,
    )
```

```python
import functools

import jax
import jax.numpy as jnp
from jax import lax
from jax.experimental import pallas as pl
from jax.experimental.pallas import tpu as pltpu
from jax.sharding import PartitionSpec as P


ITERS = 2

COURANT = 0.1
STEP_SIZE = 0.1
EPSILON = 1e-06
PAD = 8
NOW, PREV, LAST, LATE, DENS, VEL, LAP = range(7)


def even_pairs(count):
    return [(i, i ^ 1) for i in range(count) if i ^ 1 < count]


def odd_pairs(count):
    ups = [(i, i + 1) for i in range(1, count - 1, 2)]
    return ups + [(b, a) for a, b in ups]


def send(block, axis, pairs):
    if not pairs:
        return jnp.zeros_like(block)
    return lax.ppermute(block, axis, pairs)


def on_chip(kernel, out_shapes, args, scratch=(), flops=0, limit=8, keep=True):
    spec = pl.BlockSpec(memory_space=pltpu.VMEM)
    place = pltpu.VMEM if keep else jax.ShapeDtypeStruct
    outs = tuple(place(shape, jnp.float32) for shape in out_shapes)
    moved = sum(a.size * 4 for a in args)
    return pl.pallas_call(
        kernel,
        out_shape=outs,
        in_specs=[spec] * len(args),
        out_specs=tuple(spec for _ in outs),
        scratch_shapes=[pltpu.VMEM(shape, jnp.float32) for shape in scratch],
        compiler_params=pltpu.CompilerParams(vmem_limit_bytes=limit << 20),
        cost_estimate=pl.CostEstimate(flops=flops, bytes_accessed=moved, transcendentals=0),
    )(*[pltpu.with_memory_space_constraint(a, pltpu.VMEM) for a in args])


def copy_all(copies, sems):
    copies = [
        pltpu.make_async_copy(source, target, sems.at[index])
        for index, (source, target) in enumerate(copies)
    ]
    for copy in copies:
        copy.start()
    for copy in copies:
        copy.wait()


def first_kernel(now, dens, vel, out, edges, vel_buf, sems):
    shots, planes, rows, cols = now.shape
    count = shots * planes
    copies = [
        (now.at[shot], out.at[shot * planes : (shot + 1) * planes]) for shot in range(shots)
    ]
    copies += [(dens, out.at[count : count + planes]), (vel, vel_buf)]
    copy_all(copies, sems)
    lines = [vel_buf[at] for at in range(planes)]
    spare = cols - planes * vel.shape[2]
    if spare:
        lines.append(jnp.zeros((rows, spare), jnp.float32))
    out[count + planes] = jnp.concatenate(lines, axis=1)
    first = lax.axis_index("lat") == 0
    for at in range(count + planes):
        edges[at * PAD : (at + 1) * PAD] = jnp.where(
            first, out[at, rows - PAD :], out[at, :PAD]
        )


def second_kernel(prev, last, late, out, late_out, sems):
    shots, planes, _, _ = prev.shape
    copies = []
    start = 0
    for field in (prev, last):
        for shot in range(shots):
            copies.append((field.at[shot], out.at[start : start + planes]))
            start += planes
    copy_all(copies + [(late, late_out)], sems)


def spread_kernel(row_ref, col_ref, obs_ref, out_ref):
    nrec = row_ref.shape[1]
    rows, cols = out_ref.shape[1:]
    steps = obs_ref.shape[0]
    row_iota = lax.broadcasted_iota(jnp.int32, (rows, nrec), 0)
    col_iota = lax.broadcasted_iota(jnp.int32, (cols, nrec), 0)
    at_row = (row_ref[...] == row_iota).astype(jnp.float32).astype(jnp.bfloat16)
    at_col = col_ref[...] == col_iota
    parts = [(0, at_col.astype(jnp.float32).astype(jnp.bfloat16))]
    for step in range(steps):
        obs = obs_ref[step : step + 1, :]
        high = obs.astype(jnp.bfloat16).astype(jnp.float32)
        rest = obs - high
        middle = rest.astype(jnp.bfloat16).astype(jnp.float32)
        for piece in (high, middle, rest - middle):
            parts.append((1 + step, jnp.where(at_col, piece, 0.0).astype(jnp.bfloat16)))
    sums = [None] * (1 + steps)
    for start in range(0, len(parts), 2):
        pair = parts[start : start + 2]
        both = lax.dot_general(
            at_row,
            jnp.concatenate([p for _, p in pair], axis=0),
            (((1,), (1,)), ((), ())),
            preferred_element_type=jnp.float32,
        )
        for place, (which, _) in enumerate(pair):
            term = both[:, place * cols : (place + 1) * cols]
            sums[which] = term if sums[which] is None else sums[which] + term
    for which, value in enumerate(sums):
        out_ref[which] = value


class Halo:
    def __init__(self, first, second, late, first_by, second_by, third_by, vel):
        self.even = lax.axis_index("depth") % 2 == 0
        self.first, self.second, self.late, self.vel = first, second, late, vel
        self.first_by, self.second_by, self.third_by = first_by, second_by, third_by
        self.shots, self.planes, self.rows, self.cols = late.shape

    def pick(self, pair, upper, index):
        a, b = pair if upper else pair[::-1]
        return jnp.where(self.even, a[index], b[index])

    def plane(self, item):
        which, shot, at = item
        planes, shots = self.planes, self.shots
        inside = 0 <= at < planes
        upper = at >= planes
        step = at if inside else (at - planes if upper else planes + at)
        if which == VEL:
            block, lane = (0, 1, 2)[(at + planes) // planes], (at + planes) % planes
            own = self.cols // len(self.vel)
            column = lax.broadcasted_iota(jnp.int32, (self.rows, self.cols), 1)
            value = None
            for index, part in enumerate(self.vel):
                shifted = pltpu.roll(part[block], (index - lane) * own % self.cols, 1)
                value = shifted if value is None else jnp.where(column >= index * own, shifted, value)
            return value
        if which == LAP:
            return self.pick(self.third_by, upper, shots + shot)
        if which == LATE:
            return self.late[shot, at] if inside else self.pick(self.third_by, upper, shot)
        if which in (NOW, DENS):
            index = (shot if which == NOW else shots) * planes + step
            return self.first[index] if inside else self.pick(self.first_by, upper, index)
        index = ((0 if which == PREV else shots) + shot) * planes + step
        return self.second[index] if inside else self.pick(self.second_by, upper, index)

    def plane_list(self):
        planes = self.planes
        out = []
        for which, margin in ((NOW, 2), (PREV, 2), (LAST, 2), (LATE, 1)):
            for shot in range(self.shots):
                for at in range(-margin, planes + margin):
                    out.append((which, shot, at))
        for shot in range(self.shots):
            out += [(LAP, shot, -2), (LAP, shot, planes + 1)]
        for which in (DENS, VEL):
            for at in range(-2, planes + 2):
                out.append((which, 0, at))
        return out


def halo_of(refs):
    first, second, late, fe, fo, se, so, te, to, *vel = refs
    return Halo(first, second, late, (fe, fo), (se, so), (te, to), vel)


def edge_kernel(*refs):
    halo = halo_of(refs[:-1])
    out = refs[-1]
    first = lax.axis_index("lat") == 0
    rows = halo.rows
    for index, item in enumerate(halo.plane_list()):
        value = halo.plane(item)
        out[index * PAD : (index + 1) * PAD] = jnp.where(first, value[rows - PAD :], value[:PAD])


def near_cols(value):
    lane = lax.broadcasted_iota(jnp.int32, value.shape, 1)
    cols = value.shape[1]
    above = jnp.where(lane == cols - 1, 0.0, pltpu.roll(value, cols - 1, 1))
    below = jnp.where(lane == 0, 0.0, pltpu.roll(value, 1, 1))
    return above, below


def laplace(field, at, cz, cx, cp, cm):
    middle = field(at)
    rows = middle.shape[0]
    flux = cx(at) * (pltpu.roll(middle, rows - 1, 0) - middle)
    total = flux - pltpu.roll(flux, 1, 0)
    above, below = near_cols(middle)
    total = total + (cp(at) * (above - middle) + cm(at) * (below - middle))
    return total + (cz(at) * (field(at + 1) - middle) + cz(at - 1) * (field(at - 1) - middle))


def inverse(density):
    inside = density > 0.0
    return jnp.where(inside, 1.0 / jnp.where(inside, density, 1.0), 0.0)


def with_rows(part, value, lat_at):
    low = jnp.where(lat_at == 1, part, 0.0)
    high = jnp.where(lat_at == 0, part, 0.0)
    return jnp.concatenate([low, value, high], axis=0)


def couple(buoy, at, cz, cx, cp, cm):
    plane = buoy(at)
    cz(at, 0.5 * (plane + buoy(at + 1)))
    cx(at, 0.5 * (plane + pltpu.roll(plane, plane.shape[0] - 1, 0)))
    above, below = near_cols(plane)
    cp(at, 0.5 * (plane + above))
    cm(at, 0.5 * (plane + below))


def third_kernel(first, by_even, by_odd, edges, late, to_even, to_odd, now_buf, buoy_buf, cz, cx, cp, cm):
    even = lax.axis_index("depth") % 2 == 0
    lat_at = lax.axis_index("lat")
    shots, planes, rows, cols = late.shape

    def whole(index, at):
        if 0 <= at < planes:
            place = index * planes + at
            return with_rows(edges[place * PAD : (place + 1) * PAD], first[place], lat_at)
        upper = at >= planes
        a, b = (by_even, by_odd) if upper else (by_odd, by_even)
        place = index * planes + (0 if upper else planes - 1)
        empty = jnp.zeros((PAD, cols), jnp.float32)
        return jnp.concatenate([empty, jnp.where(even, a[place], b[place]), empty], axis=0)

    for at in range(-1, planes + 1):
        buoy_buf[at + 1] = inverse(whole(shots, at))
        for shot in range(shots):
            now_buf[shot, at + 1] = whole(shot, at)

    def put(ref):
        def store(at, value):
            ref[at + 1] = value

        return store

    for at in range(-1, planes):
        couple(lambda k: buoy_buf[k + 1], at, put(cz), put(cx), put(cp), put(cm))
    for shot in range(shots):
        ends = [
            laplace(
                lambda k: now_buf[shot, k + 1],
                at,
                lambda k: cz[k + 1],
                lambda k: cx[k + 1],
                lambda k: cp[k + 1],
                lambda k: cm[k + 1],
            )[PAD : PAD + rows]
            for at in (planes - 2, 1)
        ]
        low, top = late[shot, 0], late[shot, planes - 1]
        to_even[shot] = jnp.where(even, top, low)
        to_odd[shot] = jnp.where(even, low, top)
        to_even[shots + shot] = jnp.where(even, ends[0], ends[1])
        to_odd[shots + shot] = jnp.where(even, ends[1], ends[0])


def prepare_kernel(halos, shots, *refs):
    halo = halo_of(refs[:halos])
    edges, *dense = refs[halos : halos + 1 + shots]
    source_at, wavelet = refs[halos + 1 + shots : halos + 3 + shots]
    outs = refs[halos + 3 + shots :]
    lap_out, base_out, turn_out, late_out, last_out, low_out, stiff_out = outs[:7]
    cz, cx, cp, cm, now_buf, buoy_buf = outs[7:]
    lat_at = lax.axis_index("lat")
    rows, cols, planes = halo.rows, halo.cols, halo.planes
    wide = rows + 2 * PAD
    where_is = {item: index for index, item in enumerate(halo.plane_list())}

    def whole(which, shot, at):
        item = (which, shot, at)
        index = where_is[item]
        return with_rows(edges[index * PAD : (index + 1) * PAD], halo.plane(item), lat_at)

    for at in range(-2, planes + 2):
        density = whole(DENS, 0, at)
        buoy_buf[at + 2] = inverse(density)
        speed = whole(VEL, 0, at) * COURANT
        stiff_out[at + 2] = speed * speed * density
        for shot in range(shots):
            now_buf[shot, at + 2] = whole(NOW, shot, at)

    def put(ref):
        def store(at, value):
            ref[at + 2] = value

        return store

    for at in range(-2, planes + 1):
        couple(lambda k: buoy_buf[k + 2], at, put(cz), put(cx), put(cp), put(cm))
    line = lax.broadcasted_iota(jnp.int32, (wide, cols), 0)
    column = lax.broadcasted_iota(jnp.int32, (wide, cols), 1)
    for shot in range(shots):
        for at in range(-2, planes + 2):
            here = (line + (at + 2) * wide == source_at[shot, 0]) & (column == source_at[shot, 1])
            middle = now_buf[shot, at + 2]
            if -1 <= at < planes + 1:
                lap_out[shot, at + 2] = laplace(
                    lambda k: now_buf[shot, k + 2],
                    at,
                    lambda k: cz[k + 2],
                    lambda k: cx[k + 2],
                    lambda k: cp[k + 2],
                    lambda k: cm[k + 2],
                )
            else:
                lap_out[shot, at + 2] = whole(LAP, shot, at)
            base_out[shot, at + 2] = (
                2.0 * middle - whole(PREV, shot, at) + jnp.where(here, wavelet[shot, 0], 0.0)
            )
            newest = whole(LAST, shot, at)
            last_out[shot, at + 2] = newest
            if -1 <= at < planes + 1:
                turn_out[shot, at + 1] = jnp.where(here, wavelet[shot, 1], 0.0) - middle
                late_out[shot, at + 1] = (
                    2.0 * newest
                    - whole(LATE, shot, at)
                    - dense[shot][2, (at + 1) * wide : (at + 2) * wide]
                )
            if 0 <= at < planes:
                low_out[shot, at] = newest + dense[shot][1, (at + 1) * wide : (at + 2) * wide]


def update_kernel(shots, *refs):
    stiff, lap, base, turn, late, last, low, cz_ref, cx_ref, cp_ref, cm_ref = refs[:11]
    dense = refs[11 : 11 + shots]
    out, second, scaled, upper, lap_second = refs[11 + shots :]
    planes = low.shape[1]
    wide, _ = low.shape[2:]
    cz = lambda k: cz_ref[k]
    cx = lambda k: cx_ref[k]
    cp = lambda k: cp_ref[k]
    cm = lambda k: cm_ref[k]
    for at in range(planes + 4):
        rigid = stiff[at]
        for shot in range(shots):
            second[shot, at] = base[shot, at] + rigid * lap[shot, at]
            scaled[shot, at] = rigid * last[shot, at]
    for at in range(1, planes + 3):
        rigid = stiff[at]
        for shot in range(shots):
            hits = dense[shot][0, (at - 1) * wide : at * wide]
            lap_now = laplace(lambda k: second[shot, k], at, cz, cx, cp, cm)
            third = 2.0 * second[shot, at] + turn[shot, at - 1] + rigid * lap_now
            adj = late[shot, at - 1] + hits * third
            adj = adj + laplace(lambda k: scaled[shot, k], at, cz, cx, cp, cm)
            upper[shot, at - 1] = adj
            if 2 <= at < planes + 2:
                lap_second[shot, at - 2] = lap_now
    for at in range(1, planes + 3):
        for shot in range(shots):
            scaled[shot, at] = stiff[at] * upper[shot, at - 1]
    for at in range(2, planes + 2):
        total = None
        for shot in range(shots):
            hits = dense[shot][0, (at - 1) * wide : at * wide]
            lower = 2.0 * upper[shot, at - 1] - low[shot, at - 2] + hits * second[shot, at]
            lower = lower + laplace(lambda k: scaled[shot, k], at, cz, cx, cp, cm)
            term = upper[shot, at - 1] * lap_second[shot, at - 2] + lower * lap[shot, at]
            total = term if total is None else total + term
        out[at - 2] = (stiff[at] * total)[PAD : wide - PAD]


def tile_max(value):
    planes, rows, cols = value.shape
    return jnp.max(jnp.abs(value).reshape(planes * rows // 8, 8, cols), axis=0)


def sum_kernel(mine, other, total, edges):
    value = mine[...] + other[...]
    total[...] = value
    first = lax.axis_index("lat") == 0
    planes, rows, _ = value.shape
    for at in range(planes):
        edges[at * PAD : (at + 1) * PAD] = jnp.where(
            first, value[at, rows - PAD :], value[at, :PAD]
        )
    edges[planes * PAD :] = tile_max(value)


def last_sum_kernel(mine, other, total, largest):
    value = mine[...] + other[...]
    total[...] = value
    largest[...] = tile_max(value)


def widen_kernel(total, mine, got, out, largest):
    planes, rows, _ = total.shape
    wide = rows + 2 * PAD
    lat_at = lax.axis_index("lat")
    for at in range(planes):
        part = got[at * PAD : (at + 1) * PAD]
        start = at * wide
        out[start : start + PAD] = jnp.where(lat_at == 1, part, 0.0)
        out[start + PAD : start + PAD + rows] = total[at]
        out[start + PAD + rows : start + wide] = jnp.where(lat_at == 0, part, 0.0)
    largest[...] = jnp.maximum(mine[planes * PAD :], got[planes * PAD :])


def restiff_kernel(stiff, mine, by_even, by_odd, largest, velocity, stiff_out, vel_out):
    planes, rows, own = velocity.shape
    wide = rows + 2 * PAD
    even = lax.axis_index("depth") % 2 == 0
    shot_at = lax.axis_index("shot")
    cols = mine.shape[1]
    scale = jnp.max(jnp.max(largest[...], axis=1, keepdims=True), axis=0, keepdims=True) + EPSILON
    for at in range(-2, planes + 2):
        if 0 <= at < planes:
            value = mine[at * wide : (at + 1) * wide]
        else:
            upper = at >= planes
            step = at - planes if upper else planes + at
            first, second = (by_even, by_odd) if upper else (by_odd, by_even)
            value = jnp.where(
                even, first[step * wide : (step + 1) * wide], second[step * wide : (step + 1) * wide]
            )
        value = value / scale
        stiff_out[at + 2] = stiff[at + 2] * jnp.exp(-2.0 * STEP_SIZE * value)
        if 0 <= at < planes:
            shifted = pltpu.roll(value[PAD : PAD + rows], (cols - shot_at * own) % cols, 1)
            vel_out[at] = velocity[at] * jnp.exp(-STEP_SIZE * shifted[:, :own])


def finish_kernel(total, largest, velocity, vel_out, dir_out):
    planes, _, own = velocity.shape
    shot_at = lax.axis_index("shot")
    cols = total.shape[2]
    scale = jnp.max(jnp.max(largest[...], axis=1, keepdims=True), axis=0, keepdims=True) + EPSILON
    for at in range(planes):
        value = total[at] / scale
        shifted = pltpu.roll(value, (cols - shot_at * own) % cols, 1)[:, :own]
        dir_out[at] = shifted
        vel_out[at] = velocity[at] * jnp.exp(-STEP_SIZE * shifted)


def shards(
    fwd_prev,
    fwd_now,
    adj_late,
    adj_last,
    velocity,
    density,
    wavelet,
    source_cell,
    receiver_cell,
    observed,
):
    shots, planes, rows, cols = fwd_now.shape
    depth_count = lax.axis_size("depth")
    shot_count = lax.axis_size("shot")
    lat_count = lax.axis_size("lat")
    if planes != 2 or wavelet.shape[1] != 2 or lat_count != 2:
        raise ValueError("unsupported split")
    depth_at = lax.axis_index("depth")
    lat_at = lax.axis_index("lat")
    shot_at = lax.axis_index("shot")
    evens = even_pairs(depth_count)
    odds = odd_pairs(depth_count)
    swap = [(0, 1), (1, 0)]
    wide = rows + 2 * PAD

    def shot_terms(block):
        if shot_count == 2:
            return block, lax.ppermute(block, "shot", swap)
        return lax.psum(block, "shot"), jnp.zeros_like(block)

    def depth_max(value, from_pair=None):
        if depth_count & (depth_count - 1):
            return lax.pmax(value, "depth")
        first = 1 if from_pair is None else 2
        if depth_count <= 4 and from_pair is None:
            parts = [
                lax.ppermute(value, "depth", [(i, i ^ k) for i in range(depth_count)])
                for k in range(1, depth_count)
            ]
            for part in parts:
                value = jnp.maximum(value, part)
            return value
        if from_pair is not None:
            value = jnp.maximum(value, from_pair)
        step = first
        while step < depth_count:
            pairs = [(i, i ^ step) for i in range(depth_count)]
            value = jnp.maximum(value, send(value, "depth", pairs))
            step *= 2
        return value

    hbm = pl.BlockSpec(memory_space=pltpu.HBM)
    spec = pl.BlockSpec(memory_space=pltpu.VMEM)

    def load(kernel, shapes, args, scratch, count):
        return pl.pallas_call(
            kernel,
            out_shape=tuple(pltpu.VMEM(shape, jnp.float32) for shape in shapes),
            in_specs=[hbm] * len(args),
            out_specs=tuple(spec for _ in shapes),
            scratch_shapes=scratch + [pltpu.SemaphoreType.DMA((count,))],
            compiler_params=pltpu.CompilerParams(vmem_limit_bytes=4 << 20),
        )(*[pltpu.with_memory_space_constraint(a, pltpu.HBM) for a in args])

    own_planes = (shots + 1) * planes
    first, first_edges = load(
        first_kernel,
        [(own_planes + 1, rows, cols), (own_planes * PAD, cols)],
        (fwd_now, density, velocity),
        [pltpu.VMEM(velocity.shape, jnp.float32)],
        shots + 2,
    )
    first_odd = send(first, "depth", odds)
    first_even = send(first, "depth", evens)
    first_edges = send(first_edges, "lat", swap)
    second, late = load(
        second_kernel,
        [(2 * shots * planes, rows, cols), adj_late.shape],
        (fwd_prev, adj_last, adj_late),
        [],
        2 * shots + 1,
    )
    second_odd = send(second, "depth", odds)
    second_even = send(second, "depth", evens)

    even = depth_at % 2 == 0
    lines = jnp.stack(
        [
            jnp.where(even, first_odd[own_planes], first_even[own_planes]),
            first[own_planes],
            jnp.where(even, first_even[own_planes], first_odd[own_planes]),
        ]
    )
    if shot_count == 2:
        other = send(lines, "shot", swap)
        parts = [jnp.where(shot_at == 0, lines, other), jnp.where(shot_at == 0, other, lines)]
    else:
        gathered = lax.all_gather(lines, "shot")
        parts = [gathered[k] for k in range(shot_count)]
    small = (planes + 1, wide, cols)
    to_even, to_odd = on_chip(
        third_kernel,
        [(2 * shots, rows, cols)] * 2,
        (first, first_even, first_odd, first_edges, late),
        scratch=[(shots, planes + 2, wide, cols), (planes + 2, wide, cols)] + [small] * 4,
    )
    third_odd = send(to_odd, "depth", odds)
    third_even = send(to_even, "depth", evens)

    full_rows = rows * lat_count
    depth_start = depth_at * planes
    row_start = lat_at * rows

    def place(cells, margin):
        plane_at = cells // (full_rows * cols) - depth_start + margin
        row_at = cells // cols % full_rows - row_start + PAD
        inside = (
            (plane_at >= 0)
            & (plane_at < planes + 2 * margin)
            & (row_at >= 0)
            & (row_at < wide)
        )
        return jnp.where(inside, plane_at * wide + row_at, -1), cells % cols

    row_id, col_id = place(receiver_cell, 1)
    spread_shape = (3, (planes + 2) * wide, cols)

    def receivers(shot):
        (out,) = on_chip(
            spread_kernel,
            [spread_shape],
            (row_id[shot : shot + 1], col_id[shot : shot + 1], observed[shot]),
            flops=14 * spread_shape[1] * cols * row_id.shape[1],
            limit=24,
        )
        return out

    dense = []
    for shot in range(shots):
        dense.append(receivers(shot))
    dense = tuple(dense)
    source_at = jnp.stack(place(source_cell, 2), axis=1)

    halos = (first, second, late, first_even, first_odd, second_even, second_odd)
    halos += (third_even, third_odd) + tuple(parts)
    strips = shots * (4 * planes + 16) + 2 * (planes + 4)
    (edges,) = on_chip(edge_kernel, [(strips * PAD, cols)], halos)
    edges = send(edges, "lat", swap)

    deep = planes + 4
    model = (wide, cols)
    scalars = pl.BlockSpec(memory_space=pltpu.SMEM)
    prepared_shapes = [
        (shots, deep) + model,
        (shots, deep) + model,
        (shots, planes + 2) + model,
        (shots, planes + 2) + model,
        (shots, deep) + model,
        (shots, planes) + model,
        (deep,) + model,
        (planes + 3,) + model,
        (planes + 3,) + model,
        (planes + 3,) + model,
        (planes + 3,) + model,
    ]
    vectors = halos + (edges,) + dense
    prepared = pl.pallas_call(
        functools.partial(prepare_kernel, len(halos), shots),
        out_shape=tuple(pltpu.VMEM(shape, jnp.float32) for shape in prepared_shapes),
        in_specs=[spec] * len(vectors) + [scalars, scalars],
        out_specs=tuple(spec for _ in prepared_shapes),
        scratch_shapes=[
            pltpu.VMEM((shots, deep) + model, jnp.float32),
            pltpu.VMEM((deep,) + model, jnp.float32),
        ],
        compiler_params=pltpu.CompilerParams(vmem_limit_bytes=8 << 20),
        name="prepare",
    )(
        *[pltpu.with_memory_space_constraint(a, pltpu.VMEM) for a in vectors],
        source_at,
        wavelet,
    )
    lap, base, turn, late, last, low, stiff, cz, cx, cp, cm = prepared

    def gradient_of(stiff):
        (out,) = on_chip(
            functools.partial(update_kernel, shots),
            [(planes, rows, cols)],
            (stiff, lap, base, turn, late, last, low, cz, cx, cp, cm) + dense,
            scratch=[
                (shots, deep) + model,
                (shots, deep) + model,
                (shots, planes + 2) + model,
                (shots, planes) + model,
            ],
        )
        return out

    own_velocity = velocity
    for update_index in range(ITERS):
        mine, other = shot_terms(gradient_of(stiff))
        if update_index + 1 == ITERS:
            summed, largest = on_chip(
                last_sum_kernel, [(planes, rows, cols), (8, cols)], (mine, other)
            )
            largest = jnp.maximum(largest, lax.ppermute(largest, "lat", swap))
            largest = depth_max(largest)
            return tuple(
                on_chip(
                    finish_kernel,
                    [velocity.shape, velocity.shape],
                    (summed, largest, own_velocity),
                    keep=False,
                )
            )
        edge_rows = planes * PAD + 8
        summed, tail = on_chip(sum_kernel, [(planes, rows, cols), (edge_rows, cols)], (mine, other))
        got = lax.ppermute(tail, "lat", swap)
        widened, largest = on_chip(
            widen_kernel, [(planes * wide, cols), (8, cols)], (summed, tail, got)
        )
        if depth_count & (depth_count - 1):
            largest = lax.pmax(largest, "depth")
        else:
            from_pair = send(largest, "depth", evens)
        by_even = send(widened, "depth", evens)
        by_odd = send(widened, "depth", odds)
        if not depth_count & (depth_count - 1):
            largest = depth_max(largest, from_pair)
        stiff, own_velocity = on_chip(
            restiff_kernel,
            [stiff.shape, velocity.shape],
            (stiff, widened, by_even, by_odd, largest, own_velocity),
        )


def solution(mesh):
    fields = P(("grp", "shot"), "depth", "lat", None)
    model = P(("grp", "depth"), "lat", "shot")
    placed = (
        fields,
        fields,
        fields,
        fields,
        model,
        P(("grp", "depth"), "lat", None),
        P(("grp", "shot"), None),
        P(("grp", "shot")),
        P(("grp", "shot"), None),
        P(("grp", "shot"), None, None),
    )

    return jax.shard_map(
        shards,
        mesh=mesh,
        in_specs=placed,
        out_specs=(model, model),
        check_vma=False,
    )
```

```python
import functools

import jax
import jax.numpy as jnp
from jax import lax
from jax.experimental import pallas as pl
from jax.experimental.pallas import tpu as pltpu
from jax.sharding import PartitionSpec as P


ITERS = 2

COURANT = 0.1
STEP_SIZE = 0.1
EPSILON = 1e-06
PAD = 8
NOW, PREV, LAST, LATE, DENS, VEL, LAP = range(7)


def even_pairs(count):
    return [(i, i ^ 1) for i in range(count) if i ^ 1 < count]


def odd_pairs(count):
    ups = [(i, i + 1) for i in range(1, count - 1, 2)]
    return ups + [(b, a) for a, b in ups]


def send(block, axis, pairs):
    if not pairs:
        return jnp.zeros_like(block)
    return lax.ppermute(block, axis, pairs)


def on_chip(kernel, out_shapes, args, scratch=(), flops=0, limit=8, keep=True):
    spec = pl.BlockSpec(memory_space=pltpu.VMEM)
    place = pltpu.VMEM if keep else jax.ShapeDtypeStruct
    outs = tuple(place(shape, jnp.float32) for shape in out_shapes)
    moved = sum(a.size * 4 for a in args)
    return pl.pallas_call(
        kernel,
        out_shape=outs,
        in_specs=[spec] * len(args),
        out_specs=tuple(spec for _ in outs),
        scratch_shapes=[pltpu.VMEM(shape, jnp.float32) for shape in scratch],
        compiler_params=pltpu.CompilerParams(vmem_limit_bytes=limit << 20),
        cost_estimate=pl.CostEstimate(flops=flops, bytes_accessed=moved, transcendentals=0),
    )(*[pltpu.with_memory_space_constraint(a, pltpu.VMEM) for a in args])


def copy_all(copies, sems):
    copies = [
        pltpu.make_async_copy(source, target, sems.at[index])
        for index, (source, target) in enumerate(copies)
    ]
    for copy in copies:
        copy.start()
    for copy in copies:
        copy.wait()


def first_kernel(now, dens, vel, out, edges, vel_buf, sems):
    shots, planes, rows, cols = now.shape
    count = shots * planes
    copies = [
        (now.at[shot], out.at[shot * planes : (shot + 1) * planes]) for shot in range(shots)
    ]
    copies += [(dens, out.at[count : count + planes]), (vel, vel_buf)]
    copy_all(copies, sems)
    lines = [vel_buf[at] for at in range(planes)]
    spare = cols - planes * vel.shape[2]
    if spare:
        lines.append(jnp.zeros((rows, spare), jnp.float32))
    out[count + planes] = jnp.concatenate(lines, axis=1)
    first = lax.axis_index("lat") == 0
    for at in range(count + planes):
        edges[at * PAD : (at + 1) * PAD] = jnp.where(
            first, out[at, rows - PAD :], out[at, :PAD]
        )


def second_kernel(prev, last, late, cells, observed, out, late_out, cells_out, observed_out, sems):
    shots, planes, _, _ = prev.shape
    copies = []
    start = 0
    for field in (prev, last):
        for shot in range(shots):
            copies.append((field.at[shot], out.at[start : start + planes]))
            start += planes
    copies += [(late, late_out), (cells, cells_out), (observed, observed_out)]
    copy_all(copies, sems)


def spread_kernel(row_ref, col_ref, obs_ref, out_ref):
    nrec = row_ref.shape[1]
    rows, cols = out_ref.shape[1:]
    steps = obs_ref.shape[0]
    row_iota = lax.broadcasted_iota(jnp.int32, (rows, nrec), 0)
    col_iota = lax.broadcasted_iota(jnp.int32, (cols, nrec), 0)
    at_row = (row_ref[...] == row_iota).astype(jnp.float32).astype(jnp.bfloat16)
    at_col = col_ref[...] == col_iota
    parts = [(0, at_col.astype(jnp.float32).astype(jnp.bfloat16))]
    for step in range(steps):
        obs = obs_ref[step : step + 1, :]
        high = obs.astype(jnp.bfloat16).astype(jnp.float32)
        rest = obs - high
        middle = rest.astype(jnp.bfloat16).astype(jnp.float32)
        for piece in (high, middle, rest - middle):
            parts.append((1 + step, jnp.where(at_col, piece, 0.0).astype(jnp.bfloat16)))
    sums = [None] * (1 + steps)
    for start in range(0, len(parts), 2):
        pair = parts[start : start + 2]
        both = lax.dot_general(
            at_row,
            jnp.concatenate([p for _, p in pair], axis=0),
            (((1,), (1,)), ((), ())),
            preferred_element_type=jnp.float32,
        )
        for place, (which, _) in enumerate(pair):
            term = both[:, place * cols : (place + 1) * cols]
            sums[which] = term if sums[which] is None else sums[which] + term
    for which, value in enumerate(sums):
        out_ref[which] = value


class Halo:
    def __init__(self, first, second, late, first_by, second_by, third_by, vel):
        self.even = lax.axis_index("depth") % 2 == 0
        self.first, self.second, self.late, self.vel = first, second, late, vel
        self.first_by, self.second_by, self.third_by = first_by, second_by, third_by
        self.shots, self.planes, self.rows, self.cols = late.shape

    def pick(self, pair, upper, index):
        a, b = pair if upper else pair[::-1]
        return jnp.where(self.even, a[index], b[index])

    def plane(self, item):
        which, shot, at = item
        planes, shots = self.planes, self.shots
        inside = 0 <= at < planes
        upper = at >= planes
        step = at if inside else (at - planes if upper else planes + at)
        if which == VEL:
            block, lane = (0, 1, 2)[(at + planes) // planes], (at + planes) % planes
            own = self.cols // len(self.vel)
            column = lax.broadcasted_iota(jnp.int32, (self.rows, self.cols), 1)
            value = None
            for index, part in enumerate(self.vel):
                shifted = pltpu.roll(part[block], (index - lane) * own % self.cols, 1)
                value = shifted if value is None else jnp.where(column >= index * own, shifted, value)
            return value
        if which == LAP:
            return self.pick(self.third_by, upper, shots + shot)
        if which == LATE:
            return self.late[shot, at] if inside else self.pick(self.third_by, upper, shot)
        if which in (NOW, DENS):
            index = (shot if which == NOW else shots) * planes + step
            return self.first[index] if inside else self.pick(self.first_by, upper, index)
        index = ((0 if which == PREV else shots) + shot) * planes + step
        return self.second[index] if inside else self.pick(self.second_by, upper, index)

    def plane_list(self):
        planes = self.planes
        out = []
        for which, margin in ((NOW, 2), (PREV, 2), (LAST, 2), (LATE, 1)):
            for shot in range(self.shots):
                for at in range(-margin, planes + margin):
                    out.append((which, shot, at))
        for shot in range(self.shots):
            out += [(LAP, shot, -2), (LAP, shot, planes + 1)]
        for which in (DENS, VEL):
            for at in range(-2, planes + 2):
                out.append((which, 0, at))
        return out


def halo_of(refs):
    first, second, late, fe, fo, se, so, te, to, *vel = refs
    return Halo(first, second, late, (fe, fo), (se, so), (te, to), vel)


def edge_kernel(*refs):
    halo = halo_of(refs[:-1])
    out = refs[-1]
    first = lax.axis_index("lat") == 0
    rows = halo.rows
    for index, item in enumerate(halo.plane_list()):
        value = halo.plane(item)
        out[index * PAD : (index + 1) * PAD] = jnp.where(first, value[rows - PAD :], value[:PAD])


def near_cols(value):
    lane = lax.broadcasted_iota(jnp.int32, value.shape, 1)
    cols = value.shape[1]
    above = jnp.where(lane == cols - 1, 0.0, pltpu.roll(value, cols - 1, 1))
    below = jnp.where(lane == 0, 0.0, pltpu.roll(value, 1, 1))
    return above, below


def laplace(field, at, cz, cx, cp, cm):
    middle = field(at)
    rows = middle.shape[0]
    flux = cx(at) * (pltpu.roll(middle, rows - 1, 0) - middle)
    total = flux - pltpu.roll(flux, 1, 0)
    above, below = near_cols(middle)
    total = total + (cp(at) * (above - middle) + cm(at) * (below - middle))
    return total + (cz(at) * (field(at + 1) - middle) + cz(at - 1) * (field(at - 1) - middle))


def inverse(density):
    inside = density > 0.0
    return jnp.where(inside, 1.0 / jnp.where(inside, density, 1.0), 0.0)


def with_rows(part, value, lat_at):
    low = jnp.where(lat_at == 1, part, 0.0)
    high = jnp.where(lat_at == 0, part, 0.0)
    return jnp.concatenate([low, value, high], axis=0)


def couple(buoy, at, cz, cx, cp, cm):
    plane = buoy(at)
    cz(at, 0.5 * (plane + buoy(at + 1)))
    cx(at, 0.5 * (plane + pltpu.roll(plane, plane.shape[0] - 1, 0)))
    above, below = near_cols(plane)
    cp(at, 0.5 * (plane + above))
    cm(at, 0.5 * (plane + below))


def third_kernel(first, by_even, by_odd, edges, late, to_even, to_odd, now_buf, buoy_buf, cz, cx, cp, cm):
    even = lax.axis_index("depth") % 2 == 0
    lat_at = lax.axis_index("lat")
    shots, planes, rows, cols = late.shape

    def whole(index, at):
        if 0 <= at < planes:
            place = index * planes + at
            return with_rows(edges[place * PAD : (place + 1) * PAD], first[place], lat_at)
        upper = at >= planes
        a, b = (by_even, by_odd) if upper else (by_odd, by_even)
        place = index * planes + (0 if upper else planes - 1)
        empty = jnp.zeros((PAD, cols), jnp.float32)
        return jnp.concatenate([empty, jnp.where(even, a[place], b[place]), empty], axis=0)

    for at in range(-1, planes + 1):
        buoy_buf[at + 1] = inverse(whole(shots, at))
        for shot in range(shots):
            now_buf[shot, at + 1] = whole(shot, at)

    def put(ref):
        def store(at, value):
            ref[at + 1] = value

        return store

    for at in range(-1, planes):
        couple(lambda k: buoy_buf[k + 1], at, put(cz), put(cx), put(cp), put(cm))
    for shot in range(shots):
        ends = [
            laplace(
                lambda k: now_buf[shot, k + 1],
                at,
                lambda k: cz[k + 1],
                lambda k: cx[k + 1],
                lambda k: cp[k + 1],
                lambda k: cm[k + 1],
            )[PAD : PAD + rows]
            for at in (planes - 2, 1)
        ]
        low, top = late[shot, 0], late[shot, planes - 1]
        to_even[shot] = jnp.where(even, top, low)
        to_odd[shot] = jnp.where(even, low, top)
        to_even[shots + shot] = jnp.where(even, ends[0], ends[1])
        to_odd[shots + shot] = jnp.where(even, ends[1], ends[0])


def prepare_kernel(halos, shots, *refs):
    halo = halo_of(refs[:halos])
    edges, *dense = refs[halos : halos + 1 + shots]
    source_at, wavelet = refs[halos + 1 + shots : halos + 3 + shots]
    outs = refs[halos + 3 + shots :]
    lap_out, base_out, turn_out, late_out, last_out, low_out, stiff_out = outs[:7]
    cz, cx, cp, cm, now_buf, buoy_buf = outs[7:]
    lat_at = lax.axis_index("lat")
    rows, cols, planes = halo.rows, halo.cols, halo.planes
    wide = rows + 2 * PAD
    where_is = {item: index for index, item in enumerate(halo.plane_list())}

    def whole(which, shot, at):
        item = (which, shot, at)
        index = where_is[item]
        return with_rows(edges[index * PAD : (index + 1) * PAD], halo.plane(item), lat_at)

    for at in range(-2, planes + 2):
        density = whole(DENS, 0, at)
        buoy_buf[at + 2] = inverse(density)
        speed = whole(VEL, 0, at) * COURANT
        stiff_out[at + 2] = speed * speed * density
        for shot in range(shots):
            now_buf[shot, at + 2] = whole(NOW, shot, at)

    def put(ref):
        def store(at, value):
            ref[at + 2] = value

        return store

    for at in range(-2, planes + 1):
        couple(lambda k: buoy_buf[k + 2], at, put(cz), put(cx), put(cp), put(cm))
    line = lax.broadcasted_iota(jnp.int32, (wide, cols), 0)
    column = lax.broadcasted_iota(jnp.int32, (wide, cols), 1)
    for shot in range(shots):
        for at in range(-2, planes + 2):
            here = (line + (at + 2) * wide == source_at[shot, 0]) & (column == source_at[shot, 1])
            middle = now_buf[shot, at + 2]
            if -1 <= at < planes + 1:
                lap_out[shot, at + 2] = laplace(
                    lambda k: now_buf[shot, k + 2],
                    at,
                    lambda k: cz[k + 2],
                    lambda k: cx[k + 2],
                    lambda k: cp[k + 2],
                    lambda k: cm[k + 2],
                )
            else:
                lap_out[shot, at + 2] = whole(LAP, shot, at)
            base_out[shot, at + 2] = (
                2.0 * middle - whole(PREV, shot, at) + jnp.where(here, wavelet[shot, 0], 0.0)
            )
            newest = whole(LAST, shot, at)
            last_out[shot, at + 2] = newest
            if -1 <= at < planes + 1:
                turn_out[shot, at + 1] = jnp.where(here, wavelet[shot, 1], 0.0) - middle
                late_out[shot, at + 1] = (
                    2.0 * newest
                    - whole(LATE, shot, at)
                    - dense[shot][2, (at + 1) * wide : (at + 2) * wide]
                )
            if 0 <= at < planes:
                low_out[shot, at] = newest + dense[shot][1, (at + 1) * wide : (at + 2) * wide]


def update_kernel(shots, *refs):
    stiff, lap, base, turn, late, last, low, cz_ref, cx_ref, cp_ref, cm_ref = refs[:11]
    dense = refs[11 : 11 + shots]
    out, second, scaled, upper, lap_second = refs[11 + shots :]
    planes = low.shape[1]
    wide, _ = low.shape[2:]
    cz = lambda k: cz_ref[k]
    cx = lambda k: cx_ref[k]
    cp = lambda k: cp_ref[k]
    cm = lambda k: cm_ref[k]
    for at in range(planes + 4):
        rigid = stiff[at]
        for shot in range(shots):
            second[shot, at] = base[shot, at] + rigid * lap[shot, at]
            scaled[shot, at] = rigid * last[shot, at]
    for at in range(1, planes + 3):
        rigid = stiff[at]
        for shot in range(shots):
            hits = dense[shot][0, (at - 1) * wide : at * wide]
            lap_now = laplace(lambda k: second[shot, k], at, cz, cx, cp, cm)
            third = 2.0 * second[shot, at] + turn[shot, at - 1] + rigid * lap_now
            adj = late[shot, at - 1] + hits * third
            adj = adj + laplace(lambda k: scaled[shot, k], at, cz, cx, cp, cm)
            upper[shot, at - 1] = adj
            if 2 <= at < planes + 2:
                lap_second[shot, at - 2] = lap_now
    for at in range(1, planes + 3):
        for shot in range(shots):
            scaled[shot, at] = stiff[at] * upper[shot, at - 1]
    for at in range(2, planes + 2):
        total = None
        for shot in range(shots):
            hits = dense[shot][0, (at - 1) * wide : at * wide]
            lower = 2.0 * upper[shot, at - 1] - low[shot, at - 2] + hits * second[shot, at]
            lower = lower + laplace(lambda k: scaled[shot, k], at, cz, cx, cp, cm)
            term = upper[shot, at - 1] * lap_second[shot, at - 2] + lower * lap[shot, at]
            total = term if total is None else total + term
        out[at - 2] = (stiff[at] * total)[PAD : wide - PAD]


def tile_max(value):
    planes, rows, cols = value.shape
    return jnp.max(jnp.abs(value).reshape(planes * rows // 8, 8, cols), axis=0)


def sum_kernel(mine, other, total, edges):
    value = mine[...] + other[...]
    total[...] = value
    first = lax.axis_index("lat") == 0
    planes, rows, _ = value.shape
    for at in range(planes):
        edges[at * PAD : (at + 1) * PAD] = jnp.where(
            first, value[at, rows - PAD :], value[at, :PAD]
        )
    edges[planes * PAD :] = tile_max(value)


def last_sum_kernel(mine, other, total, largest):
    value = mine[...] + other[...]
    total[...] = value
    largest[...] = tile_max(value)


def halo_edge_kernel(by_even, by_odd, out):
    even = lax.axis_index("depth") % 2 == 0
    first = lax.axis_index("lat") == 0
    planes, rows, _ = by_even.shape
    for side, (a, b) in enumerate(((by_odd, by_even), (by_even, by_odd))):
        for at in range(planes):
            value = jnp.where(even, a[at], b[at])
            start = (side * planes + at) * PAD
            out[start : start + PAD] = jnp.where(first, value[rows - PAD :], value[:PAD])


def restiff_kernel(stiff, total, got, by_even, by_odd, got_halo, largest, velocity, stiff_out, vel_out):
    planes, rows, own = velocity.shape
    even = lax.axis_index("depth") % 2 == 0
    shot_at = lax.axis_index("shot")
    lat_at = lax.axis_index("lat")
    cols = total.shape[2]
    scale = jnp.max(jnp.max(largest[...], axis=1, keepdims=True), axis=0, keepdims=True) + EPSILON
    for at in range(-2, planes + 2):
        if 0 <= at < planes:
            value, part = total[at], got[at * PAD : (at + 1) * PAD]
        else:
            upper = at >= planes
            step = at - planes if upper else planes + at
            a, b = (by_even, by_odd) if upper else (by_odd, by_even)
            value = jnp.where(even, a[step], b[step])
            start = (upper * planes + step) * PAD
            part = got_halo[start : start + PAD]
        value = with_rows(part, value, lat_at) / scale
        stiff_out[at + 2] = stiff[at + 2] * jnp.exp(-2.0 * STEP_SIZE * value)
        if 0 <= at < planes:
            shifted = pltpu.roll(value[PAD : PAD + rows], (cols - shot_at * own) % cols, 1)
            vel_out[at] = velocity[at] * jnp.exp(-STEP_SIZE * shifted[:, :own])


def finish_kernel(total, largest, velocity, vel_out, dir_out):
    planes, _, own = velocity.shape
    shot_at = lax.axis_index("shot")
    cols = total.shape[2]
    scale = jnp.max(jnp.max(largest[...], axis=1, keepdims=True), axis=0, keepdims=True) + EPSILON
    for at in range(planes):
        value = total[at] / scale
        shifted = pltpu.roll(value, (cols - shot_at * own) % cols, 1)[:, :own]
        dir_out[at] = shifted
        vel_out[at] = velocity[at] * jnp.exp(-STEP_SIZE * shifted)


def shards(
    fwd_prev,
    fwd_now,
    adj_late,
    adj_last,
    velocity,
    density,
    wavelet,
    source_cell,
    receiver_cell,
    observed,
):
    shots, planes, rows, cols = fwd_now.shape
    depth_count = lax.axis_size("depth")
    shot_count = lax.axis_size("shot")
    lat_count = lax.axis_size("lat")
    if depth_count < 2 or planes != 2 or wavelet.shape[1] != 2 or lat_count != 2:
        raise ValueError("unsupported split")
    depth_at = lax.axis_index("depth")
    lat_at = lax.axis_index("lat")
    shot_at = lax.axis_index("shot")
    evens = even_pairs(depth_count)
    odds = odd_pairs(depth_count)
    swap = [(0, 1), (1, 0)]
    wide = rows + 2 * PAD

    def shot_terms(block):
        if shot_count == 2:
            return block, lax.ppermute(block, "shot", swap)
        return lax.psum(block, "shot"), jnp.zeros_like(block)

    def depth_max(value):
        if depth_count & (depth_count - 1):
            return lax.pmax(value, "depth")
        if depth_count <= 4:
            parts = [
                send(value, "depth", [(i, i ^ k) for i in range(depth_count)])
                for k in range(1, depth_count)
            ]
            for part in parts:
                value = jnp.maximum(value, part)
            return value
        step = 1
        while step < depth_count:
            pairs = [(i, i ^ step) for i in range(depth_count)]
            value = jnp.maximum(value, send(value, "depth", pairs))
            step *= 2
        return value

    hbm = pl.BlockSpec(memory_space=pltpu.HBM)
    spec = pl.BlockSpec(memory_space=pltpu.VMEM)

    def load(kernel, shapes, args, scratch, count):
        return pl.pallas_call(
            kernel,
            out_shape=tuple(pltpu.VMEM(*shape) for shape in shapes),
            in_specs=[hbm] * len(args),
            out_specs=tuple(spec for _ in shapes),
            scratch_shapes=scratch + [pltpu.SemaphoreType.DMA((count,))],
            compiler_params=pltpu.CompilerParams(vmem_limit_bytes=4 << 20),
        )(*[pltpu.with_memory_space_constraint(a, pltpu.HBM) for a in args])

    own_planes = (shots + 1) * planes
    first, first_edges = load(
        first_kernel,
        [((own_planes + 1, rows, cols), jnp.float32), ((own_planes * PAD, cols), jnp.float32)],
        (fwd_now, density, velocity),
        [pltpu.VMEM(velocity.shape, jnp.float32)],
        shots + 2,
    )
    first_odd = send(first, "depth", odds)
    first_even = send(first, "depth", evens)
    first_edges = send(first_edges, "lat", swap)
    second, late, cells, recorded = load(
        second_kernel,
        [
            ((2 * shots * planes, rows, cols), jnp.float32),
            (adj_late.shape, jnp.float32),
            (receiver_cell.shape, receiver_cell.dtype),
            (observed.shape, jnp.float32),
        ],
        (fwd_prev, adj_last, adj_late, receiver_cell, observed),
        [],
        2 * shots + 3,
    )
    second_odd = send(second, "depth", odds)
    second_even = send(second, "depth", evens)

    even = depth_at % 2 == 0
    lines = jnp.stack(
        [
            jnp.where(even, first_odd[own_planes], first_even[own_planes]),
            first[own_planes],
            jnp.where(even, first_even[own_planes], first_odd[own_planes]),
        ]
    )
    if shot_count == 2:
        other = send(lines, "shot", swap)
        parts = [jnp.where(shot_at == 0, lines, other), jnp.where(shot_at == 0, other, lines)]
    else:
        gathered = lax.all_gather(lines, "shot")
        parts = [gathered[k] for k in range(shot_count)]
    small = (planes + 1, wide, cols)
    to_even, to_odd = on_chip(
        third_kernel,
        [(2 * shots, rows, cols)] * 2,
        (first, first_even, first_odd, first_edges, late),
        scratch=[(shots, planes + 2, wide, cols), (planes + 2, wide, cols)] + [small] * 4,
    )
    third_odd = send(to_odd, "depth", odds)
    third_even = send(to_even, "depth", evens)

    full_rows = rows * lat_count
    depth_start = depth_at * planes
    row_start = lat_at * rows

    def place(cells, margin):
        plane_at = cells // (full_rows * cols) - depth_start + margin
        row_at = cells // cols % full_rows - row_start + PAD
        inside = (
            (plane_at >= 0)
            & (plane_at < planes + 2 * margin)
            & (row_at >= 0)
            & (row_at < wide)
        )
        return jnp.where(inside, plane_at * wide + row_at, -1), cells % cols

    row_id, col_id = place(cells, 1)
    spread_shape = (3, (planes + 2) * wide, cols)

    def receivers(shot):
        (out,) = on_chip(
            spread_kernel,
            [spread_shape],
            (row_id[shot : shot + 1], col_id[shot : shot + 1], recorded[shot]),
            flops=14 * spread_shape[1] * cols * row_id.shape[1],
            limit=24,
        )
        return out

    dense = []
    for shot in range(shots):
        dense.append(receivers(shot))
    dense = tuple(dense)
    source_at = jnp.stack(place(source_cell, 2), axis=1)

    halos = (first, second, late, first_even, first_odd, second_even, second_odd)
    halos += (third_even, third_odd) + tuple(parts)
    strips = shots * (4 * planes + 16) + 2 * (planes + 4)
    (edges,) = on_chip(edge_kernel, [(strips * PAD, cols)], halos)
    edges = send(edges, "lat", swap)

    deep = planes + 4
    model = (wide, cols)
    scalars = pl.BlockSpec(memory_space=pltpu.SMEM)
    prepared_shapes = [
        (shots, deep) + model,
        (shots, deep) + model,
        (shots, planes + 2) + model,
        (shots, planes + 2) + model,
        (shots, deep) + model,
        (shots, planes) + model,
        (deep,) + model,
        (planes + 3,) + model,
        (planes + 3,) + model,
        (planes + 3,) + model,
        (planes + 3,) + model,
    ]
    vectors = halos + (edges,) + dense
    prepared = pl.pallas_call(
        functools.partial(prepare_kernel, len(halos), shots),
        out_shape=tuple(pltpu.VMEM(shape, jnp.float32) for shape in prepared_shapes),
        in_specs=[spec] * len(vectors) + [scalars, scalars],
        out_specs=tuple(spec for _ in prepared_shapes),
        scratch_shapes=[
            pltpu.VMEM((shots, deep) + model, jnp.float32),
            pltpu.VMEM((deep,) + model, jnp.float32),
        ],
        compiler_params=pltpu.CompilerParams(vmem_limit_bytes=8 << 20),
        name="prepare",
    )(
        *[pltpu.with_memory_space_constraint(a, pltpu.VMEM) for a in vectors],
        source_at,
        wavelet,
    )
    lap, base, turn, late, last, low, stiff, cz, cx, cp, cm = prepared

    def gradient_of(stiff):
        (out,) = on_chip(
            functools.partial(update_kernel, shots),
            [(planes, rows, cols)],
            (stiff, lap, base, turn, late, last, low, cz, cx, cp, cm) + dense,
            scratch=[
                (shots, deep) + model,
                (shots, deep) + model,
                (shots, planes + 2) + model,
                (shots, planes) + model,
            ],
        )
        return out

    own_velocity = velocity
    for update_index in range(ITERS):
        mine, other = shot_terms(gradient_of(stiff))
        if update_index + 1 == ITERS:
            summed, largest = on_chip(
                last_sum_kernel, [(planes, rows, cols), (8, cols)], (mine, other)
            )
            largest = jnp.maximum(largest, lax.ppermute(largest, "lat", swap))
            largest = depth_max(largest)
            return tuple(
                on_chip(
                    finish_kernel,
                    [velocity.shape, velocity.shape],
                    (summed, largest, own_velocity),
                    keep=False,
                )
            )
        edge_rows = planes * PAD + 8
        summed, tail = on_chip(sum_kernel, [(planes, rows, cols), (edge_rows, cols)], (mine, other))
        got = send(tail, "lat", swap)
        by_even = send(summed, "depth", evens)
        by_odd = send(summed, "depth", odds)
        largest = depth_max(jnp.maximum(tail[planes * PAD :], got[planes * PAD :]))
        (halo_tail,) = on_chip(halo_edge_kernel, [(2 * planes * PAD, cols)], (by_even, by_odd))
        got_halo = send(halo_tail, "lat", swap)
        stiff, own_velocity = on_chip(
            restiff_kernel,
            [stiff.shape, velocity.shape],
            (stiff, summed, got, by_even, by_odd, got_halo, largest, own_velocity),
        )


def solution(mesh):
    fields = P(("grp", "shot"), "depth", "lat", None)
    model = P(("grp", "depth"), "lat", "shot")
    placed = (
        fields,
        fields,
        fields,
        fields,
        model,
        P(("grp", "depth"), "lat", None),
        P(("grp", "shot"), None),
        P(("grp", "shot")),
        P(("grp", "shot"), None),
        P(("grp", "shot"), None, None),
    )

    return jax.shard_map(
        shards,
        mesh=mesh,
        in_specs=placed,
        out_specs=(model, model),
        check_vma=False,
    )
```

```python
import functools

import jax
import jax.numpy as jnp
from jax import lax
from jax.experimental import pallas as pl
from jax.experimental.pallas import tpu as pltpu
from jax.sharding import PartitionSpec as P


ITERS = 2

COURANT = 0.1
STEP_SIZE = 0.1
EPSILON = 1e-06
PAD = 8
NOW, PREV, LAST, LATE, DENS, VEL, LAP = range(7)


def even_pairs(count):
    return [(i, i ^ 1) for i in range(count) if i ^ 1 < count]


def odd_pairs(count):
    ups = [(i, i + 1) for i in range(1, count - 1, 2)]
    return ups + [(b, a) for a, b in ups]


def send(block, axis, pairs):
    if not pairs:
        return jnp.zeros_like(block)
    return lax.ppermute(block, axis, pairs)


def on_chip(kernel, out_shapes, args, scratch=(), flops=0, limit=8, keep=True):
    spec = pl.BlockSpec(memory_space=pltpu.VMEM)
    place = pltpu.VMEM if keep else jax.ShapeDtypeStruct
    outs = tuple(place(shape, jnp.float32) for shape in out_shapes)
    moved = sum(a.size * 4 for a in args)
    return pl.pallas_call(
        kernel,
        out_shape=outs,
        in_specs=[spec] * len(args),
        out_specs=tuple(spec for _ in outs),
        scratch_shapes=[pltpu.VMEM(shape, jnp.float32) for shape in scratch],
        compiler_params=pltpu.CompilerParams(vmem_limit_bytes=limit << 20),
        cost_estimate=pl.CostEstimate(flops=flops, bytes_accessed=moved, transcendentals=0),
    )(*[pltpu.with_memory_space_constraint(a, pltpu.VMEM) for a in args])


def copy_all(copies, sems):
    copies = [
        pltpu.make_async_copy(source, target, sems.at[index])
        for index, (source, target) in enumerate(copies)
    ]
    for copy in copies:
        copy.start()
    for copy in copies:
        copy.wait()


def first_kernel(now, dens, vel, out, edges, vel_buf, sems):
    shots, planes, rows, cols = now.shape
    count = shots * planes
    copies = [
        (now.at[shot], out.at[shot * planes : (shot + 1) * planes]) for shot in range(shots)
    ]
    copies += [(dens, out.at[count : count + planes]), (vel, vel_buf)]
    copy_all(copies, sems)
    lines = [vel_buf[at] for at in range(planes)]
    spare = cols - planes * vel.shape[2]
    if spare:
        lines.append(jnp.zeros((rows, spare), jnp.float32))
    out[count + planes] = jnp.concatenate(lines, axis=1)
    first = lax.axis_index("lat") == 0
    for at in range(count + planes):
        edges[at * PAD : (at + 1) * PAD] = jnp.where(
            first, out[at, rows - PAD :], out[at, :PAD]
        )


def second_kernel(prev, last, late, cells, observed, out, late_out, cells_out, observed_out, sems):
    shots, planes, _, _ = prev.shape
    copies = []
    start = 0
    for field in (prev, last):
        for shot in range(shots):
            copies.append((field.at[shot], out.at[start : start + planes]))
            start += planes
    copies += [(late, late_out), (cells, cells_out), (observed, observed_out)]
    copy_all(copies, sems)


def spread_kernel(row_ref, col_ref, obs_ref, out_ref):
    nrec = row_ref.shape[1]
    rows, cols = out_ref.shape[1:]
    steps = obs_ref.shape[0]
    row_iota = lax.broadcasted_iota(jnp.int32, (rows, nrec), 0)
    col_iota = lax.broadcasted_iota(jnp.int32, (cols, nrec), 0)
    at_row = (row_ref[...] == row_iota).astype(jnp.float32).astype(jnp.bfloat16)
    at_col = col_ref[...] == col_iota
    parts = [(0, at_col.astype(jnp.float32).astype(jnp.bfloat16))]
    for step in range(steps):
        obs = obs_ref[step : step + 1, :]
        high = obs.astype(jnp.bfloat16).astype(jnp.float32)
        rest = obs - high
        middle = rest.astype(jnp.bfloat16).astype(jnp.float32)
        for piece in (high, middle, rest - middle):
            parts.append((1 + step, jnp.where(at_col, piece, 0.0).astype(jnp.bfloat16)))
    sums = [None] * (1 + steps)
    for start in range(0, len(parts), 2):
        pair = parts[start : start + 2]
        both = lax.dot_general(
            at_row,
            jnp.concatenate([p for _, p in pair], axis=0),
            (((1,), (1,)), ((), ())),
            preferred_element_type=jnp.float32,
        )
        for place, (which, _) in enumerate(pair):
            term = both[:, place * cols : (place + 1) * cols]
            sums[which] = term if sums[which] is None else sums[which] + term
    for which, value in enumerate(sums):
        out_ref[which] = value


class Halo:
    def __init__(self, shape, first=None, second=None, late=None, by=(), vel=()):
        self.even = lax.axis_index("depth") % 2 == 0
        self.first, self.second, self.late, self.vel = first, second, late, vel
        self.by = by
        self.shots, self.planes, self.rows, self.cols = shape

    def pick(self, batch, upper, index):
        even, odd = self.by[batch]
        a, b = (even, odd) if upper else (odd, even)
        return jnp.where(self.even, a[index], b[index])

    def plane(self, item):
        which, shot, at = item
        planes, shots = self.planes, self.shots
        inside = 0 <= at < planes
        upper = at >= planes
        step = at if inside else (at - planes if upper else planes + at)
        if which == VEL:
            block, lane = (0, 1, 2)[(at + planes) // planes], (at + planes) % planes
            own = self.cols // len(self.vel)
            column = lax.broadcasted_iota(jnp.int32, (self.rows, self.cols), 1)
            value = None
            for index, part in enumerate(self.vel):
                shifted = pltpu.roll(part[block], (index - lane) * own % self.cols, 1)
                value = shifted if value is None else jnp.where(column >= index * own, shifted, value)
            return value
        if which == LAP:
            return self.pick("third", upper, shots + shot)
        if which == LATE:
            return self.late[shot, at] if inside else self.pick("third", upper, shot)
        if which in (NOW, DENS):
            index = (shot if which == NOW else shots) * planes + step
            return self.first[index] if inside else self.pick("first", upper, index)
        index = ((0 if which == PREV else shots) + shot) * planes + step
        return self.second[index] if inside else self.pick("second", upper, index)

    def early_list(self):
        planes = self.planes
        out = []
        for which, margin in ((NOW, 2), (PREV, 2), (LAST, 2), (LATE, 0)):
            for shot in range(self.shots):
                for at in range(-margin, planes + margin):
                    out.append((which, shot, at))
        return out + [(DENS, 0, at) for at in range(-2, planes + 2)]

    def final_list(self):
        planes = self.planes
        out = []
        for shot in range(self.shots):
            out += [(LATE, shot, -1), (LATE, shot, planes), (LAP, shot, -2), (LAP, shot, planes + 1)]
        return out + [(VEL, 0, at) for at in range(-2, planes + 2)]


def write_edges(halo, items, out):
    first = lax.axis_index("lat") == 0
    rows = halo.rows
    for index, item in enumerate(items):
        value = halo.plane(item)
        out[index * PAD : (index + 1) * PAD] = jnp.where(first, value[rows - PAD :], value[:PAD])


def reader(halo, items, edges):
    lat_at = lax.axis_index("lat")
    where_is = {item: index for index, item in enumerate(items)}

    def whole(which, shot, at):
        item = (which, shot, at)
        index = where_is[item]
        return with_rows(edges[index * PAD : (index + 1) * PAD], halo.plane(item), lat_at)

    return whole


def early_halo(first, second, late, fe, fo, se, so):
    return Halo(late.shape, first, second, late, {"first": (fe, fo), "second": (se, so)})


def final_halo(shape, te, to, *vel):
    return Halo(shape, by={"third": (te, to)}, vel=vel)


def early_edge_kernel(*refs):
    halo = early_halo(*refs[:7])
    write_edges(halo, halo.early_list(), refs[7])


def final_edge_kernel(shape, *refs):
    halo = final_halo(shape, *refs[:-1])
    write_edges(halo, halo.final_list(), refs[-1])


def near_cols(value):
    lane = lax.broadcasted_iota(jnp.int32, value.shape, 1)
    cols = value.shape[1]
    above = jnp.where(lane == cols - 1, 0.0, pltpu.roll(value, cols - 1, 1))
    below = jnp.where(lane == 0, 0.0, pltpu.roll(value, 1, 1))
    return above, below


def laplace(field, at, cz, cx, cp, cm):
    middle = field(at)
    rows = middle.shape[0]
    flux = cx(at) * (pltpu.roll(middle, rows - 1, 0) - middle)
    total = flux - pltpu.roll(flux, 1, 0)
    above, below = near_cols(middle)
    total = total + (cp(at) * (above - middle) + cm(at) * (below - middle))
    return total + (cz(at) * (field(at + 1) - middle) + cz(at - 1) * (field(at - 1) - middle))


def inverse(density):
    inside = density > 0.0
    return jnp.where(inside, 1.0 / jnp.where(inside, density, 1.0), 0.0)


def with_rows(part, value, lat_at):
    low = jnp.where(lat_at == 1, part, 0.0)
    high = jnp.where(lat_at == 0, part, 0.0)
    return jnp.concatenate([low, value, high], axis=0)


def couple(buoy, at, cz, cx, cp, cm):
    plane = buoy(at)
    cz(at, 0.5 * (plane + buoy(at + 1)))
    cx(at, 0.5 * (plane + pltpu.roll(plane, plane.shape[0] - 1, 0)))
    above, below = near_cols(plane)
    cp(at, 0.5 * (plane + above))
    cm(at, 0.5 * (plane + below))


def third_kernel(first, by_even, by_odd, edges, late, to_even, to_odd, now_buf, buoy_buf, cz, cx, cp, cm):
    even = lax.axis_index("depth") % 2 == 0
    lat_at = lax.axis_index("lat")
    shots, planes, rows, cols = late.shape

    def whole(index, at):
        if 0 <= at < planes:
            place = index * planes + at
            return with_rows(edges[place * PAD : (place + 1) * PAD], first[place], lat_at)
        upper = at >= planes
        a, b = (by_even, by_odd) if upper else (by_odd, by_even)
        place = index * planes + (0 if upper else planes - 1)
        empty = jnp.zeros((PAD, cols), jnp.float32)
        return jnp.concatenate([empty, jnp.where(even, a[place], b[place]), empty], axis=0)

    for at in range(-1, planes + 1):
        buoy_buf[at + 1] = inverse(whole(shots, at))
        for shot in range(shots):
            now_buf[shot, at + 1] = whole(shot, at)

    def put(ref):
        def store(at, value):
            ref[at + 1] = value

        return store

    for at in range(-1, planes):
        couple(lambda k: buoy_buf[k + 1], at, put(cz), put(cx), put(cp), put(cm))
    for shot in range(shots):
        ends = [
            laplace(
                lambda k: now_buf[shot, k + 1],
                at,
                lambda k: cz[k + 1],
                lambda k: cx[k + 1],
                lambda k: cp[k + 1],
                lambda k: cm[k + 1],
            )[PAD : PAD + rows]
            for at in (planes - 2, 1)
        ]
        low, top = late[shot, 0], late[shot, planes - 1]
        to_even[shot] = jnp.where(even, top, low)
        to_odd[shot] = jnp.where(even, low, top)
        to_even[shots + shot] = jnp.where(even, ends[0], ends[1])
        to_odd[shots + shot] = jnp.where(even, ends[1], ends[0])


def early_kernel(full_rows, shots, *refs):
    halo = early_halo(*refs[:7])
    edges, *dense = refs[7 : 8 + shots]
    source, wavelet = refs[8 + shots : 10 + shots]
    lap_out, base_out, turn_out, late_own, late_near, last_out, low_out = refs[10 + shots : 17 + shots]
    dens_out, cz, cx, cp, cm, now_buf, buoy_buf = refs[17 + shots :]
    rows, cols, planes = halo.rows, halo.cols, halo.planes
    wide = rows + 2 * PAD
    whole = reader(halo, halo.early_list(), edges)

    for at in range(-2, planes + 2):
        density = whole(DENS, 0, at)
        dens_out[at + 2] = density
        buoy_buf[at + 2] = inverse(density)
        for shot in range(shots):
            now_buf[shot, at + 2] = whole(NOW, shot, at)

    def put(ref):
        def store(at, value):
            ref[at + 2] = value

        return store

    for at in range(-2, planes + 1):
        couple(lambda k: buoy_buf[k + 2], at, put(cz), put(cx), put(cp), put(cm))
    line = lax.broadcasted_iota(jnp.int32, (wide, cols), 0)
    column = lax.broadcasted_iota(jnp.int32, (wide, cols), 1)
    depth_start = lax.axis_index("depth") * planes
    row_start = lax.axis_index("lat") * rows
    for shot in range(shots):
        cell = source[shot]
        source_line = lax.div(cell, cols)
        source_plane = lax.div(source_line, full_rows) - depth_start
        source_row = lax.rem(source_line, full_rows) - row_start + PAD
        spot = (line == source_row) & (column == lax.rem(cell, cols))
        for at in range(-2, planes + 2):
            here = spot & (source_plane == at)
            middle = now_buf[shot, at + 2]
            if -1 <= at < planes + 1:
                lap_out[shot, at + 1] = laplace(
                    lambda k: now_buf[shot, k + 2],
                    at,
                    lambda k: cz[k + 2],
                    lambda k: cx[k + 2],
                    lambda k: cp[k + 2],
                    lambda k: cm[k + 2],
                )
            base_out[shot, at + 2] = (
                2.0 * middle - whole(PREV, shot, at) + jnp.where(here, wavelet[shot, 0], 0.0)
            )
            newest = whole(LAST, shot, at)
            last_out[shot, at + 2] = newest
            if -1 <= at < planes + 1:
                turn_out[shot, at + 1] = jnp.where(here, wavelet[shot, 1], 0.0) - middle
                ahead = 2.0 * newest - dense[shot][2, (at + 1) * wide : (at + 2) * wide]
                if 0 <= at < planes:
                    late_own[shot, at] = ahead - whole(LATE, shot, at)
                else:
                    late_near[shot, int(at >= 0)] = ahead
            if 0 <= at < planes:
                low_out[shot, at] = newest + dense[shot][1, (at + 1) * wide : (at + 2) * wide]


def final_kernel(shape, vels, *refs):
    te, to = refs[:2]
    halo = final_halo(shape, te, to, *refs[2 : 2 + vels])
    edges, dens, ahead, lap_far, late_near, stiff_out = refs[2 + vels :]
    whole = reader(halo, halo.final_list(), edges)
    planes = halo.planes
    for at in range(-2, planes + 2):
        speed = whole(VEL, 0, at) * COURANT
        stiff_out[at + 2] = speed * speed * dens[at + 2]
    for shot in range(halo.shots):
        for side, (near, far) in enumerate(((-1, -2), (planes, planes + 1))):
            lap_far[shot, side] = whole(LAP, shot, far)
            late_near[shot, side] = ahead[shot, side] - whole(LATE, shot, near)


def update_kernel(shots, *refs):
    stiff, lap_mid, lap_far, base, turn, late_own, late_near, last, low = refs[:9]
    cz_ref, cx_ref, cp_ref, cm_ref = refs[9:13]
    dense = refs[13 : 13 + shots]
    out, second, scaled, upper, lap_second = refs[13 + shots :]
    planes = low.shape[1]
    wide, _ = low.shape[2:]

    def lap(shot, at):
        if 1 <= at < planes + 3:
            return lap_mid[shot, at - 1]
        return lap_far[shot, int(at > 0)]

    def late(shot, at):
        if 2 <= at < planes + 2:
            return late_own[shot, at - 2]
        return late_near[shot, int(at > 1)]

    cz = lambda k: cz_ref[k]
    cx = lambda k: cx_ref[k]
    cp = lambda k: cp_ref[k]
    cm = lambda k: cm_ref[k]
    for at in range(planes + 4):
        rigid = stiff[at]
        for shot in range(shots):
            second[shot, at] = base[shot, at] + rigid * lap(shot, at)
            scaled[shot, at] = rigid * last[shot, at]
    for at in range(1, planes + 3):
        rigid = stiff[at]
        for shot in range(shots):
            hits = dense[shot][0, (at - 1) * wide : at * wide]
            lap_now = laplace(lambda k: second[shot, k], at, cz, cx, cp, cm)
            third = 2.0 * second[shot, at] + turn[shot, at - 1] + rigid * lap_now
            adj = late(shot, at) + hits * third
            adj = adj + laplace(lambda k: scaled[shot, k], at, cz, cx, cp, cm)
            upper[shot, at - 1] = adj
            if 2 <= at < planes + 2:
                lap_second[shot, at - 2] = lap_now
    for at in range(1, planes + 3):
        for shot in range(shots):
            scaled[shot, at] = stiff[at] * upper[shot, at - 1]
    for at in range(2, planes + 2):
        total = None
        for shot in range(shots):
            hits = dense[shot][0, (at - 1) * wide : at * wide]
            lower = 2.0 * upper[shot, at - 1] - low[shot, at - 2] + hits * second[shot, at]
            lower = lower + laplace(lambda k: scaled[shot, k], at, cz, cx, cp, cm)
            term = upper[shot, at - 1] * lap_second[shot, at - 2] + lower * lap(shot, at)
            total = term if total is None else total + term
        out[at - 2] = (stiff[at] * total)[PAD : wide - PAD]


def tile_max(value):
    planes, rows, cols = value.shape
    return jnp.max(jnp.abs(value).reshape(planes * rows // 8, 8, cols), axis=0)


def sum_kernel(mine, other, total, edges):
    value = mine[...] + other[...]
    total[...] = value
    first = lax.axis_index("lat") == 0
    planes, rows, _ = value.shape
    for at in range(planes):
        edges[at * PAD : (at + 1) * PAD] = jnp.where(
            first, value[at, rows - PAD :], value[at, :PAD]
        )
    edges[planes * PAD :] = tile_max(value)


def last_sum_kernel(mine, other, total, largest):
    value = mine[...] + other[...]
    total[...] = value
    largest[...] = tile_max(value)


def widen_kernel(total, mine, got, out):
    planes, rows, _ = total.shape
    wide = rows + 2 * PAD
    lat_at = lax.axis_index("lat")
    for at in range(planes):
        part = got[at * PAD : (at + 1) * PAD]
        out[at * wide : (at + 1) * wide] = with_rows(part, total[at], lat_at)
    out[planes * wide :] = jnp.maximum(mine[planes * PAD :], got[planes * PAD :])


def restiff_kernel(stiff, mine, by_even, by_odd, largest, velocity, stiff_out, vel_out):
    planes, rows, own = velocity.shape
    wide = rows + 2 * PAD
    even = lax.axis_index("depth") % 2 == 0
    shot_at = lax.axis_index("shot")
    cols = mine.shape[1]
    scale = jnp.max(jnp.max(largest[...], axis=1, keepdims=True), axis=0, keepdims=True) + EPSILON
    for at in range(-2, planes + 2):
        if 0 <= at < planes:
            value = mine[at * wide : (at + 1) * wide]
        else:
            upper = at >= planes
            step = at - planes if upper else planes + at
            a, b = (by_even, by_odd) if upper else (by_odd, by_even)
            value = jnp.where(
                even, a[step * wide : (step + 1) * wide], b[step * wide : (step + 1) * wide]
            )
        value = value / scale
        stiff_out[at + 2] = stiff[at + 2] * jnp.exp(-2.0 * STEP_SIZE * value)
        if 0 <= at < planes:
            shifted = pltpu.roll(value[PAD : PAD + rows], (cols - shot_at * own) % cols, 1)
            vel_out[at] = velocity[at] * jnp.exp(-STEP_SIZE * shifted[:, :own])


def finish_kernel(total, largest, velocity, vel_out, dir_out):
    planes, _, own = velocity.shape
    shot_at = lax.axis_index("shot")
    cols = total.shape[2]
    scale = jnp.max(jnp.max(largest[...], axis=1, keepdims=True), axis=0, keepdims=True) + EPSILON
    for at in range(planes):
        value = total[at] / scale
        shifted = pltpu.roll(value, (cols - shot_at * own) % cols, 1)[:, :own]
        dir_out[at] = shifted
        vel_out[at] = velocity[at] * jnp.exp(-STEP_SIZE * shifted)


def shards(
    fwd_prev,
    fwd_now,
    adj_late,
    adj_last,
    velocity,
    density,
    wavelet,
    source_cell,
    receiver_cell,
    observed,
):
    shots, planes, rows, cols = fwd_now.shape
    depth_count = lax.axis_size("depth")
    shot_count = lax.axis_size("shot")
    lat_count = lax.axis_size("lat")
    if depth_count < 2 or planes != 2 or wavelet.shape[1] != 2 or lat_count != 2:
        raise ValueError("unsupported split")
    depth_at = lax.axis_index("depth")
    lat_at = lax.axis_index("lat")
    shot_at = lax.axis_index("shot")
    evens = even_pairs(depth_count)
    odds = odd_pairs(depth_count)
    swap = [(0, 1), (1, 0)]
    wide = rows + 2 * PAD

    def shot_terms(block):
        if shot_count == 2:
            return block, lax.ppermute(block, "shot", swap)
        return lax.psum(block, "shot"), jnp.zeros_like(block)

    def depth_max(value):
        if depth_count & (depth_count - 1):
            return lax.pmax(value, "depth")
        if depth_count <= 4:
            parts = [
                send(value, "depth", [(i, i ^ k) for i in range(depth_count)])
                for k in range(1, depth_count)
            ]
            for part in parts:
                value = jnp.maximum(value, part)
            return value
        step = 1
        while step < depth_count:
            pairs = [(i, i ^ step) for i in range(depth_count)]
            value = jnp.maximum(value, send(value, "depth", pairs))
            step *= 2
        return value

    hbm = pl.BlockSpec(memory_space=pltpu.HBM)
    spec = pl.BlockSpec(memory_space=pltpu.VMEM)

    def load(kernel, shapes, args, scratch, count):
        return pl.pallas_call(
            kernel,
            out_shape=tuple(pltpu.VMEM(*shape) for shape in shapes),
            in_specs=[hbm] * len(args),
            out_specs=tuple(spec for _ in shapes),
            scratch_shapes=scratch + [pltpu.SemaphoreType.DMA((count,))],
            compiler_params=pltpu.CompilerParams(vmem_limit_bytes=4 << 20),
        )(*[pltpu.with_memory_space_constraint(a, pltpu.HBM) for a in args])

    own_planes = (shots + 1) * planes
    first, first_edges = load(
        first_kernel,
        [((own_planes + 1, rows, cols), jnp.float32), ((own_planes * PAD, cols), jnp.float32)],
        (fwd_now, density, velocity),
        [pltpu.VMEM(velocity.shape, jnp.float32)],
        shots + 2,
    )
    first_odd = send(first, "depth", odds)
    first_even = send(first, "depth", evens)
    first_edges = send(first_edges, "lat", swap)
    second, late, cells, recorded = load(
        second_kernel,
        [
            ((2 * shots * planes, rows, cols), jnp.float32),
            (adj_late.shape, jnp.float32),
            (receiver_cell.shape, receiver_cell.dtype),
            (observed.shape, jnp.float32),
        ],
        (fwd_prev, adj_last, adj_late, receiver_cell, observed),
        [],
        2 * shots + 3,
    )
    second_odd = send(second, "depth", odds)
    second_even = send(second, "depth", evens)

    even = depth_at % 2 == 0
    lines = jnp.stack(
        [
            jnp.where(even, first_odd[own_planes], first_even[own_planes]),
            first[own_planes],
            jnp.where(even, first_even[own_planes], first_odd[own_planes]),
        ]
    )
    if shot_count == 2:
        other = send(lines, "shot", swap)
        parts = [jnp.where(shot_at == 0, lines, other), jnp.where(shot_at == 0, other, lines)]
    else:
        gathered = lax.all_gather(lines, "shot")
        parts = [gathered[k] for k in range(shot_count)]
    small = (planes + 1, wide, cols)
    to_even, to_odd = on_chip(
        third_kernel,
        [(2 * shots, rows, cols)] * 2,
        (first, first_even, first_odd, first_edges, late),
        scratch=[(shots, planes + 2, wide, cols), (planes + 2, wide, cols)] + [small] * 4,
    )
    third_odd = send(to_odd, "depth", odds)
    third_even = send(to_even, "depth", evens)

    full_rows = rows * lat_count
    depth_start = depth_at * planes
    row_start = lat_at * rows

    def place(cells, margin):
        plane_at = cells // (full_rows * cols) - depth_start + margin
        row_at = cells // cols % full_rows - row_start + PAD
        inside = (
            (plane_at >= 0)
            & (plane_at < planes + 2 * margin)
            & (row_at >= 0)
            & (row_at < wide)
        )
        return jnp.where(inside, plane_at * wide + row_at, -1), cells % cols

    row_id, col_id = place(cells, 1)
    spread_shape = (3, (planes + 2) * wide, cols)

    def receivers(shot):
        (out,) = on_chip(
            spread_kernel,
            [spread_shape],
            (row_id[shot : shot + 1], col_id[shot : shot + 1], recorded[shot]),
            flops=14 * spread_shape[1] * cols * row_id.shape[1],
            limit=24,
        )
        return out

    dense = []
    for shot in range(shots):
        dense.append(receivers(shot))
    dense = tuple(dense)
    early = (first, second, late, first_even, first_odd, second_even, second_odd)
    strips = shots * (4 * planes + 12) + planes + 4
    (edges,) = on_chip(early_edge_kernel, [(strips * PAD, cols)], early)
    edges = send(edges, "lat", swap)
    deep = planes + 4
    model = (wide, cols)
    scalars = pl.BlockSpec(memory_space=pltpu.SMEM)
    shapes = [
        (shots, planes + 2) + model,
        (shots, deep) + model,
        (shots, planes + 2) + model,
        (shots, planes) + model,
        (shots, 2) + model,
        (shots, deep) + model,
        (shots, planes) + model,
        (deep,) + model,
        (planes + 3,) + model,
        (planes + 3,) + model,
        (planes + 3,) + model,
        (planes + 3,) + model,
    ]
    vectors = early + (edges,) + dense
    outs = pl.pallas_call(
        functools.partial(early_kernel, full_rows, shots),
        out_shape=tuple(pltpu.VMEM(shape, jnp.float32) for shape in shapes),
        in_specs=[spec] * len(vectors) + [scalars, scalars],
        out_specs=tuple(spec for _ in shapes),
        scratch_shapes=[
            pltpu.VMEM((shots, deep) + model, jnp.float32),
            pltpu.VMEM((deep,) + model, jnp.float32),
        ],
        compiler_params=pltpu.CompilerParams(vmem_limit_bytes=8 << 20),
        name="early",
    )(*[pltpu.with_memory_space_constraint(a, pltpu.VMEM) for a in vectors], source_cell, wavelet)
    lap, base, turn, late_own, ahead, last, low, dens, cz, cx, cp, cm = outs

    final = (third_even, third_odd) + tuple(parts)
    shape = adj_late.shape
    strips = 4 * shots + planes + 4
    (edges,) = on_chip(functools.partial(final_edge_kernel, shape), [(strips * PAD, cols)], final)
    edges = send(edges, "lat", swap)
    lap_far, late_near, stiff = on_chip(
        functools.partial(final_kernel, shape, len(parts)),
        [(shots, 2) + model, (shots, 2) + model, (deep,) + model],
        final + (edges, dens, ahead),
    )

    def gradient_of(stiff):
        (out,) = on_chip(
            functools.partial(update_kernel, shots),
            [(planes, rows, cols)],
            (stiff, lap, lap_far, base, turn, late_own, late_near, last, low, cz, cx, cp, cm) + dense,
            scratch=[
                (shots, deep) + model,
                (shots, deep) + model,
                (shots, planes + 2) + model,
                (shots, planes) + model,
            ],
        )
        return out

    own_velocity = velocity
    for update_index in range(ITERS):
        mine, other = shot_terms(gradient_of(stiff))
        if update_index + 1 == ITERS:
            summed, largest = on_chip(
                last_sum_kernel, [(planes, rows, cols), (8, cols)], (mine, other)
            )
            largest = jnp.maximum(largest, lax.ppermute(largest, "lat", swap))
            largest = depth_max(largest)
            return tuple(
                on_chip(
                    finish_kernel,
                    [velocity.shape, velocity.shape],
                    (summed, largest, own_velocity),
                    keep=False,
                )
            )
        edge_rows = planes * PAD + 8
        summed, tail = on_chip(sum_kernel, [(planes, rows, cols), (edge_rows, cols)], (mine, other))
        got = send(tail, "lat", swap)
        (widened,) = on_chip(widen_kernel, [(planes * wide + 8, cols)], (summed, tail, got))
        end = planes * wide
        if depth_count == 4:
            by_odd, by_even = [
                send(widened, "depth", [(i, i ^ k) for i in range(4)]) for k in (3, 1)
            ]
            further = send(widened[end:], "depth", [(i, i ^ 2) for i in range(4)])
            largest = jnp.maximum(
                jnp.maximum(widened[end:], further), jnp.maximum(by_odd[end:], by_even[end:])
            )
        else:
            by_even = send(widened, "depth", evens)
            by_odd = send(widened, "depth", odds)
            largest = depth_max(widened[end:])
        stiff, own_velocity = on_chip(
            restiff_kernel,
            [stiff.shape, velocity.shape],
            (stiff, widened, by_even, by_odd, largest, own_velocity),
        )


def solution(mesh):
    fields = P(("grp", "shot"), "depth", "lat", None)
    model = P(("grp", "depth"), "lat", "shot")
    placed = (
        fields,
        fields,
        fields,
        fields,
        model,
        P(("grp", "depth"), "lat", None),
        P(("grp", "shot"), None),
        P(("grp", "shot")),
        P(("grp", "shot"), None),
        P(("grp", "shot"), None, None),
    )

    return jax.shard_map(
        shards,
        mesh=mesh,
        in_specs=placed,
        out_specs=(model, model),
        check_vma=False,
    )
```

```python
import functools

import jax
import jax.numpy as jnp
from jax import lax
from jax.experimental import pallas as pl
from jax.experimental.pallas import tpu as pltpu
from jax.sharding import PartitionSpec as P


ITERS = 2

COURANT = 0.1
STEP_SIZE = 0.1
EPSILON = 1e-06
PAD = 8
NOW, PREV, LAST, LATE, DENS, VEL, LAP = range(7)


def even_pairs(count):
    return [(i, i ^ 1) for i in range(count) if i ^ 1 < count]


def odd_pairs(count):
    ups = [(i, i + 1) for i in range(1, count - 1, 2)]
    return ups + [(b, a) for a, b in ups]


def send(block, axis, pairs):
    if not pairs:
        return jnp.zeros_like(block)
    return lax.ppermute(block, axis, pairs)


def on_chip(kernel, out_shapes, args, scratch=(), flops=0, limit=8, keep=True):
    spec = pl.BlockSpec(memory_space=pltpu.VMEM)
    place = pltpu.VMEM if keep else jax.ShapeDtypeStruct
    outs = tuple(place(shape, jnp.float32) for shape in out_shapes)
    moved = sum(a.size * 4 for a in args)
    return pl.pallas_call(
        kernel,
        out_shape=outs,
        in_specs=[spec] * len(args),
        out_specs=tuple(spec for _ in outs),
        scratch_shapes=[pltpu.VMEM(shape, jnp.float32) for shape in scratch],
        compiler_params=pltpu.CompilerParams(vmem_limit_bytes=limit << 20),
        cost_estimate=pl.CostEstimate(flops=flops, bytes_accessed=moved, transcendentals=0),
    )(*[pltpu.with_memory_space_constraint(a, pltpu.VMEM) for a in args])


def copy_all(copies, sems):
    copies = [
        pltpu.make_async_copy(source, target, sems.at[index])
        for index, (source, target) in enumerate(copies)
    ]
    for copy in copies:
        copy.start()
    for copy in copies:
        copy.wait()


def first_kernel(now, dens, vel, out, edges, vel_buf, sems):
    shots, planes, rows, cols = now.shape
    count = shots * planes
    copies = [
        (now.at[shot], out.at[shot * planes : (shot + 1) * planes]) for shot in range(shots)
    ]
    copies += [(dens, out.at[count : count + planes]), (vel, vel_buf)]
    copy_all(copies, sems)
    lines = [vel_buf[at] for at in range(planes)]
    spare = cols - planes * vel.shape[2]
    if spare:
        lines.append(jnp.zeros((rows, spare), jnp.float32))
    out[count + planes] = jnp.concatenate(lines, axis=1)
    first = lax.axis_index("lat") == 0
    for at in range(count + planes):
        edges[at * PAD : (at + 1) * PAD] = jnp.where(
            first, out[at, rows - PAD :], out[at, :PAD]
        )


def second_kernel(prev, last, late, cells, observed, out, late_out, cells_out, observed_out, sems):
    shots, planes, _, _ = prev.shape
    copies = []
    start = 0
    for field in (prev, last):
        for shot in range(shots):
            copies.append((field.at[shot], out.at[start : start + planes]))
            start += planes
    copies += [(late, late_out), (cells, cells_out), (observed, observed_out)]
    copy_all(copies, sems)


def spread_kernel(row_ref, col_ref, obs_ref, out_ref):
    nrec = row_ref.shape[1]
    rows, cols = out_ref.shape[1:]
    steps = obs_ref.shape[0]
    row_iota = lax.broadcasted_iota(jnp.int32, (rows, nrec), 0)
    col_iota = lax.broadcasted_iota(jnp.int32, (cols, nrec), 0)
    at_row = (row_ref[...] == row_iota).astype(jnp.float32).astype(jnp.bfloat16)
    at_col = col_ref[...] == col_iota
    parts = [(0, at_col.astype(jnp.float32).astype(jnp.bfloat16))]
    for step in range(steps):
        obs = obs_ref[step : step + 1, :]
        high = obs.astype(jnp.bfloat16).astype(jnp.float32)
        rest = obs - high
        middle = rest.astype(jnp.bfloat16).astype(jnp.float32)
        for piece in (high, middle, rest - middle):
            parts.append((1 + step, jnp.where(at_col, piece, 0.0).astype(jnp.bfloat16)))
    sums = [None] * (1 + steps)
    for start in range(0, len(parts), 2):
        pair = parts[start : start + 2]
        both = lax.dot_general(
            at_row,
            jnp.concatenate([p for _, p in pair], axis=0),
            (((1,), (1,)), ((), ())),
            preferred_element_type=jnp.float32,
        )
        for place, (which, _) in enumerate(pair):
            term = both[:, place * cols : (place + 1) * cols]
            sums[which] = term if sums[which] is None else sums[which] + term
    for which, value in enumerate(sums):
        out_ref[which] = value


class Halo:
    def __init__(self, shape, first=None, second=None, late=None, by=(), vel=()):
        self.even = lax.axis_index("depth") % 2 == 0
        self.first, self.second, self.late, self.vel = first, second, late, vel
        self.by = by
        self.shots, self.planes, self.rows, self.cols = shape

    def pick(self, batch, upper, index):
        even, odd = self.by[batch]
        a, b = (even, odd) if upper else (odd, even)
        return jnp.where(self.even, a[index], b[index])

    def plane(self, item):
        which, shot, at = item
        planes, shots = self.planes, self.shots
        inside = 0 <= at < planes
        upper = at >= planes
        step = at if inside else (at - planes if upper else planes + at)
        if which == VEL:
            block, lane = (0, 1, 2)[(at + planes) // planes], (at + planes) % planes
            own = self.cols // len(self.vel)
            column = lax.broadcasted_iota(jnp.int32, (self.rows, self.cols), 1)
            value = None
            planes_of = [part[block] for part in self.vel]
            if len(planes_of) == 2:
                mine, other = planes_of
                here = lax.axis_index("shot") == 0
                planes_of = [jnp.where(here, mine, other), jnp.where(here, other, mine)]
            for index, part in enumerate(planes_of):
                shifted = pltpu.roll(part, (index - lane) * own % self.cols, 1)
                value = shifted if value is None else jnp.where(column >= index * own, shifted, value)
            return value
        if which == LAP:
            return self.pick("third", upper, shots + shot)
        if which == LATE:
            return self.late[shot, at] if inside else self.pick("third", upper, shot)
        if which in (NOW, DENS):
            index = (shot if which == NOW else shots) * planes + step
            return self.first[index] if inside else self.pick("first", upper, index)
        index = ((0 if which == PREV else shots) + shot) * planes + step
        return self.second[index] if inside else self.pick("second", upper, index)

    def early_list(self):
        planes = self.planes
        out = []
        for which, margin in ((NOW, 2), (PREV, 2), (LAST, 2), (LATE, 0)):
            for shot in range(self.shots):
                for at in range(-margin, planes + margin):
                    out.append((which, shot, at))
        return out + [(DENS, 0, at) for at in range(-2, planes + 2)]

    def final_list(self):
        planes = self.planes
        out = []
        for shot in range(self.shots):
            out += [(LATE, shot, -1), (LATE, shot, planes), (LAP, shot, -2), (LAP, shot, planes + 1)]
        return out + [(VEL, 0, at) for at in range(-2, planes + 2)]


def write_edges(halo, items, out):
    first = lax.axis_index("lat") == 0
    rows = halo.rows
    for index, item in enumerate(items):
        value = halo.plane(item)
        out[index * PAD : (index + 1) * PAD] = jnp.where(first, value[rows - PAD :], value[:PAD])


def reader(halo, items, edges):
    lat_at = lax.axis_index("lat")
    where_is = {item: index for index, item in enumerate(items)}

    def whole(which, shot, at):
        item = (which, shot, at)
        index = where_is[item]
        return with_rows(edges[index * PAD : (index + 1) * PAD], halo.plane(item), lat_at)

    return whole


def early_halo(first, second, late, fe, fo, se, so):
    return Halo(late.shape, first, second, late, {"first": (fe, fo), "second": (se, so)})


def final_halo(shape, te, to, *vel):
    return Halo(shape, by={"third": (te, to)}, vel=vel)


def early_edge_kernel(*refs):
    halo = early_halo(*refs[:7])
    write_edges(halo, halo.early_list(), refs[7])


def final_edge_kernel(shape, *refs):
    halo = final_halo(shape, *refs[:-1])
    write_edges(halo, halo.final_list(), refs[-1])


def near_cols(value):
    lane = lax.broadcasted_iota(jnp.int32, value.shape, 1)
    cols = value.shape[1]
    above = jnp.where(lane == cols - 1, 0.0, pltpu.roll(value, cols - 1, 1))
    below = jnp.where(lane == 0, 0.0, pltpu.roll(value, 1, 1))
    return above, below


def laplace(field, at, cz, cx, cp, cm):
    middle = field(at)
    rows = middle.shape[0]
    flux = cx(at) * (pltpu.roll(middle, rows - 1, 0) - middle)
    total = flux - pltpu.roll(flux, 1, 0)
    above, below = near_cols(middle)
    total = total + (cp(at) * (above - middle) + cm(at) * (below - middle))
    return total + (cz(at) * (field(at + 1) - middle) + cz(at - 1) * (field(at - 1) - middle))


def inverse(density):
    inside = density > 0.0
    return jnp.where(inside, 1.0 / jnp.where(inside, density, 1.0), 0.0)


def with_rows(part, value, lat_at):
    low = jnp.where(lat_at == 1, part, 0.0)
    high = jnp.where(lat_at == 0, part, 0.0)
    return jnp.concatenate([low, value, high], axis=0)


def couple(buoy, at, cz, cx, cp, cm):
    plane = buoy(at)
    cz(at, 0.5 * (plane + buoy(at + 1)))
    cx(at, 0.5 * (plane + pltpu.roll(plane, plane.shape[0] - 1, 0)))
    above, below = near_cols(plane)
    cp(at, 0.5 * (plane + above))
    cm(at, 0.5 * (plane + below))


def third_kernel(first, by_even, by_odd, edges, late, to_even, to_odd, lines, now_buf, buoy_buf, cz, cx, cp, cm):
    even = lax.axis_index("depth") % 2 == 0
    lat_at = lax.axis_index("lat")
    shots, planes, rows, cols = late.shape
    place = (shots + 1) * planes
    lines[0] = jnp.where(even, by_odd[place], by_even[place])
    lines[1] = first[place]
    lines[2] = jnp.where(even, by_even[place], by_odd[place])

    def whole(index, at):
        if 0 <= at < planes:
            place = index * planes + at
            return with_rows(edges[place * PAD : (place + 1) * PAD], first[place], lat_at)
        upper = at >= planes
        a, b = (by_even, by_odd) if upper else (by_odd, by_even)
        place = index * planes + (0 if upper else planes - 1)
        empty = jnp.zeros((PAD, cols), jnp.float32)
        return jnp.concatenate([empty, jnp.where(even, a[place], b[place]), empty], axis=0)

    for at in range(-1, planes + 1):
        buoy_buf[at + 1] = inverse(whole(shots, at))
        for shot in range(shots):
            now_buf[shot, at + 1] = whole(shot, at)

    def put(ref):
        def store(at, value):
            ref[at + 1] = value

        return store

    for at in range(-1, planes):
        couple(lambda k: buoy_buf[k + 1], at, put(cz), put(cx), put(cp), put(cm))
    for shot in range(shots):
        ends = [
            laplace(
                lambda k: now_buf[shot, k + 1],
                at,
                lambda k: cz[k + 1],
                lambda k: cx[k + 1],
                lambda k: cp[k + 1],
                lambda k: cm[k + 1],
            )[PAD : PAD + rows]
            for at in (planes - 2, 1)
        ]
        low, top = late[shot, 0], late[shot, planes - 1]
        to_even[shot] = jnp.where(even, top, low)
        to_odd[shot] = jnp.where(even, low, top)
        to_even[shots + shot] = jnp.where(even, ends[0], ends[1])
        to_odd[shots + shot] = jnp.where(even, ends[1], ends[0])


def early_kernel(full_rows, shots, *refs):
    halo = early_halo(*refs[:7])
    edges, *dense = refs[7 : 8 + shots]
    source, wavelet = refs[8 + shots : 10 + shots]
    lap_out, base_out, turn_out, late_own, late_near, last_out, low_out = refs[10 + shots : 17 + shots]
    dens_out, cz, cx, cp, cm, now_buf, buoy_buf = refs[17 + shots :]
    rows, cols, planes = halo.rows, halo.cols, halo.planes
    wide = rows + 2 * PAD
    whole = reader(halo, halo.early_list(), edges)

    for at in range(-2, planes + 2):
        density = whole(DENS, 0, at)
        dens_out[at + 2] = density
        buoy_buf[at + 2] = inverse(density)
        for shot in range(shots):
            now_buf[shot, at + 2] = whole(NOW, shot, at)

    def put(ref):
        def store(at, value):
            ref[at + 2] = value

        return store

    for at in range(-2, planes + 1):
        couple(lambda k: buoy_buf[k + 2], at, put(cz), put(cx), put(cp), put(cm))
    line = lax.broadcasted_iota(jnp.int32, (wide, cols), 0)
    column = lax.broadcasted_iota(jnp.int32, (wide, cols), 1)
    depth_start = lax.axis_index("depth") * planes
    row_start = lax.axis_index("lat") * rows
    for shot in range(shots):
        cell = source[shot]
        source_line = lax.div(cell, cols)
        source_plane = lax.div(source_line, full_rows) - depth_start
        source_row = lax.rem(source_line, full_rows) - row_start + PAD
        spot = (line == source_row) & (column == lax.rem(cell, cols))
        for at in range(-2, planes + 2):
            here = spot & (source_plane == at)
            middle = now_buf[shot, at + 2]
            if -1 <= at < planes + 1:
                lap_out[shot, at + 1] = laplace(
                    lambda k: now_buf[shot, k + 2],
                    at,
                    lambda k: cz[k + 2],
                    lambda k: cx[k + 2],
                    lambda k: cp[k + 2],
                    lambda k: cm[k + 2],
                )
            base_out[shot, at + 2] = (
                2.0 * middle - whole(PREV, shot, at) + jnp.where(here, wavelet[shot, 0], 0.0)
            )
            newest = whole(LAST, shot, at)
            last_out[shot, at + 2] = newest
            if -1 <= at < planes + 1:
                turn_out[shot, at + 1] = jnp.where(here, wavelet[shot, 1], 0.0) - middle
                ahead = 2.0 * newest - dense[shot][2, (at + 1) * wide : (at + 2) * wide]
                if 0 <= at < planes:
                    late_own[shot, at] = ahead - whole(LATE, shot, at)
                else:
                    late_near[shot, int(at >= 0)] = ahead
            if 0 <= at < planes:
                low_out[shot, at] = newest + dense[shot][1, (at + 1) * wide : (at + 2) * wide]


def final_kernel(shape, vels, *refs):
    te, to = refs[:2]
    halo = final_halo(shape, te, to, *refs[2 : 2 + vels])
    edges, dens, ahead, lap_far, late_near, stiff_out = refs[2 + vels :]
    whole = reader(halo, halo.final_list(), edges)
    planes = halo.planes
    for at in range(-2, planes + 2):
        speed = whole(VEL, 0, at) * COURANT
        stiff_out[at + 2] = speed * speed * dens[at + 2]
    for shot in range(halo.shots):
        for side, (near, far) in enumerate(((-1, -2), (planes, planes + 1))):
            lap_far[shot, side] = whole(LAP, shot, far)
            late_near[shot, side] = ahead[shot, side] - whole(LATE, shot, near)


def update_kernel(shots, *refs):
    stiff, lap_mid, lap_far, base, turn, late_own, late_near, last, low = refs[:9]
    cz_ref, cx_ref, cp_ref, cm_ref = refs[9:13]
    dense = refs[13 : 13 + shots]
    out, second, scaled, upper, lap_second = refs[13 + shots :]
    planes = low.shape[1]
    wide, _ = low.shape[2:]

    def lap(shot, at):
        if 1 <= at < planes + 3:
            return lap_mid[shot, at - 1]
        return lap_far[shot, int(at > 0)]

    def late(shot, at):
        if 2 <= at < planes + 2:
            return late_own[shot, at - 2]
        return late_near[shot, int(at > 1)]

    cz = lambda k: cz_ref[k]
    cx = lambda k: cx_ref[k]
    cp = lambda k: cp_ref[k]
    cm = lambda k: cm_ref[k]
    for at in range(planes + 4):
        rigid = stiff[at]
        for shot in range(shots):
            second[shot, at] = base[shot, at] + rigid * lap(shot, at)
            scaled[shot, at] = rigid * last[shot, at]
    for at in range(1, planes + 3):
        rigid = stiff[at]
        for shot in range(shots):
            hits = dense[shot][0, (at - 1) * wide : at * wide]
            lap_now = laplace(lambda k: second[shot, k], at, cz, cx, cp, cm)
            third = 2.0 * second[shot, at] + turn[shot, at - 1] + rigid * lap_now
            adj = late(shot, at) + hits * third
            adj = adj + laplace(lambda k: scaled[shot, k], at, cz, cx, cp, cm)
            upper[shot, at - 1] = adj
            if 2 <= at < planes + 2:
                lap_second[shot, at - 2] = lap_now
    for at in range(1, planes + 3):
        for shot in range(shots):
            scaled[shot, at] = stiff[at] * upper[shot, at - 1]
    for at in range(2, planes + 2):
        total = None
        for shot in range(shots):
            hits = dense[shot][0, (at - 1) * wide : at * wide]
            lower = 2.0 * upper[shot, at - 1] - low[shot, at - 2] + hits * second[shot, at]
            lower = lower + laplace(lambda k: scaled[shot, k], at, cz, cx, cp, cm)
            term = upper[shot, at - 1] * lap_second[shot, at - 2] + lower * lap(shot, at)
            total = term if total is None else total + term
        out[at - 2] = (stiff[at] * total)[PAD : wide - PAD]


def tile_max(value):
    planes, rows, cols = value.shape
    return jnp.max(jnp.abs(value).reshape(planes * rows // 8, 8, cols), axis=0)


def sum_kernel(mine, other, total, edges):
    value = mine[...] + other[...]
    total[...] = value
    first = lax.axis_index("lat") == 0
    planes, rows, _ = value.shape
    for at in range(planes):
        edges[at * PAD : (at + 1) * PAD] = jnp.where(
            first, value[at, rows - PAD :], value[at, :PAD]
        )
    edges[planes * PAD :] = tile_max(value)


def last_sum_kernel(mine, other, total, largest):
    value = mine[...] + other[...]
    total[...] = value
    largest[...] = tile_max(value)


def widen_kernel(total, mine, got, out):
    planes, rows, _ = total.shape
    wide = rows + 2 * PAD
    lat_at = lax.axis_index("lat")
    for at in range(planes):
        part = got[at * PAD : (at + 1) * PAD]
        out[at * wide : (at + 1) * wide] = with_rows(part, total[at], lat_at)
    out[planes * wide :] = jnp.maximum(mine[planes * PAD :], got[planes * PAD :])


def restiff_kernel(stiff, mine, by_even, by_odd, largest, velocity, stiff_out, vel_out):
    planes, rows, own = velocity.shape
    wide = rows + 2 * PAD
    even = lax.axis_index("depth") % 2 == 0
    shot_at = lax.axis_index("shot")
    cols = mine.shape[1]
    scale = jnp.max(jnp.max(largest[...], axis=1, keepdims=True), axis=0, keepdims=True) + EPSILON
    for at in range(-2, planes + 2):
        if 0 <= at < planes:
            value = mine[at * wide : (at + 1) * wide]
        else:
            upper = at >= planes
            step = at - planes if upper else planes + at
            a, b = (by_even, by_odd) if upper else (by_odd, by_even)
            value = jnp.where(
                even, a[step * wide : (step + 1) * wide], b[step * wide : (step + 1) * wide]
            )
        value = value / scale
        stiff_out[at + 2] = stiff[at + 2] * jnp.exp(-2.0 * STEP_SIZE * value)
        if 0 <= at < planes:
            shifted = pltpu.roll(value[PAD : PAD + rows], (cols - shot_at * own) % cols, 1)
            vel_out[at] = velocity[at] * jnp.exp(-STEP_SIZE * shifted[:, :own])


def finish_kernel(total, largest, velocity, vel_out, dir_out):
    planes, _, own = velocity.shape
    shot_at = lax.axis_index("shot")
    cols = total.shape[2]
    scale = jnp.max(jnp.max(largest[...], axis=1, keepdims=True), axis=0, keepdims=True) + EPSILON
    for at in range(planes):
        value = total[at] / scale
        shifted = pltpu.roll(value, (cols - shot_at * own) % cols, 1)[:, :own]
        dir_out[at] = shifted
        vel_out[at] = velocity[at] * jnp.exp(-STEP_SIZE * shifted)


def shards(
    fwd_prev,
    fwd_now,
    adj_late,
    adj_last,
    velocity,
    density,
    wavelet,
    source_cell,
    receiver_cell,
    observed,
):
    shots, planes, rows, cols = fwd_now.shape
    depth_count = lax.axis_size("depth")
    shot_count = lax.axis_size("shot")
    lat_count = lax.axis_size("lat")
    if depth_count < 2 or planes != 2 or wavelet.shape[1] != 2 or lat_count != 2:
        raise ValueError("unsupported split")
    depth_at = lax.axis_index("depth")
    lat_at = lax.axis_index("lat")
    evens = even_pairs(depth_count)
    odds = odd_pairs(depth_count)
    swap = [(0, 1), (1, 0)]
    wide = rows + 2 * PAD

    def shot_terms(block):
        if shot_count == 2:
            return block, lax.ppermute(block, "shot", swap)
        return lax.psum(block, "shot"), jnp.zeros_like(block)

    def depth_max(value):
        if depth_count & (depth_count - 1):
            return lax.pmax(value, "depth")
        if depth_count <= 4:
            parts = [
                send(value, "depth", [(i, i ^ k) for i in range(depth_count)])
                for k in range(1, depth_count)
            ]
            for part in parts:
                value = jnp.maximum(value, part)
            return value
        step = 1
        while step < depth_count:
            pairs = [(i, i ^ step) for i in range(depth_count)]
            value = jnp.maximum(value, send(value, "depth", pairs))
            step *= 2
        return value

    hbm = pl.BlockSpec(memory_space=pltpu.HBM)
    spec = pl.BlockSpec(memory_space=pltpu.VMEM)

    def load(kernel, shapes, args, scratch, count):
        return pl.pallas_call(
            kernel,
            out_shape=tuple(pltpu.VMEM(*shape) for shape in shapes),
            in_specs=[hbm] * len(args),
            out_specs=tuple(spec for _ in shapes),
            scratch_shapes=scratch + [pltpu.SemaphoreType.DMA((count,))],
            compiler_params=pltpu.CompilerParams(vmem_limit_bytes=4 << 20),
        )(*[pltpu.with_memory_space_constraint(a, pltpu.HBM) for a in args])

    own_planes = (shots + 1) * planes
    first, first_edges = load(
        first_kernel,
        [((own_planes + 1, rows, cols), jnp.float32), ((own_planes * PAD, cols), jnp.float32)],
        (fwd_now, density, velocity),
        [pltpu.VMEM(velocity.shape, jnp.float32)],
        shots + 2,
    )
    first_odd = send(first, "depth", odds)
    first_even = send(first, "depth", evens)
    first_edges = send(first_edges, "lat", swap)
    second, late, cells, recorded = load(
        second_kernel,
        [
            ((2 * shots * planes, rows, cols), jnp.float32),
            (adj_late.shape, jnp.float32),
            (receiver_cell.shape, receiver_cell.dtype),
            (observed.shape, jnp.float32),
        ],
        (fwd_prev, adj_last, adj_late, receiver_cell, observed),
        [],
        2 * shots + 3,
    )
    second_odd = send(second, "depth", odds)
    second_even = send(second, "depth", evens)

    small = (planes + 1, wide, cols)
    to_even, to_odd, lines = on_chip(
        third_kernel,
        [(2 * shots, rows, cols)] * 2 + [(3, rows, cols)],
        (first, first_even, first_odd, first_edges, late),
        scratch=[(shots, planes + 2, wide, cols), (planes + 2, wide, cols)] + [small] * 4,
    )
    third_odd = send(to_odd, "depth", odds)
    third_even = send(to_even, "depth", evens)

    if shot_count == 2:
        parts = (lines, send(lines, "shot", swap))
    else:
        gathered = lax.all_gather(lines, "shot")
        parts = tuple(gathered[k] for k in range(shot_count))

    full_rows = rows * lat_count
    depth_start = depth_at * planes
    row_start = lat_at * rows

    def place(cells, margin):
        plane_at = cells // (full_rows * cols) - depth_start + margin
        row_at = cells // cols % full_rows - row_start + PAD
        inside = (
            (plane_at >= 0)
            & (plane_at < planes + 2 * margin)
            & (row_at >= 0)
            & (row_at < wide)
        )
        return jnp.where(inside, plane_at * wide + row_at, -1), cells % cols

    row_id, col_id = place(cells, 1)
    spread_shape = (3, (planes + 2) * wide, cols)

    def receivers(shot):
        (out,) = on_chip(
            spread_kernel,
            [spread_shape],
            (row_id[shot : shot + 1], col_id[shot : shot + 1], recorded[shot]),
            flops=14 * spread_shape[1] * cols * row_id.shape[1],
            limit=24,
        )
        return out

    dense = []
    for shot in range(shots):
        dense.append(receivers(shot))
    dense = tuple(dense)
    early = (first, second, late, first_even, first_odd, second_even, second_odd)
    strips = shots * (4 * planes + 12) + planes + 4
    (edges,) = on_chip(early_edge_kernel, [(strips * PAD, cols)], early)
    edges = send(edges, "lat", swap)
    deep = planes + 4
    model = (wide, cols)
    scalars = pl.BlockSpec(memory_space=pltpu.SMEM)
    shapes = [
        (shots, planes + 2) + model,
        (shots, deep) + model,
        (shots, planes + 2) + model,
        (shots, planes) + model,
        (shots, 2) + model,
        (shots, deep) + model,
        (shots, planes) + model,
        (deep,) + model,
        (planes + 3,) + model,
        (planes + 3,) + model,
        (planes + 3,) + model,
        (planes + 3,) + model,
    ]
    vectors = early + (edges,) + dense
    outs = pl.pallas_call(
        functools.partial(early_kernel, full_rows, shots),
        out_shape=tuple(pltpu.VMEM(shape, jnp.float32) for shape in shapes),
        in_specs=[spec] * len(vectors) + [scalars, scalars],
        out_specs=tuple(spec for _ in shapes),
        scratch_shapes=[
            pltpu.VMEM((shots, deep) + model, jnp.float32),
            pltpu.VMEM((deep,) + model, jnp.float32),
        ],
        compiler_params=pltpu.CompilerParams(vmem_limit_bytes=8 << 20),
        name="early",
    )(*[pltpu.with_memory_space_constraint(a, pltpu.VMEM) for a in vectors], source_cell, wavelet)
    lap, base, turn, late_own, ahead, last, low, dens, cz, cx, cp, cm = outs

    final = (third_even, third_odd) + parts
    shape = adj_late.shape
    strips = 4 * shots + planes + 4
    (edges,) = on_chip(functools.partial(final_edge_kernel, shape), [(strips * PAD, cols)], final)
    edges = send(edges, "lat", swap)
    lap_far, late_near, stiff = on_chip(
        functools.partial(final_kernel, shape, len(parts)),
        [(shots, 2) + model, (shots, 2) + model, (deep,) + model],
        final + (edges, dens, ahead),
    )

    def gradient_of(stiff):
        (out,) = on_chip(
            functools.partial(update_kernel, shots),
            [(planes, rows, cols)],
            (stiff, lap, lap_far, base, turn, late_own, late_near, last, low, cz, cx, cp, cm) + dense,
            scratch=[
                (shots, deep) + model,
                (shots, deep) + model,
                (shots, planes + 2) + model,
                (shots, planes) + model,
            ],
        )
        return out

    own_velocity = velocity
    for update_index in range(ITERS):
        mine, other = shot_terms(gradient_of(stiff))
        if update_index + 1 == ITERS:
            summed, largest = on_chip(
                last_sum_kernel, [(planes, rows, cols), (8, cols)], (mine, other)
            )
            largest = jnp.maximum(largest, lax.ppermute(largest, "lat", swap))
            largest = depth_max(largest)
            return tuple(
                on_chip(
                    finish_kernel,
                    [velocity.shape, velocity.shape],
                    (summed, largest, own_velocity),
                    keep=False,
                )
            )
        edge_rows = planes * PAD + 8
        summed, tail = on_chip(sum_kernel, [(planes, rows, cols), (edge_rows, cols)], (mine, other))
        got = send(tail, "lat", swap)
        (widened,) = on_chip(widen_kernel, [(planes * wide + 8, cols)], (summed, tail, got))
        end = planes * wide
        if depth_count == 4:
            by_odd, by_even = [
                send(widened, "depth", [(i, i ^ k) for i in range(4)]) for k in (3, 1)
            ]
            further = send(widened[end:], "depth", [(i, i ^ 2) for i in range(4)])
            largest = jnp.maximum(
                jnp.maximum(widened[end:], further), jnp.maximum(by_odd[end:], by_even[end:])
            )
        else:
            by_even = send(widened, "depth", evens)
            by_odd = send(widened, "depth", odds)
            largest = depth_max(widened[end:])
        stiff, own_velocity = on_chip(
            restiff_kernel,
            [stiff.shape, velocity.shape],
            (stiff, widened, by_even, by_odd, largest, own_velocity),
        )


def solution(mesh):
    fields = P(("grp", "shot"), "depth", "lat", None)
    model = P(("grp", "depth"), "lat", "shot")
    placed = (
        fields,
        fields,
        fields,
        fields,
        model,
        P(("grp", "depth"), "lat", None),
        P(("grp", "shot"), None),
        P(("grp", "shot")),
        P(("grp", "shot"), None),
        P(("grp", "shot"), None, None),
    )

    return jax.shard_map(
        shards,
        mesh=mesh,
        in_specs=placed,
        out_specs=(model, model),
        check_vma=False,
    )
```

```python
import functools

import jax
import jax.numpy as jnp
from jax import lax
from jax.experimental import pallas as pl
from jax.experimental.pallas import tpu as pltpu
from jax.sharding import PartitionSpec as P


ITERS = 2

COURANT = 0.1
STEP_SIZE = 0.1
EPSILON = 1e-06
PAD = 8
NOW, PREV, LAST, LATE, DENS, VEL, LAP = range(7)


def even_pairs(count):
    return [(i, i ^ 1) for i in range(count) if i ^ 1 < count]


def odd_pairs(count):
    ups = [(i, i + 1) for i in range(1, count - 1, 2)]
    return ups + [(b, a) for a, b in ups]


def send(block, axis, pairs):
    if not pairs:
        return jnp.zeros_like(block)
    return lax.ppermute(block, axis, pairs)


def on_chip(kernel, out_shapes, args, scratch=(), flops=0, limit=8, keep=True):
    spec = pl.BlockSpec(memory_space=pltpu.VMEM)
    place = pltpu.VMEM if keep else jax.ShapeDtypeStruct
    outs = tuple(place(shape, jnp.float32) for shape in out_shapes)
    moved = sum(a.size * 4 for a in args)
    return pl.pallas_call(
        kernel,
        out_shape=outs,
        in_specs=[spec] * len(args),
        out_specs=tuple(spec for _ in outs),
        scratch_shapes=[pltpu.VMEM(shape, jnp.float32) for shape in scratch],
        compiler_params=pltpu.CompilerParams(vmem_limit_bytes=limit << 20),
        cost_estimate=pl.CostEstimate(flops=flops, bytes_accessed=moved, transcendentals=0),
    )(*[pltpu.with_memory_space_constraint(a, pltpu.VMEM) for a in args])


def copy_all(copies, sems):
    copies = [
        pltpu.make_async_copy(source, target, sems.at[index])
        for index, (source, target) in enumerate(copies)
    ]
    for copy in copies:
        copy.start()
    for copy in copies:
        copy.wait()


def first_kernel(now, dens, vel, out, edges, vel_buf, sems):
    shots, planes, rows, cols = now.shape
    count = shots * planes
    copies = [
        (now.at[shot], out.at[shot * planes : (shot + 1) * planes]) for shot in range(shots)
    ]
    copies += [(dens, out.at[count : count + planes]), (vel, vel_buf)]
    copy_all(copies, sems)
    lines = [vel_buf[at] for at in range(planes)]
    spare = cols - planes * vel.shape[2]
    if spare:
        lines.append(jnp.zeros((rows, spare), jnp.float32))
    out[count + planes] = jnp.concatenate(lines, axis=1)
    first = lax.axis_index("lat") == 0
    for at in range(count + planes):
        edges[at * PAD : (at + 1) * PAD] = jnp.where(
            first, out[at, rows - PAD :], out[at, :PAD]
        )


def second_kernel(prev, last, late, cells, observed, out, late_out, cells_out, observed_out, sems):
    shots, planes, _, _ = prev.shape
    copies = []
    start = 0
    for field in (prev, last):
        for shot in range(shots):
            copies.append((field.at[shot], out.at[start : start + planes]))
            start += planes
    copies += [(late, late_out), (cells, cells_out), (observed, observed_out)]
    copy_all(copies, sems)


def spread_kernel(row_ref, col_ref, obs_ref, out_ref):
    nrec = row_ref.shape[1]
    rows, cols = out_ref.shape[1:]
    steps = obs_ref.shape[0]
    row_iota = lax.broadcasted_iota(jnp.int32, (rows, nrec), 0)
    col_iota = lax.broadcasted_iota(jnp.int32, (cols, nrec), 0)
    at_row = (row_ref[...] == row_iota).astype(jnp.float32).astype(jnp.bfloat16)
    at_col = col_ref[...] == col_iota
    parts = [(0, at_col.astype(jnp.float32).astype(jnp.bfloat16))]
    for step in range(steps):
        obs = obs_ref[step : step + 1, :]
        high = obs.astype(jnp.bfloat16).astype(jnp.float32)
        rest = obs - high
        middle = rest.astype(jnp.bfloat16).astype(jnp.float32)
        for piece in (high, middle, rest - middle):
            parts.append((1 + step, jnp.where(at_col, piece, 0.0).astype(jnp.bfloat16)))
    sums = [None] * (1 + steps)
    for start in range(0, len(parts), 2):
        pair = parts[start : start + 2]
        both = lax.dot_general(
            at_row,
            jnp.concatenate([p for _, p in pair], axis=0),
            (((1,), (1,)), ((), ())),
            preferred_element_type=jnp.float32,
        )
        for place, (which, _) in enumerate(pair):
            term = both[:, place * cols : (place + 1) * cols]
            sums[which] = term if sums[which] is None else sums[which] + term
    for which, value in enumerate(sums):
        out_ref[which] = value


class Halo:
    def __init__(self, shape, first=None, second=None, late=None, by=(), vel=()):
        self.even = lax.axis_index("depth") % 2 == 0
        self.first, self.second, self.late, self.vel = first, second, late, vel
        self.by = by
        self.shots, self.planes, self.rows, self.cols = shape

    def pick(self, batch, upper, index):
        even, odd = self.by[batch]
        a, b = (even, odd) if upper else (odd, even)
        return jnp.where(self.even, a[index], b[index])

    def plane(self, item):
        which, shot, at = item
        planes, shots = self.planes, self.shots
        inside = 0 <= at < planes
        upper = at >= planes
        step = at if inside else (at - planes if upper else planes + at)
        if which == VEL:
            block, lane = (0, 1, 2)[(at + planes) // planes], (at + planes) % planes
            own = self.cols // len(self.vel)
            column = lax.broadcasted_iota(jnp.int32, self.vel[0].shape[1:], 1)
            value = None
            planes_of = [part[block] for part in self.vel]
            if len(planes_of) == 2:
                mine, other = planes_of
                here = lax.axis_index("shot") == 0
                planes_of = [jnp.where(here, mine, other), jnp.where(here, other, mine)]
            for index, part in enumerate(planes_of):
                shifted = pltpu.roll(part, (index - lane) * own % self.cols, 1)
                value = shifted if value is None else jnp.where(column >= index * own, shifted, value)
            return value
        if which == LAP:
            return self.pick("third", upper, shots + shot)
        if which == LATE:
            return self.late[shot, at] if inside else self.pick("third", upper, shot)
        if which in (NOW, DENS):
            index = (shot if which == NOW else shots) * planes + step
            return self.first[index] if inside else self.pick("first", upper, index)
        index = ((0 if which == PREV else shots) + shot) * planes + step
        return self.second[index] if inside else self.pick("second", upper, index)

    def early_list(self):
        planes = self.planes
        out = []
        for which, margin in ((NOW, 2), (PREV, 2), (LAST, 2), (LATE, 0)):
            for shot in range(self.shots):
                for at in range(-margin, planes + margin):
                    out.append((which, shot, at))
        return out + [(DENS, 0, at) for at in range(-2, planes + 2)]


def write_edges(halo, items, out):
    first = lax.axis_index("lat") == 0
    rows = halo.rows
    for index, item in enumerate(items):
        value = halo.plane(item)
        out[index * PAD : (index + 1) * PAD] = jnp.where(first, value[rows - PAD :], value[:PAD])


def reader(halo, items, edges):
    lat_at = lax.axis_index("lat")
    where_is = {item: index for index, item in enumerate(items)}

    def whole(which, shot, at):
        item = (which, shot, at)
        index = where_is[item]
        return with_rows(edges[index * PAD : (index + 1) * PAD], halo.plane(item), lat_at)

    return whole


def early_halo(first, second, late, fe, fo, se, so):
    return Halo(late.shape, first, second, late, {"first": (fe, fo), "second": (se, so)})


def final_halo(shape, te, to, *vel):
    return Halo(shape, by={"third": (te, to)}, vel=vel)


def early_edge_kernel(*refs):
    halo = early_halo(*refs[:7])
    write_edges(halo, halo.early_list(), refs[7])


def stretch_kernel(lines, got, out):
    lat_at = lax.axis_index("lat")
    for block in range(3):
        out[block] = with_rows(got[block * PAD : (block + 1) * PAD], lines[block], lat_at)


def near_cols(value):
    lane = lax.broadcasted_iota(jnp.int32, value.shape, 1)
    cols = value.shape[1]
    above = jnp.where(lane == cols - 1, 0.0, pltpu.roll(value, cols - 1, 1))
    below = jnp.where(lane == 0, 0.0, pltpu.roll(value, 1, 1))
    return above, below


def laplace(field, at, cz, cx, cp, cm):
    middle = field(at)
    rows = middle.shape[0]
    flux = cx(at) * (pltpu.roll(middle, rows - 1, 0) - middle)
    total = flux - pltpu.roll(flux, 1, 0)
    above, below = near_cols(middle)
    total = total + (cp(at) * (above - middle) + cm(at) * (below - middle))
    return total + (cz(at) * (field(at + 1) - middle) + cz(at - 1) * (field(at - 1) - middle))


def inverse(density):
    inside = density > 0.0
    return jnp.where(inside, 1.0 / jnp.where(inside, density, 1.0), 0.0)


def with_rows(part, value, lat_at):
    low = jnp.where(lat_at == 1, part, 0.0)
    high = jnp.where(lat_at == 0, part, 0.0)
    return jnp.concatenate([low, value, high], axis=0)


def couple(buoy, at, cz, cx, cp, cm):
    plane = buoy(at)
    cz(at, 0.5 * (plane + buoy(at + 1)))
    cx(at, 0.5 * (plane + pltpu.roll(plane, plane.shape[0] - 1, 0)))
    above, below = near_cols(plane)
    cp(at, 0.5 * (plane + above))
    cm(at, 0.5 * (plane + below))


def third_kernel(
    first, by_even, by_odd, edges, late, to_even, to_odd, lines, line_edges, now_buf, buoy_buf, cz, cx, cp, cm
):
    even = lax.axis_index("depth") % 2 == 0
    lat_at = lax.axis_index("lat")
    shots, planes, rows, cols = late.shape
    place = (shots + 1) * planes
    lines[0] = jnp.where(even, by_odd[place], by_even[place])
    lines[1] = first[place]
    lines[2] = jnp.where(even, by_even[place], by_odd[place])
    for block in range(3):
        line_edges[block * PAD : (block + 1) * PAD] = jnp.where(
            lat_at == 0, lines[block, rows - PAD :], lines[block, :PAD]
        )

    def whole(index, at):
        if 0 <= at < planes:
            place = index * planes + at
            return with_rows(edges[place * PAD : (place + 1) * PAD], first[place], lat_at)
        upper = at >= planes
        a, b = (by_even, by_odd) if upper else (by_odd, by_even)
        place = index * planes + (0 if upper else planes - 1)
        empty = jnp.zeros((PAD, cols), jnp.float32)
        return jnp.concatenate([empty, jnp.where(even, a[place], b[place]), empty], axis=0)

    for at in range(-1, planes + 1):
        buoy_buf[at + 1] = inverse(whole(shots, at))
        for shot in range(shots):
            now_buf[shot, at + 1] = whole(shot, at)

    def put(ref):
        def store(at, value):
            ref[at + 1] = value

        return store

    for at in range(-1, planes):
        couple(lambda k: buoy_buf[k + 1], at, put(cz), put(cx), put(cp), put(cm))
    for shot in range(shots):
        ends = [
            laplace(
                lambda k: now_buf[shot, k + 1],
                at,
                lambda k: cz[k + 1],
                lambda k: cx[k + 1],
                lambda k: cp[k + 1],
                lambda k: cm[k + 1],
            )[PAD : PAD + rows]
            for at in (planes - 2, 1)
        ]
        low, top = late[shot, 0], late[shot, planes - 1]
        to_even[shot] = jnp.where(even, top, low)
        to_odd[shot] = jnp.where(even, low, top)
        to_even[shots + shot] = jnp.where(even, ends[0], ends[1])
        to_odd[shots + shot] = jnp.where(even, ends[1], ends[0])


def early_kernel(full_rows, shots, *refs):
    halo = early_halo(*refs[:7])
    edges, *dense = refs[7 : 8 + shots]
    source, wavelet = refs[8 + shots : 10 + shots]
    lap_out, base_out, turn_out, late_own, late_near, last_out, low_out = refs[10 + shots : 17 + shots]
    dens_out, cz, cx, cp, cm, now_buf, buoy_buf = refs[17 + shots :]
    rows, cols, planes = halo.rows, halo.cols, halo.planes
    wide = rows + 2 * PAD
    whole = reader(halo, halo.early_list(), edges)

    for at in range(-2, planes + 2):
        density = whole(DENS, 0, at)
        dens_out[at + 2] = density
        buoy_buf[at + 2] = inverse(density)
        for shot in range(shots):
            now_buf[shot, at + 2] = whole(NOW, shot, at)

    def put(ref):
        def store(at, value):
            ref[at + 2] = value

        return store

    for at in range(-2, planes + 1):
        couple(lambda k: buoy_buf[k + 2], at, put(cz), put(cx), put(cp), put(cm))
    line = lax.broadcasted_iota(jnp.int32, (wide, cols), 0)
    column = lax.broadcasted_iota(jnp.int32, (wide, cols), 1)
    depth_start = lax.axis_index("depth") * planes
    row_start = lax.axis_index("lat") * rows
    for shot in range(shots):
        cell = source[shot]
        source_line = lax.div(cell, cols)
        source_plane = lax.div(source_line, full_rows) - depth_start
        source_row = lax.rem(source_line, full_rows) - row_start + PAD
        spot = (line == source_row) & (column == lax.rem(cell, cols))
        for at in range(-2, planes + 2):
            here = spot & (source_plane == at)
            middle = now_buf[shot, at + 2]
            if -1 <= at < planes + 1:
                lap_out[shot, at + 1] = laplace(
                    lambda k: now_buf[shot, k + 2],
                    at,
                    lambda k: cz[k + 2],
                    lambda k: cx[k + 2],
                    lambda k: cp[k + 2],
                    lambda k: cm[k + 2],
                )
            base_out[shot, at + 2] = (
                2.0 * middle - whole(PREV, shot, at) + jnp.where(here, wavelet[shot, 0], 0.0)
            )
            newest = whole(LAST, shot, at)
            last_out[shot, at + 2] = newest
            if -1 <= at < planes + 1:
                turn_out[shot, at + 1] = jnp.where(here, wavelet[shot, 1], 0.0) - middle
                ahead = 2.0 * newest - dense[shot][2, (at + 1) * wide : (at + 2) * wide]
                if 0 <= at < planes:
                    late_own[shot, at] = ahead - whole(LATE, shot, at)
                else:
                    late_near[shot, int(at >= 0)] = ahead
            if 0 <= at < planes:
                low_out[shot, at] = newest + dense[shot][1, (at + 1) * wide : (at + 2) * wide]


def final_kernel(shape, vels, *refs):
    halo = final_halo(shape, *refs[: 2 + vels])
    dens, ahead, lap_far, late_near, stiff_out = refs[2 + vels :]
    planes = halo.planes
    empty = jnp.zeros((PAD, halo.cols), jnp.float32)

    def whole(which, shot, at):
        return jnp.concatenate([empty, halo.plane((which, shot, at)), empty], axis=0)

    for at in range(-2, planes + 2):
        speed = halo.plane((VEL, 0, at)) * COURANT
        stiff_out[at + 2] = speed * speed * dens[at + 2]
    for shot in range(halo.shots):
        for side, (near, far) in enumerate(((-1, -2), (planes, planes + 1))):
            lap_far[shot, side] = whole(LAP, shot, far)
            late_near[shot, side] = ahead[shot, side] - whole(LATE, shot, near)


def update_kernel(shots, *refs):
    stiff, lap_mid, lap_far, base, turn, late_own, late_near, last, low = refs[:9]
    cz_ref, cx_ref, cp_ref, cm_ref = refs[9:13]
    dense = refs[13 : 13 + shots]
    out, second, scaled, upper, lap_second = refs[13 + shots :]
    planes = low.shape[1]
    wide, _ = low.shape[2:]

    def lap(shot, at):
        if 1 <= at < planes + 3:
            return lap_mid[shot, at - 1]
        return lap_far[shot, int(at > 0)]

    def late(shot, at):
        if 2 <= at < planes + 2:
            return late_own[shot, at - 2]
        return late_near[shot, int(at > 1)]

    cz = lambda k: cz_ref[k]
    cx = lambda k: cx_ref[k]
    cp = lambda k: cp_ref[k]
    cm = lambda k: cm_ref[k]
    for at in range(planes + 4):
        rigid = stiff[at]
        for shot in range(shots):
            second[shot, at] = base[shot, at] + rigid * lap(shot, at)
            scaled[shot, at] = rigid * last[shot, at]
    for at in range(1, planes + 3):
        rigid = stiff[at]
        for shot in range(shots):
            hits = dense[shot][0, (at - 1) * wide : at * wide]
            lap_now = laplace(lambda k: second[shot, k], at, cz, cx, cp, cm)
            third = 2.0 * second[shot, at] + turn[shot, at - 1] + rigid * lap_now
            adj = late(shot, at) + hits * third
            adj = adj + laplace(lambda k: scaled[shot, k], at, cz, cx, cp, cm)
            upper[shot, at - 1] = adj
            if 2 <= at < planes + 2:
                lap_second[shot, at - 2] = lap_now
    for at in range(1, planes + 3):
        for shot in range(shots):
            scaled[shot, at] = stiff[at] * upper[shot, at - 1]
    for at in range(2, planes + 2):
        total = None
        for shot in range(shots):
            hits = dense[shot][0, (at - 1) * wide : at * wide]
            lower = 2.0 * upper[shot, at - 1] - low[shot, at - 2] + hits * second[shot, at]
            lower = lower + laplace(lambda k: scaled[shot, k], at, cz, cx, cp, cm)
            term = upper[shot, at - 1] * lap_second[shot, at - 2] + lower * lap(shot, at)
            total = term if total is None else total + term
        out[at - 2] = (stiff[at] * total)[PAD : wide - PAD]


def tile_max(value):
    planes, rows, cols = value.shape
    return jnp.max(jnp.abs(value).reshape(planes * rows // 8, 8, cols), axis=0)


def sum_kernel(mine, other, total, edges):
    value = mine[...] + other[...]
    total[...] = value
    first = lax.axis_index("lat") == 0
    planes, rows, _ = value.shape
    for at in range(planes):
        edges[at * PAD : (at + 1) * PAD] = jnp.where(
            first, value[at, rows - PAD :], value[at, :PAD]
        )
    edges[planes * PAD :] = tile_max(value)


def last_sum_kernel(mine, other, total, largest):
    value = mine[...] + other[...]
    total[...] = value
    largest[...] = tile_max(value)


def widen_kernel(total, mine, got, out, to_even, to_odd):
    planes, rows, _ = total.shape
    wide = rows + 2 * PAD
    lat_at = lax.axis_index("lat")
    even = lax.axis_index("depth") % 2 == 0
    for at in range(planes):
        part = got[at * PAD : (at + 1) * PAD]
        out[at * wide : (at + 1) * wide] = with_rows(part, total[at], lat_at)
    low, top = out[:wide], out[(planes - 1) * wide :]
    to_even[:wide] = jnp.where(even, top, low)
    to_odd[:wide] = jnp.where(even, low, top)
    low, top = total[0], total[planes - 1]
    to_even[wide : wide + rows] = jnp.where(even, low, top)
    to_odd[wide : wide + rows] = jnp.where(even, top, low)
    largest = jnp.maximum(mine[planes * PAD :], got[planes * PAD :])
    to_even[wide + rows :] = largest
    to_odd[wide + rows :] = largest


def restiff_kernel(stiff, mine, by_even, by_odd, largest, velocity, stiff_out, vel_out):
    planes, rows, own = velocity.shape
    wide = rows + 2 * PAD
    even = lax.axis_index("depth") % 2 == 0
    shot_at = lax.axis_index("shot")
    cols = mine.shape[1]
    scale = jnp.max(jnp.max(largest[...], axis=1, keepdims=True), axis=0, keepdims=True) + EPSILON
    for at in range(-2, planes + 2):
        if 0 <= at < planes:
            value = mine[at * wide : (at + 1) * wide]
        else:
            a, b = (by_even, by_odd) if at >= planes else (by_odd, by_even)
            if at in (-1, planes):
                value = jnp.where(even, a[:wide], b[:wide])
            else:
                value = jnp.where(even, a[wide : wide + rows], b[wide : wide + rows])
                empty = jnp.zeros((PAD, cols), jnp.float32)
                value = jnp.concatenate([empty, value, empty], axis=0)
        value = value / scale
        stiff_out[at + 2] = stiff[at + 2] * jnp.exp(-2.0 * STEP_SIZE * value)
        if 0 <= at < planes:
            shifted = pltpu.roll(value[PAD : PAD + rows], (cols - shot_at * own) % cols, 1)
            vel_out[at] = velocity[at] * jnp.exp(-STEP_SIZE * shifted[:, :own])


def finish_kernel(total, largest, velocity, vel_out, dir_out):
    planes, _, own = velocity.shape
    shot_at = lax.axis_index("shot")
    cols = total.shape[2]
    scale = jnp.max(jnp.max(largest[...], axis=1, keepdims=True), axis=0, keepdims=True) + EPSILON
    for at in range(planes):
        value = total[at] / scale
        shifted = pltpu.roll(value, (cols - shot_at * own) % cols, 1)[:, :own]
        dir_out[at] = shifted
        vel_out[at] = velocity[at] * jnp.exp(-STEP_SIZE * shifted)


def shards(
    fwd_prev,
    fwd_now,
    adj_late,
    adj_last,
    velocity,
    density,
    wavelet,
    source_cell,
    receiver_cell,
    observed,
):
    shots, planes, rows, cols = fwd_now.shape
    depth_count = lax.axis_size("depth")
    shot_count = lax.axis_size("shot")
    lat_count = lax.axis_size("lat")
    if depth_count < 2 or planes != 2 or wavelet.shape[1] != 2 or lat_count != 2:
        raise ValueError("unsupported split")
    depth_at = lax.axis_index("depth")
    lat_at = lax.axis_index("lat")
    evens = even_pairs(depth_count)
    odds = odd_pairs(depth_count)
    swap = [(0, 1), (1, 0)]
    wide = rows + 2 * PAD

    def shot_terms(block):
        if shot_count == 2:
            return block, lax.ppermute(block, "shot", swap)
        return lax.psum(block, "shot"), jnp.zeros_like(block)

    def depth_max(value):
        if depth_count & (depth_count - 1):
            return lax.pmax(value, "depth")
        if depth_count <= 4:
            parts = [
                send(value, "depth", [(i, i ^ k) for i in range(depth_count)])
                for k in range(1, depth_count)
            ]
            for part in parts:
                value = jnp.maximum(value, part)
            return value
        step = 1
        while step < depth_count:
            pairs = [(i, i ^ step) for i in range(depth_count)]
            value = jnp.maximum(value, send(value, "depth", pairs))
            step *= 2
        return value

    hbm = pl.BlockSpec(memory_space=pltpu.HBM)
    spec = pl.BlockSpec(memory_space=pltpu.VMEM)

    def load(kernel, shapes, args, scratch, count):
        return pl.pallas_call(
            kernel,
            out_shape=tuple(pltpu.VMEM(*shape) for shape in shapes),
            in_specs=[hbm] * len(args),
            out_specs=tuple(spec for _ in shapes),
            scratch_shapes=scratch + [pltpu.SemaphoreType.DMA((count,))],
            compiler_params=pltpu.CompilerParams(vmem_limit_bytes=4 << 20),
        )(*[pltpu.with_memory_space_constraint(a, pltpu.HBM) for a in args])

    own_planes = (shots + 1) * planes
    first, first_edges = load(
        first_kernel,
        [((own_planes + 1, rows, cols), jnp.float32), ((own_planes * PAD, cols), jnp.float32)],
        (fwd_now, density, velocity),
        [pltpu.VMEM(velocity.shape, jnp.float32)],
        shots + 2,
    )
    first_odd = send(first, "depth", odds)
    first_even = send(first, "depth", evens)
    first_edges = send(first_edges, "lat", swap)
    second, late, cells, recorded = load(
        second_kernel,
        [
            ((2 * shots * planes, rows, cols), jnp.float32),
            (adj_late.shape, jnp.float32),
            (receiver_cell.shape, receiver_cell.dtype),
            (observed.shape, jnp.float32),
        ],
        (fwd_prev, adj_last, adj_late, receiver_cell, observed),
        [],
        2 * shots + 3,
    )
    second_odd = send(second, "depth", odds)
    second_even = send(second, "depth", evens)

    small = (planes + 1, wide, cols)
    to_even, to_odd, lines, line_edges = on_chip(
        third_kernel,
        [(2 * shots, rows, cols)] * 2 + [(3, rows, cols), (3 * PAD, cols)],
        (first, first_even, first_odd, first_edges, late),
        scratch=[(shots, planes + 2, wide, cols), (planes + 2, wide, cols)] + [small] * 4,
    )
    line_edges = send(line_edges, "lat", swap)
    third_odd = send(to_odd, "depth", odds)
    third_even = send(to_even, "depth", evens)

    (lines,) = on_chip(stretch_kernel, [(3, wide, cols)], (lines, line_edges))
    if shot_count == 2:
        parts = (lines, send(lines, "shot", swap))
    else:
        gathered = lax.all_gather(lines, "shot")
        parts = tuple(gathered[k] for k in range(shot_count))

    full_rows = rows * lat_count
    depth_start = depth_at * planes
    row_start = lat_at * rows

    def place(cells, margin):
        plane_at = cells // (full_rows * cols) - depth_start + margin
        row_at = cells // cols % full_rows - row_start + PAD
        inside = (
            (plane_at >= 0)
            & (plane_at < planes + 2 * margin)
            & (row_at >= 0)
            & (row_at < wide)
        )
        return jnp.where(inside, plane_at * wide + row_at, -1), cells % cols

    row_id, col_id = place(cells, 1)
    spread_shape = (3, (planes + 2) * wide, cols)

    def receivers(shot):
        (out,) = on_chip(
            spread_kernel,
            [spread_shape],
            (row_id[shot : shot + 1], col_id[shot : shot + 1], recorded[shot]),
            flops=14 * spread_shape[1] * cols * row_id.shape[1],
            limit=24,
        )
        return out

    dense = []
    for shot in range(shots):
        dense.append(receivers(shot))
    dense = tuple(dense)
    early = (first, second, late, first_even, first_odd, second_even, second_odd)
    strips = shots * (4 * planes + 12) + planes + 4
    (edges,) = on_chip(early_edge_kernel, [(strips * PAD, cols)], early)
    edges = send(edges, "lat", swap)
    deep = planes + 4
    model = (wide, cols)
    scalars = pl.BlockSpec(memory_space=pltpu.SMEM)
    shapes = [
        (shots, planes + 2) + model,
        (shots, deep) + model,
        (shots, planes + 2) + model,
        (shots, planes) + model,
        (shots, 2) + model,
        (shots, deep) + model,
        (shots, planes) + model,
        (deep,) + model,
        (planes + 3,) + model,
        (planes + 3,) + model,
        (planes + 3,) + model,
        (planes + 3,) + model,
    ]
    vectors = early + (edges,) + dense
    outs = pl.pallas_call(
        functools.partial(early_kernel, full_rows, shots),
        out_shape=tuple(pltpu.VMEM(shape, jnp.float32) for shape in shapes),
        in_specs=[spec] * len(vectors) + [scalars, scalars],
        out_specs=tuple(spec for _ in shapes),
        scratch_shapes=[
            pltpu.VMEM((shots, deep) + model, jnp.float32),
            pltpu.VMEM((deep,) + model, jnp.float32),
        ],
        compiler_params=pltpu.CompilerParams(vmem_limit_bytes=8 << 20),
        name="early",
    )(*[pltpu.with_memory_space_constraint(a, pltpu.VMEM) for a in vectors], source_cell, wavelet)
    lap, base, turn, late_own, ahead, last, low, dens, cz, cx, cp, cm = outs

    final = (third_even, third_odd) + parts
    shape = adj_late.shape
    lap_far, late_near, stiff = on_chip(
        functools.partial(final_kernel, shape, len(parts)),
        [(shots, 2) + model, (shots, 2) + model, (deep,) + model],
        final + (dens, ahead),
    )

    def gradient_of(stiff):
        (out,) = on_chip(
            functools.partial(update_kernel, shots),
            [(planes, rows, cols)],
            (stiff, lap, lap_far, base, turn, late_own, late_near, last, low, cz, cx, cp, cm) + dense,
            scratch=[
                (shots, deep) + model,
                (shots, deep) + model,
                (shots, planes + 2) + model,
                (shots, planes) + model,
            ],
        )
        return out

    own_velocity = velocity
    for update_index in range(ITERS):
        mine, other = shot_terms(gradient_of(stiff))
        if update_index + 1 == ITERS:
            summed, largest = on_chip(
                last_sum_kernel, [(planes, rows, cols), (8, cols)], (mine, other)
            )
            largest = jnp.maximum(largest, lax.ppermute(largest, "lat", swap))
            largest = depth_max(largest)
            return tuple(
                on_chip(
                    finish_kernel,
                    [velocity.shape, velocity.shape],
                    (summed, largest, own_velocity),
                    keep=False,
                )
            )
        edge_rows = planes * PAD + 8
        summed, tail = on_chip(sum_kernel, [(planes, rows, cols), (edge_rows, cols)], (mine, other))
        got = send(tail, "lat", swap)
        widened, to_even, to_odd = on_chip(
            widen_kernel,
            [(planes * wide, cols)] + [(wide + rows + 8, cols)] * 2,
            (summed, tail, got),
        )
        end = wide + rows
        if depth_count == 4:
            by_odd = send(to_odd, "depth", [(i, i ^ 3) for i in range(4)])
            by_even = send(to_even, "depth", evens)
            further = send(to_even[end:], "depth", [(i, i ^ 2) for i in range(4)])
            largest = jnp.maximum(
                jnp.maximum(to_even[end:], further), jnp.maximum(by_odd[end:], by_even[end:])
            )
        else:
            by_even = send(to_even, "depth", evens)
            by_odd = send(to_odd, "depth", odds)
            largest = depth_max(to_even[end:])
        stiff, own_velocity = on_chip(
            restiff_kernel,
            [stiff.shape, velocity.shape],
            (stiff, widened, by_even, by_odd, largest, own_velocity),
        )


def solution(mesh):
    fields = P(("grp", "shot"), "depth", "lat", None)
    model = P(("grp", "depth"), "lat", "shot")
    placed = (
        fields,
        fields,
        fields,
        fields,
        model,
        P(("grp", "depth"), "lat", None),
        P(("grp", "shot"), None),
        P(("grp", "shot")),
        P(("grp", "shot"), None),
        P(("grp", "shot"), None, None),
    )

    return jax.shard_map(
        shards,
        mesh=mesh,
        in_specs=placed,
        out_specs=(model, model),
        check_vma=False,
    )
```

```python
import functools

import jax
import jax.numpy as jnp
from jax import lax
from jax.experimental import pallas as pl
from jax.experimental.pallas import tpu as pltpu
from jax.sharding import PartitionSpec as P


ITERS = 2

COURANT = 0.1
STEP_SIZE = 0.1
EPSILON = 1e-06
PAD = 8
NOW, PREV, LAST, LATE, DENS, VEL, LAP = range(7)


def even_pairs(count):
    return [(i, i ^ 1) for i in range(count) if i ^ 1 < count]


def odd_pairs(count):
    ups = [(i, i + 1) for i in range(1, count - 1, 2)]
    return ups + [(b, a) for a, b in ups]


def send(block, axis, pairs):
    if not pairs:
        return jnp.zeros_like(block)
    return lax.ppermute(block, axis, pairs)


def on_chip(kernel, out_shapes, args, scratch=(), flops=0, limit=8, keep=True):
    spec = pl.BlockSpec(memory_space=pltpu.VMEM)
    place = pltpu.VMEM if keep else jax.ShapeDtypeStruct
    outs = tuple(place(shape, jnp.float32) for shape in out_shapes)
    moved = sum(a.size * 4 for a in args)
    return pl.pallas_call(
        kernel,
        out_shape=outs,
        in_specs=[spec] * len(args),
        out_specs=tuple(spec for _ in outs),
        scratch_shapes=[pltpu.VMEM(shape, jnp.float32) for shape in scratch],
        compiler_params=pltpu.CompilerParams(vmem_limit_bytes=limit << 20),
        cost_estimate=pl.CostEstimate(flops=flops, bytes_accessed=moved, transcendentals=0),
    )(*[pltpu.with_memory_space_constraint(a, pltpu.VMEM) for a in args])


def copy_all(copies, sems):
    copies = [
        pltpu.make_async_copy(source, target, sems.at[index])
        for index, (source, target) in enumerate(copies)
    ]
    for copy in copies:
        copy.start()
    for copy in copies:
        copy.wait()


def first_kernel(now, dens, vel, out, edges, vel_buf, sems):
    shots, planes, rows, cols = now.shape
    count = shots * planes
    copies = [
        (now.at[shot], out.at[shot * planes : (shot + 1) * planes]) for shot in range(shots)
    ]
    copies += [(dens, out.at[count : count + planes]), (vel, vel_buf)]
    copy_all(copies, sems)
    lines = [vel_buf[at] for at in range(planes)]
    spare = cols - planes * vel.shape[2]
    if spare:
        lines.append(jnp.zeros((rows, spare), jnp.float32))
    out[count + planes] = jnp.concatenate(lines, axis=1)
    first = lax.axis_index("lat") == 0
    for at in range(count + planes):
        edges[at * PAD : (at + 1) * PAD] = jnp.where(
            first, out[at, rows - PAD :], out[at, :PAD]
        )


def second_kernel(prev, last, late, cells, observed, out, late_out, cells_out, observed_out, sems):
    shots, planes, _, _ = prev.shape
    copies = []
    start = 0
    for field in (prev, last):
        for shot in range(shots):
            copies.append((field.at[shot], out.at[start : start + planes]))
            start += planes
    copies += [(late, late_out), (cells, cells_out), (observed, observed_out)]
    copy_all(copies, sems)


def spread_kernel(row_ref, col_ref, obs_ref, out_ref):
    nrec = row_ref.shape[1]
    rows, cols = out_ref.shape[1:]
    steps = obs_ref.shape[0]
    row_iota = lax.broadcasted_iota(jnp.int32, (rows, nrec), 0)
    col_iota = lax.broadcasted_iota(jnp.int32, (cols, nrec), 0)
    at_row = (row_ref[...] == row_iota).astype(jnp.float32).astype(jnp.bfloat16)
    at_col = col_ref[...] == col_iota
    parts = [(0, at_col.astype(jnp.float32).astype(jnp.bfloat16))]
    for step in range(steps):
        obs = obs_ref[step : step + 1, :]
        high = obs.astype(jnp.bfloat16).astype(jnp.float32)
        rest = obs - high
        middle = rest.astype(jnp.bfloat16).astype(jnp.float32)
        for piece in (high, middle, rest - middle):
            parts.append((1 + step, jnp.where(at_col, piece, 0.0).astype(jnp.bfloat16)))
    sums = [None] * (1 + steps)
    for start in range(0, len(parts), 2):
        pair = parts[start : start + 2]
        both = lax.dot_general(
            at_row,
            jnp.concatenate([p for _, p in pair], axis=0),
            (((1,), (1,)), ((), ())),
            preferred_element_type=jnp.float32,
        )
        for place, (which, _) in enumerate(pair):
            term = both[:, place * cols : (place + 1) * cols]
            sums[which] = term if sums[which] is None else sums[which] + term
    for which, value in enumerate(sums):
        out_ref[which] = value


class Halo:
    def __init__(self, shape, first=None, second=None, late=None, by=(), vel=()):
        self.even = lax.axis_index("depth") % 2 == 0
        self.first, self.second, self.late, self.vel = first, second, late, vel
        self.by = by
        self.shots, self.planes, self.rows, self.cols = shape

    def pick(self, batch, upper, index):
        even, odd = self.by[batch]
        a, b = (even, odd) if upper else (odd, even)
        return jnp.where(self.even, a[index], b[index])

    def plane(self, item):
        which, shot, at = item
        planes, shots = self.planes, self.shots
        inside = 0 <= at < planes
        upper = at >= planes
        step = at if inside else (at - planes if upper else planes + at)
        if which == VEL:
            block, lane = (0, 1, 2)[(at + planes) // planes], (at + planes) % planes
            own = self.cols // len(self.vel)
            column = lax.broadcasted_iota(jnp.int32, self.vel[0].shape[1:], 1)
            value = None
            planes_of = [part[block] for part in self.vel]
            if len(planes_of) == 2:
                mine, other = planes_of
                here = lax.axis_index("shot") == 0
                planes_of = [jnp.where(here, mine, other), jnp.where(here, other, mine)]
            for index, part in enumerate(planes_of):
                shifted = pltpu.roll(part, (index - lane) * own % self.cols, 1)
                value = shifted if value is None else jnp.where(column >= index * own, shifted, value)
            return value
        if which == LAP:
            return self.pick("third", upper, shots + shot)
        if which == LATE:
            return self.late[shot, at] if inside else self.pick("third", upper, shot)
        if which in (NOW, DENS):
            index = (shot if which == NOW else shots) * planes + step
            return self.first[index] if inside else self.pick("first", upper, index)
        index = ((0 if which == PREV else shots) + shot) * planes + step
        return self.second[index] if inside else self.pick("second", upper, index)

    def early_list(self):
        planes = self.planes
        out = []
        for which, margin in ((NOW, 2), (PREV, 2), (LAST, 2), (LATE, 0)):
            for shot in range(self.shots):
                for at in range(-margin, planes + margin):
                    out.append((which, shot, at))
        return out + [(DENS, 0, at) for at in range(-2, planes + 2)]


def write_edges(halo, items, out):
    first = lax.axis_index("lat") == 0
    rows = halo.rows
    for index, item in enumerate(items):
        value = halo.plane(item)
        out[index * PAD : (index + 1) * PAD] = jnp.where(first, value[rows - PAD :], value[:PAD])


def reader(halo, items, edges):
    lat_at = lax.axis_index("lat")
    where_is = {item: index for index, item in enumerate(items)}

    def whole(which, shot, at):
        item = (which, shot, at)
        index = where_is[item]
        return with_rows(edges[index * PAD : (index + 1) * PAD], halo.plane(item), lat_at)

    return whole


def early_halo(first, second, late, fe, fo, se, so):
    return Halo(late.shape, first, second, late, {"first": (fe, fo), "second": (se, so)})


def final_halo(shape, te, to, *vel):
    return Halo(shape, by={"third": (te, to)}, vel=vel)


def early_edge_kernel(*refs):
    halo = early_halo(*refs[:7])
    write_edges(halo, halo.early_list(), refs[7])


def stretch_kernel(lines, got, out):
    lat_at = lax.axis_index("lat")
    for block in range(3):
        out[block] = with_rows(got[block * PAD : (block + 1) * PAD], lines[block], lat_at)


def near_cols(value):
    lane = lax.broadcasted_iota(jnp.int32, value.shape, 1)
    cols = value.shape[1]
    above = jnp.where(lane == cols - 1, 0.0, pltpu.roll(value, cols - 1, 1))
    below = jnp.where(lane == 0, 0.0, pltpu.roll(value, 1, 1))
    return above, below


def laplace(field, at, cz, cx, cp, cm):
    middle = field(at)
    rows = middle.shape[0]
    flux = cx(at) * (pltpu.roll(middle, rows - 1, 0) - middle)
    total = flux - pltpu.roll(flux, 1, 0)
    above, below = near_cols(middle)
    total = total + (cp(at) * (above - middle) + cm(at) * (below - middle))
    return total + (cz(at) * (field(at + 1) - middle) + cz(at - 1) * (field(at - 1) - middle))


def inverse(density):
    inside = density > 0.0
    return jnp.where(inside, 1.0 / jnp.where(inside, density, 1.0), 0.0)


def with_rows(part, value, lat_at):
    low = jnp.where(lat_at == 1, part, 0.0)
    high = jnp.where(lat_at == 0, part, 0.0)
    return jnp.concatenate([low, value, high], axis=0)


def couple(buoy, at, cz, cx, cp, cm):
    plane = buoy(at)
    cz(at, 0.5 * (plane + buoy(at + 1)))
    cx(at, 0.5 * (plane + pltpu.roll(plane, plane.shape[0] - 1, 0)))
    above, below = near_cols(plane)
    cp(at, 0.5 * (plane + above))
    cm(at, 0.5 * (plane + below))


def third_kernel(
    first, by_even, by_odd, edges, late, to_even, to_odd, lines, line_edges, now_buf, buoy_buf, cz, cx, cp, cm
):
    even = lax.axis_index("depth") % 2 == 0
    lat_at = lax.axis_index("lat")
    shots, planes, rows, cols = late.shape
    place = (shots + 1) * planes
    lines[0] = jnp.where(even, by_odd[place], by_even[place])
    lines[1] = first[place]
    lines[2] = jnp.where(even, by_even[place], by_odd[place])
    for block in range(3):
        line_edges[block * PAD : (block + 1) * PAD] = jnp.where(
            lat_at == 0, lines[block, rows - PAD :], lines[block, :PAD]
        )

    def whole(index, at):
        if 0 <= at < planes:
            place = index * planes + at
            return with_rows(edges[place * PAD : (place + 1) * PAD], first[place], lat_at)
        upper = at >= planes
        a, b = (by_even, by_odd) if upper else (by_odd, by_even)
        place = index * planes + (0 if upper else planes - 1)
        empty = jnp.zeros((PAD, cols), jnp.float32)
        return jnp.concatenate([empty, jnp.where(even, a[place], b[place]), empty], axis=0)

    for at in range(-1, planes + 1):
        buoy_buf[at + 1] = inverse(whole(shots, at))
        for shot in range(shots):
            now_buf[shot, at + 1] = whole(shot, at)

    def put(ref):
        def store(at, value):
            ref[at + 1] = value

        return store

    for at in range(-1, planes):
        couple(lambda k: buoy_buf[k + 1], at, put(cz), put(cx), put(cp), put(cm))
    for shot in range(shots):
        ends = [
            laplace(
                lambda k: now_buf[shot, k + 1],
                at,
                lambda k: cz[k + 1],
                lambda k: cx[k + 1],
                lambda k: cp[k + 1],
                lambda k: cm[k + 1],
            )[PAD : PAD + rows]
            for at in (planes - 2, 1)
        ]
        low, top = late[shot, 0], late[shot, planes - 1]
        to_even[shot] = jnp.where(even, top, low)
        to_odd[shot] = jnp.where(even, low, top)
        to_even[shots + shot] = jnp.where(even, ends[0], ends[1])
        to_odd[shots + shot] = jnp.where(even, ends[1], ends[0])


def early_kernel(full_rows, shots, *refs):
    halo = early_halo(*refs[:7])
    edges, *dense = refs[7 : 8 + shots]
    source, wavelet = refs[8 + shots : 10 + shots]
    lap_out, base_out, turn_out, late_own, late_near, last_out, low_out = refs[10 + shots : 17 + shots]
    dens_out, cz, cx, cp, cm, now_buf, buoy_buf = refs[17 + shots :]
    rows, cols, planes = halo.rows, halo.cols, halo.planes
    wide = rows + 2 * PAD
    whole = reader(halo, halo.early_list(), edges)

    for at in range(-2, planes + 2):
        density = whole(DENS, 0, at)
        dens_out[at + 2] = density
        buoy_buf[at + 2] = inverse(density)
        for shot in range(shots):
            now_buf[shot, at + 2] = whole(NOW, shot, at)

    def put(ref):
        def store(at, value):
            ref[at + 2] = value

        return store

    for at in range(-2, planes + 1):
        couple(lambda k: buoy_buf[k + 2], at, put(cz), put(cx), put(cp), put(cm))
    line = lax.broadcasted_iota(jnp.int32, (wide, cols), 0)
    column = lax.broadcasted_iota(jnp.int32, (wide, cols), 1)
    depth_start = lax.axis_index("depth") * planes
    row_start = lax.axis_index("lat") * rows
    for shot in range(shots):
        cell = source[shot]
        source_line = lax.div(cell, cols)
        source_plane = lax.div(source_line, full_rows) - depth_start
        source_row = lax.rem(source_line, full_rows) - row_start + PAD
        spot = (line == source_row) & (column == lax.rem(cell, cols))
        for at in range(-2, planes + 2):
            here = spot & (source_plane == at)
            middle = now_buf[shot, at + 2]
            if -1 <= at < planes + 1:
                lap_out[shot, at + 1] = laplace(
                    lambda k: now_buf[shot, k + 2],
                    at,
                    lambda k: cz[k + 2],
                    lambda k: cx[k + 2],
                    lambda k: cp[k + 2],
                    lambda k: cm[k + 2],
                )
            base_out[shot, at + 2] = (
                2.0 * middle - whole(PREV, shot, at) + jnp.where(here, wavelet[shot, 0], 0.0)
            )
            newest = whole(LAST, shot, at)
            last_out[shot, at + 2] = newest
            if -1 <= at < planes + 1:
                turn_out[shot, at + 1] = jnp.where(here, wavelet[shot, 1], 0.0) - middle
                ahead = 2.0 * newest - dense[shot][2, (at + 1) * wide : (at + 2) * wide]
                if 0 <= at < planes:
                    late_own[shot, at] = ahead - whole(LATE, shot, at)
                else:
                    late_near[shot, int(at >= 0)] = ahead
            if 0 <= at < planes:
                low_out[shot, at] = newest + dense[shot][1, (at + 1) * wide : (at + 2) * wide]


def final_kernel(shape, vels, *refs):
    halo = final_halo(shape, *refs[: 2 + vels])
    dens, ahead, lap_far, late_near, stiff_out = refs[2 + vels :]
    planes = halo.planes
    empty = jnp.zeros((PAD, halo.cols), jnp.float32)

    def whole(which, shot, at):
        return jnp.concatenate([empty, halo.plane((which, shot, at)), empty], axis=0)

    for at in range(-2, planes + 2):
        speed = halo.plane((VEL, 0, at)) * COURANT
        stiff_out[at + 2] = speed * speed * dens[at + 2]
    for shot in range(halo.shots):
        for side, (near, far) in enumerate(((-1, -2), (planes, planes + 1))):
            lap_far[shot, side] = whole(LAP, shot, far)
            late_near[shot, side] = ahead[shot, side] - whole(LATE, shot, near)


def update_kernel(shots, *refs):
    stiff, lap_mid, lap_far, base, turn, late_own, late_near, last, low = refs[:9]
    cz_ref, cx_ref, cp_ref, cm_ref = refs[9:13]
    dense = refs[13 : 13 + shots]
    out, second, scaled, upper, lap_second, scaled_near = refs[13 + shots :]
    planes = low.shape[1]
    wide, _ = low.shape[2:]

    def lap(shot, at):
        if 1 <= at < planes + 3:
            return lap_mid[shot, at - 1]
        return lap_far[shot, int(at > 0)]

    def late(shot, at):
        if 2 <= at < planes + 2:
            return late_own[shot, at - 2]
        return late_near[shot, int(at > 1)]

    cz = lambda k: cz_ref[k]
    cx = lambda k: cx_ref[k]
    cp = lambda k: cp_ref[k]
    cm = lambda k: cm_ref[k]
    for at in range(planes + 4):
        rigid = stiff[at]
        for shot in range(shots):
            second[shot, at] = base[shot, at] + rigid * lap(shot, at)
            scaled[shot, at] = rigid * last[shot, at]
    for at in range(1, planes + 3):
        rigid = stiff[at]
        for shot in range(shots):
            hits = dense[shot][0, (at - 1) * wide : at * wide]
            lap_now = laplace(lambda k: second[shot, k], at, cz, cx, cp, cm)
            third = 2.0 * second[shot, at] + turn[shot, at - 1] + rigid * lap_now
            adj = late(shot, at) + hits * third
            adj = adj + laplace(lambda k: scaled[shot, k], at, cz, cx, cp, cm)
            if 2 <= at < planes + 2:
                upper[shot, at - 1] = adj
            else:
                scaled_near[shot, int(at > 1), PAD : wide - PAD] = (rigid * adj)[PAD : wide - PAD]
            if 2 <= at < planes + 2:
                lap_second[shot, at - 2] = lap_now
    for shot in range(shots):
        for at in range(2, planes + 2):
            scaled[shot, at] = stiff[at] * upper[shot, at - 1]
        for side, at in enumerate((1, planes + 2)):
            scaled[shot, at, PAD : wide - PAD] = scaled_near[shot, side, PAD : wide - PAD]
    for at in range(2, planes + 2):
        total = None
        for shot in range(shots):
            hits = dense[shot][0, (at - 1) * wide : at * wide]
            lower = 2.0 * upper[shot, at - 1] - low[shot, at - 2] + hits * second[shot, at]
            lower = lower + laplace(lambda k: scaled[shot, k], at, cz, cx, cp, cm)
            term = upper[shot, at - 1] * lap_second[shot, at - 2] + lower * lap(shot, at)
            total = term if total is None else total + term
        out[at - 2] = (stiff[at] * total)[PAD : wide - PAD]


def tile_max(value):
    planes, rows, cols = value.shape
    return jnp.max(jnp.abs(value).reshape(planes * rows // 8, 8, cols), axis=0)


def sum_kernel(mine, other, total, edges):
    value = mine[...] + other[...]
    total[...] = value
    first = lax.axis_index("lat") == 0
    planes, rows, _ = value.shape
    for at in range(planes):
        edges[at * PAD : (at + 1) * PAD] = jnp.where(
            first, value[at, rows - PAD :], value[at, :PAD]
        )
    edges[planes * PAD :] = tile_max(value)


def last_sum_kernel(mine, other, total, largest):
    value = mine[...] + other[...]
    total[...] = value
    largest[...] = tile_max(value)


def widen_kernel(total, mine, got, out, to_even, to_odd):
    planes, rows, _ = total.shape
    wide = rows + 2 * PAD
    lat_at = lax.axis_index("lat")
    even = lax.axis_index("depth") % 2 == 0
    for at in range(planes):
        part = got[at * PAD : (at + 1) * PAD]
        out[at * wide : (at + 1) * wide] = with_rows(part, total[at], lat_at)
    low, top = out[:wide], out[(planes - 1) * wide :]
    to_even[:wide] = jnp.where(even, top, low)
    to_odd[:wide] = jnp.where(even, low, top)
    low, top = total[0], total[planes - 1]
    to_even[wide : wide + rows] = jnp.where(even, low, top)
    to_odd[wide : wide + rows] = jnp.where(even, top, low)
    largest = jnp.maximum(mine[planes * PAD :], got[planes * PAD :])
    to_even[wide + rows :] = largest
    to_odd[wide + rows :] = largest


def restiff_kernel(stiff, mine, by_even, by_odd, largest, velocity, stiff_out, vel_out):
    planes, rows, own = velocity.shape
    wide = rows + 2 * PAD
    even = lax.axis_index("depth") % 2 == 0
    shot_at = lax.axis_index("shot")
    cols = mine.shape[1]
    scale = jnp.max(jnp.max(largest[...], axis=1, keepdims=True), axis=0, keepdims=True) + EPSILON
    for at in range(-2, planes + 2):
        if 0 <= at < planes:
            value = mine[at * wide : (at + 1) * wide]
        else:
            a, b = (by_even, by_odd) if at >= planes else (by_odd, by_even)
            if at in (-1, planes):
                value = jnp.where(even, a[:wide], b[:wide])
            else:
                value = jnp.where(even, a[wide : wide + rows], b[wide : wide + rows])
                empty = jnp.zeros((PAD, cols), jnp.float32)
                value = jnp.concatenate([empty, value, empty], axis=0)
        value = value / scale
        stiff_out[at + 2] = stiff[at + 2] * jnp.exp(-2.0 * STEP_SIZE * value)
        if 0 <= at < planes:
            shifted = pltpu.roll(value[PAD : PAD + rows], (cols - shot_at * own) % cols, 1)
            vel_out[at] = velocity[at] * jnp.exp(-STEP_SIZE * shifted[:, :own])


def finish_kernel(total, largest, velocity, vel_out, dir_out):
    planes, _, own = velocity.shape
    shot_at = lax.axis_index("shot")
    cols = total.shape[2]
    scale = jnp.max(jnp.max(largest[...], axis=1, keepdims=True), axis=0, keepdims=True) + EPSILON
    for at in range(planes):
        value = total[at] / scale
        shifted = pltpu.roll(value, (cols - shot_at * own) % cols, 1)[:, :own]
        dir_out[at] = shifted
        vel_out[at] = velocity[at] * jnp.exp(-STEP_SIZE * shifted)


def shards(
    fwd_prev,
    fwd_now,
    adj_late,
    adj_last,
    velocity,
    density,
    wavelet,
    source_cell,
    receiver_cell,
    observed,
):
    shots, planes, rows, cols = fwd_now.shape
    depth_count = lax.axis_size("depth")
    shot_count = lax.axis_size("shot")
    lat_count = lax.axis_size("lat")
    if depth_count < 2 or planes != 2 or wavelet.shape[1] != 2 or lat_count != 2:
        raise ValueError("unsupported split")
    depth_at = lax.axis_index("depth")
    lat_at = lax.axis_index("lat")
    evens = even_pairs(depth_count)
    odds = odd_pairs(depth_count)
    swap = [(0, 1), (1, 0)]
    wide = rows + 2 * PAD

    def shot_terms(block):
        if shot_count == 2:
            return block, lax.ppermute(block, "shot", swap)
        return lax.psum(block, "shot"), jnp.zeros_like(block)

    def depth_max(value):
        if depth_count & (depth_count - 1):
            return lax.pmax(value, "depth")
        if depth_count <= 4:
            parts = [
                send(value, "depth", [(i, i ^ k) for i in range(depth_count)])
                for k in range(1, depth_count)
            ]
            for part in parts:
                value = jnp.maximum(value, part)
            return value
        step = 1
        while step < depth_count:
            pairs = [(i, i ^ step) for i in range(depth_count)]
            value = jnp.maximum(value, send(value, "depth", pairs))
            step *= 2
        return value

    hbm = pl.BlockSpec(memory_space=pltpu.HBM)
    spec = pl.BlockSpec(memory_space=pltpu.VMEM)

    def load(kernel, shapes, args, scratch, count):
        return pl.pallas_call(
            kernel,
            out_shape=tuple(pltpu.VMEM(*shape) for shape in shapes),
            in_specs=[hbm] * len(args),
            out_specs=tuple(spec for _ in shapes),
            scratch_shapes=scratch + [pltpu.SemaphoreType.DMA((count,))],
            compiler_params=pltpu.CompilerParams(vmem_limit_bytes=4 << 20),
        )(*[pltpu.with_memory_space_constraint(a, pltpu.HBM) for a in args])

    own_planes = (shots + 1) * planes
    first, first_edges = load(
        first_kernel,
        [((own_planes + 1, rows, cols), jnp.float32), ((own_planes * PAD, cols), jnp.float32)],
        (fwd_now, density, velocity),
        [pltpu.VMEM(velocity.shape, jnp.float32)],
        shots + 2,
    )
    first_odd = send(first, "depth", odds)
    first_even = send(first, "depth", evens)
    first_edges = send(first_edges, "lat", swap)
    second, late, cells, recorded = load(
        second_kernel,
        [
            ((2 * shots * planes, rows, cols), jnp.float32),
            (adj_late.shape, jnp.float32),
            (receiver_cell.shape, receiver_cell.dtype),
            (observed.shape, jnp.float32),
        ],
        (fwd_prev, adj_last, adj_late, receiver_cell, observed),
        [],
        2 * shots + 3,
    )
    second_odd = send(second, "depth", odds)
    second_even = send(second, "depth", evens)

    small = (planes + 1, wide, cols)
    to_even, to_odd, lines, line_edges = on_chip(
        third_kernel,
        [(2 * shots, rows, cols)] * 2 + [(3, rows, cols), (3 * PAD, cols)],
        (first, first_even, first_odd, first_edges, late),
        scratch=[(shots, planes + 2, wide, cols), (planes + 2, wide, cols)] + [small] * 4,
    )
    line_edges = send(line_edges, "lat", swap)
    third_odd = send(to_odd, "depth", odds)
    third_even = send(to_even, "depth", evens)

    (lines,) = on_chip(stretch_kernel, [(3, wide, cols)], (lines, line_edges))
    if shot_count == 2:
        parts = (lines, send(lines, "shot", swap))
    else:
        gathered = lax.all_gather(lines, "shot")
        parts = tuple(gathered[k] for k in range(shot_count))

    full_rows = rows * lat_count
    depth_start = depth_at * planes
    row_start = lat_at * rows

    def place(cells, margin):
        plane_at = cells // (full_rows * cols) - depth_start + margin
        row_at = cells // cols % full_rows - row_start + PAD
        inside = (
            (plane_at >= 0)
            & (plane_at < planes + 2 * margin)
            & (row_at >= 0)
            & (row_at < wide)
        )
        return jnp.where(inside, plane_at * wide + row_at, -1), cells % cols

    row_id, col_id = place(cells, 1)
    spread_shape = (3, (planes + 2) * wide, cols)

    def receivers(shot):
        (out,) = on_chip(
            spread_kernel,
            [spread_shape],
            (row_id[shot : shot + 1], col_id[shot : shot + 1], recorded[shot]),
            flops=14 * spread_shape[1] * cols * row_id.shape[1],
            limit=24,
        )
        return out

    dense = []
    for shot in range(shots):
        dense.append(receivers(shot))
    dense = tuple(dense)
    early = (first, second, late, first_even, first_odd, second_even, second_odd)
    strips = shots * (4 * planes + 12) + planes + 4
    (edges,) = on_chip(early_edge_kernel, [(strips * PAD, cols)], early)
    edges = send(edges, "lat", swap)
    deep = planes + 4
    model = (wide, cols)
    scalars = pl.BlockSpec(memory_space=pltpu.SMEM)
    shapes = [
        (shots, planes + 2) + model,
        (shots, deep) + model,
        (shots, planes + 2) + model,
        (shots, planes) + model,
        (shots, 2) + model,
        (shots, deep) + model,
        (shots, planes) + model,
        (deep,) + model,
        (planes + 3,) + model,
        (planes + 3,) + model,
        (planes + 3,) + model,
        (planes + 3,) + model,
    ]
    vectors = early + (edges,) + dense
    outs = pl.pallas_call(
        functools.partial(early_kernel, full_rows, shots),
        out_shape=tuple(pltpu.VMEM(shape, jnp.float32) for shape in shapes),
        in_specs=[spec] * len(vectors) + [scalars, scalars],
        out_specs=tuple(spec for _ in shapes),
        scratch_shapes=[
            pltpu.VMEM((shots, deep) + model, jnp.float32),
            pltpu.VMEM((deep,) + model, jnp.float32),
        ],
        compiler_params=pltpu.CompilerParams(vmem_limit_bytes=8 << 20),
        name="early",
    )(*[pltpu.with_memory_space_constraint(a, pltpu.VMEM) for a in vectors], source_cell, wavelet)
    lap, base, turn, late_own, ahead, last, low, dens, cz, cx, cp, cm = outs

    final = (third_even, third_odd) + parts
    shape = adj_late.shape
    lap_far, late_near, stiff = on_chip(
        functools.partial(final_kernel, shape, len(parts)),
        [(shots, 2) + model, (shots, 2) + model, (deep,) + model],
        final + (dens, ahead),
    )

    def gradient_of(stiff):
        (out,) = on_chip(
            functools.partial(update_kernel, shots),
            [(planes, rows, cols)],
            (stiff, lap, lap_far, base, turn, late_own, late_near, last, low, cz, cx, cp, cm) + dense,
            scratch=[
                (shots, deep) + model,
                (shots, deep) + model,
                (shots, planes + 2) + model,
                (shots, planes) + model,
                (shots, 2) + model,
            ],
        )
        return out

    own_velocity = velocity
    for update_index in range(ITERS):
        mine, other = shot_terms(gradient_of(stiff))
        if update_index + 1 == ITERS:
            summed, largest = on_chip(
                last_sum_kernel, [(planes, rows, cols), (8, cols)], (mine, other)
            )
            largest = jnp.maximum(largest, lax.ppermute(largest, "lat", swap))
            largest = depth_max(largest)
            return tuple(
                on_chip(
                    finish_kernel,
                    [velocity.shape, velocity.shape],
                    (summed, largest, own_velocity),
                    keep=False,
                )
            )
        edge_rows = planes * PAD + 8
        summed, tail = on_chip(sum_kernel, [(planes, rows, cols), (edge_rows, cols)], (mine, other))
        got = send(tail, "lat", swap)
        widened, to_even, to_odd = on_chip(
            widen_kernel,
            [(planes * wide, cols)] + [(wide + rows + 8, cols)] * 2,
            (summed, tail, got),
        )
        end = wide + rows
        if depth_count == 4:
            by_odd = send(to_odd, "depth", [(i, i ^ 3) for i in range(4)])
            by_even = send(to_even, "depth", evens)
            further = send(to_even[end:], "depth", [(i, i ^ 2) for i in range(4)])
            largest = jnp.maximum(
                jnp.maximum(to_even[end:], further), jnp.maximum(by_odd[end:], by_even[end:])
            )
        else:
            by_even = send(to_even, "depth", evens)
            by_odd = send(to_odd, "depth", odds)
            largest = depth_max(to_even[end:])
        stiff, own_velocity = on_chip(
            restiff_kernel,
            [stiff.shape, velocity.shape],
            (stiff, widened, by_even, by_odd, largest, own_velocity),
        )


def solution(mesh):
    fields = P(("grp", "shot"), "depth", "lat", None)
    model = P(("grp", "depth"), "lat", "shot")
    placed = (
        fields,
        fields,
        fields,
        fields,
        model,
        P(("grp", "depth"), "lat", None),
        P(("grp", "shot"), None),
        P(("grp", "shot")),
        P(("grp", "shot"), None),
        P(("grp", "shot"), None, None),
    )

    return jax.shard_map(
        shards,
        mesh=mesh,
        in_specs=placed,
        out_specs=(model, model),
        check_vma=False,
    )
```

```python
import functools

import jax
import jax.numpy as jnp
from jax import lax
from jax.experimental import pallas as pl
from jax.experimental.pallas import tpu as pltpu
from jax.sharding import PartitionSpec as P


ITERS = 2

COURANT = 0.1
STEP_SIZE = 0.1
EPSILON = 1e-06
PAD = 8
NOW, PREV, LAST, LATE, DENS, VEL, LAP = range(7)


def even_pairs(count):
    return [(i, i ^ 1) for i in range(count) if i ^ 1 < count]


def odd_pairs(count):
    ups = [(i, i + 1) for i in range(1, count - 1, 2)]
    return ups + [(b, a) for a, b in ups]


def send(block, axis, pairs):
    if not pairs:
        return jnp.zeros_like(block)
    return lax.ppermute(block, axis, pairs)


def on_chip(kernel, out_shapes, args, scratch=(), flops=0, limit=8, keep=True):
    spec = pl.BlockSpec(memory_space=pltpu.VMEM)
    place = pltpu.VMEM if keep else jax.ShapeDtypeStruct
    outs = tuple(place(shape, jnp.float32) for shape in out_shapes)
    moved = sum(a.size * 4 for a in args)
    return pl.pallas_call(
        kernel,
        out_shape=outs,
        in_specs=[spec] * len(args),
        out_specs=tuple(spec for _ in outs),
        scratch_shapes=[pltpu.VMEM(shape, jnp.float32) for shape in scratch],
        compiler_params=pltpu.CompilerParams(vmem_limit_bytes=limit << 20),
        cost_estimate=pl.CostEstimate(flops=flops, bytes_accessed=moved, transcendentals=0),
    )(*[pltpu.with_memory_space_constraint(a, pltpu.VMEM) for a in args])


def copy_all(copies, sems):
    copies = [
        pltpu.make_async_copy(source, target, sems.at[index])
        for index, (source, target) in enumerate(copies)
    ]
    for copy in copies:
        copy.start()
    for copy in copies:
        copy.wait()


def first_kernel(now, dens, vel, out, edges, vel_buf, sems):
    shots, planes, rows, cols = now.shape
    count = shots * planes
    copies = [
        (now.at[shot], out.at[shot * planes : (shot + 1) * planes]) for shot in range(shots)
    ]
    copies += [(dens, out.at[count : count + planes]), (vel, vel_buf)]
    copy_all(copies, sems)
    lines = [vel_buf[at] for at in range(planes)]
    spare = cols - planes * vel.shape[2]
    if spare:
        lines.append(jnp.zeros((rows, spare), jnp.float32))
    out[count + planes] = jnp.concatenate(lines, axis=1)
    first = lax.axis_index("lat") == 0
    for at in range(count + planes):
        edges[at * PAD : (at + 1) * PAD] = jnp.where(
            first, out[at, rows - PAD :], out[at, :PAD]
        )


def second_kernel(prev, last, late, cells, observed, out, late_out, cells_out, observed_out, sems):
    shots, planes, _, _ = prev.shape
    copies = []
    start = 0
    for field in (prev, last):
        for shot in range(shots):
            copies.append((field.at[shot], out.at[start : start + planes]))
            start += planes
    copies += [(late, late_out), (cells, cells_out), (observed, observed_out)]
    copy_all(copies, sems)


def spread_kernel(row_ref, col_ref, obs_ref, out_ref):
    nrec = row_ref.shape[1]
    rows, cols = out_ref.shape[1:]
    steps = obs_ref.shape[0]
    row_iota = lax.broadcasted_iota(jnp.int32, (rows, nrec), 0)
    col_iota = lax.broadcasted_iota(jnp.int32, (cols, nrec), 0)
    at_row = (row_ref[...] == row_iota).astype(jnp.float32).astype(jnp.bfloat16)
    at_col = col_ref[...] == col_iota
    parts = [(0, at_col.astype(jnp.float32).astype(jnp.bfloat16))]
    for step in range(steps):
        obs = obs_ref[step : step + 1, :]
        high = obs.astype(jnp.bfloat16).astype(jnp.float32)
        rest = obs - high
        middle = rest.astype(jnp.bfloat16).astype(jnp.float32)
        for piece in (high, middle, rest - middle):
            parts.append((1 + step, jnp.where(at_col, piece, 0.0).astype(jnp.bfloat16)))
    sums = [None] * (1 + steps)
    for start in range(0, len(parts), 2):
        pair = parts[start : start + 2]
        both = lax.dot_general(
            at_row,
            jnp.concatenate([p for _, p in pair], axis=0),
            (((1,), (1,)), ((), ())),
            preferred_element_type=jnp.float32,
        )
        for place, (which, _) in enumerate(pair):
            term = both[:, place * cols : (place + 1) * cols]
            sums[which] = term if sums[which] is None else sums[which] + term
    for which, value in enumerate(sums):
        out_ref[which] = value


class Halo:
    def __init__(self, shape, first=None, second=None, late=None, by=(), vel=()):
        self.even = lax.axis_index("depth") % 2 == 0
        self.first, self.second, self.late, self.vel = first, second, late, vel
        self.by = by
        self.shots, self.planes, self.rows, self.cols = shape

    def pick(self, batch, upper, index):
        even, odd = self.by[batch]
        a, b = (even, odd) if upper else (odd, even)
        return jnp.where(self.even, a[index], b[index])

    def plane(self, item):
        which, shot, at = item
        planes, shots = self.planes, self.shots
        inside = 0 <= at < planes
        upper = at >= planes
        step = at if inside else (at - planes if upper else planes + at)
        if which == VEL:
            block, lane = (0, 1, 2)[(at + planes) // planes], (at + planes) % planes
            own = self.cols // len(self.vel)
            column = lax.broadcasted_iota(jnp.int32, self.vel[0].shape[1:], 1)
            value = None
            planes_of = [part[block] for part in self.vel]
            if len(planes_of) == 2:
                mine, other = planes_of
                here = lax.axis_index("shot") == 0
                planes_of = [jnp.where(here, mine, other), jnp.where(here, other, mine)]
            for index, part in enumerate(planes_of):
                shifted = pltpu.roll(part, (index - lane) * own % self.cols, 1)
                value = shifted if value is None else jnp.where(column >= index * own, shifted, value)
            return value
        if which == LAP:
            return self.pick("third", upper, shots + shot)
        if which == LATE:
            return self.late[shot, at] if inside else self.pick("third", upper, shot)
        if which in (NOW, DENS):
            index = (shot if which == NOW else shots) * planes + step
            return self.first[index] if inside else self.pick("first", upper, index)
        index = ((0 if which == PREV else shots) + shot) * planes + step
        return self.second[index] if inside else self.pick("second", upper, index)

    def early_list(self):
        planes = self.planes
        out = []
        for which, margin in ((NOW, 2), (PREV, 2), (LAST, 2), (LATE, 0)):
            for shot in range(self.shots):
                for at in range(-margin, planes + margin):
                    out.append((which, shot, at))
        return out + [(DENS, 0, at) for at in range(-2, planes + 2)]


def write_edges(halo, items, out):
    first = lax.axis_index("lat") == 0
    rows = halo.rows
    for index, item in enumerate(items):
        value = halo.plane(item)
        out[index * PAD : (index + 1) * PAD] = jnp.where(first, value[rows - PAD :], value[:PAD])


def reader(halo, items, edges):
    lat_at = lax.axis_index("lat")
    where_is = {item: index for index, item in enumerate(items)}

    def whole(which, shot, at):
        item = (which, shot, at)
        index = where_is[item]
        return with_rows(edges[index * PAD : (index + 1) * PAD], halo.plane(item), lat_at)

    return whole


def early_halo(first, second, late, fe, fo, se, so):
    return Halo(late.shape, first, second, late, {"first": (fe, fo), "second": (se, so)})


def final_halo(shape, te, to, *vel):
    return Halo(shape, by={"third": (te, to)}, vel=vel)


def early_edge_kernel(*refs):
    halo = early_halo(*refs[:7])
    write_edges(halo, halo.early_list(), refs[7])


def stretch_kernel(lines, got, out):
    lat_at = lax.axis_index("lat")
    for block in range(3):
        out[block] = with_rows(got[block * PAD : (block + 1) * PAD], lines[block], lat_at)


def near_cols(value):
    lane = lax.broadcasted_iota(jnp.int32, value.shape, 1)
    cols = value.shape[1]
    above = jnp.where(lane == cols - 1, 0.0, pltpu.roll(value, cols - 1, 1))
    below = jnp.where(lane == 0, 0.0, pltpu.roll(value, 1, 1))
    return above, below


def laplace(field, at, cz, cx, cp, cm):
    middle = field(at)
    rows = middle.shape[0]
    flux = cx(at) * (pltpu.roll(middle, rows - 1, 0) - middle)
    total = flux - pltpu.roll(flux, 1, 0)
    above, below = near_cols(middle)
    total = total + (cp(at) * (above - middle) + cm(at) * (below - middle))
    return total + (cz(at) * (field(at + 1) - middle) + cz(at - 1) * (field(at - 1) - middle))


def inverse(density):
    inside = density > 0.0
    return jnp.where(inside, 1.0 / jnp.where(inside, density, 1.0), 0.0)


def with_rows(part, value, lat_at):
    low = jnp.where(lat_at == 1, part, 0.0)
    high = jnp.where(lat_at == 0, part, 0.0)
    return jnp.concatenate([low, value, high], axis=0)


def couple(buoy, at, cz, cx, cp, cm):
    plane = buoy(at)
    cz(at, 0.5 * (plane + buoy(at + 1)))
    cx(at, 0.5 * (plane + pltpu.roll(plane, plane.shape[0] - 1, 0)))
    above, below = near_cols(plane)
    cp(at, 0.5 * (plane + above))
    cm(at, 0.5 * (plane + below))


def third_kernel(
    first, by_even, by_odd, edges, late, to_even, to_odd, lines, line_edges, now_buf, buoy_buf, cz, cx, cp, cm
):
    even = lax.axis_index("depth") % 2 == 0
    lat_at = lax.axis_index("lat")
    shots, planes, rows, cols = late.shape
    place = (shots + 1) * planes
    lines[0] = jnp.where(even, by_odd[place], by_even[place])
    lines[1] = first[place]
    lines[2] = jnp.where(even, by_even[place], by_odd[place])
    for block in range(3):
        line_edges[block * PAD : (block + 1) * PAD] = jnp.where(
            lat_at == 0, lines[block, rows - PAD :], lines[block, :PAD]
        )

    def whole(index, at):
        if 0 <= at < planes:
            place = index * planes + at
            return with_rows(edges[place * PAD : (place + 1) * PAD], first[place], lat_at)
        upper = at >= planes
        a, b = (by_even, by_odd) if upper else (by_odd, by_even)
        place = index * planes + (0 if upper else planes - 1)
        empty = jnp.zeros((PAD, cols), jnp.float32)
        return jnp.concatenate([empty, jnp.where(even, a[place], b[place]), empty], axis=0)

    for at in range(-1, planes + 1):
        buoy_buf[at + 1] = inverse(whole(shots, at))
        for shot in range(shots):
            now_buf[shot, at + 1] = whole(shot, at)

    def put(ref):
        def store(at, value):
            ref[at + 1] = value

        return store

    for at in range(-1, planes):
        couple(lambda k: buoy_buf[k + 1], at, put(cz), put(cx), put(cp), put(cm))
    for shot in range(shots):
        ends = [
            laplace(
                lambda k: now_buf[shot, k + 1],
                at,
                lambda k: cz[k + 1],
                lambda k: cx[k + 1],
                lambda k: cp[k + 1],
                lambda k: cm[k + 1],
            )[PAD : PAD + rows]
            for at in (planes - 2, 1)
        ]
        low, top = late[shot, 0], late[shot, planes - 1]
        to_even[shot] = jnp.where(even, top, low)
        to_odd[shot] = jnp.where(even, low, top)
        to_even[shots + shot] = jnp.where(even, ends[0], ends[1])
        to_odd[shots + shot] = jnp.where(even, ends[1], ends[0])


def early_kernel(full_rows, shots, *refs):
    halo = early_halo(*refs[:7])
    edges, *dense = refs[7 : 8 + shots]
    source, wavelet = refs[8 + shots : 10 + shots]
    lap_out, base_out, turn_out, late_own, late_near, last_out, low_out = refs[10 + shots : 17 + shots]
    dens_out, cz, cx, cp, cm, now_buf, buoy_buf = refs[17 + shots :]
    rows, cols, planes = halo.rows, halo.cols, halo.planes
    wide = rows + 2 * PAD
    whole = reader(halo, halo.early_list(), edges)

    for at in range(-2, planes + 2):
        density = whole(DENS, 0, at)
        dens_out[at + 2] = density
        buoy_buf[at + 2] = inverse(density)
        for shot in range(shots):
            now_buf[shot, at + 2] = whole(NOW, shot, at)

    def put(ref):
        def store(at, value):
            ref[at + 2] = value

        return store

    for at in range(-2, planes + 1):
        couple(lambda k: buoy_buf[k + 2], at, put(cz), put(cx), put(cp), put(cm))
    line = lax.broadcasted_iota(jnp.int32, (wide, cols), 0)
    column = lax.broadcasted_iota(jnp.int32, (wide, cols), 1)
    depth_start = lax.axis_index("depth") * planes
    row_start = lax.axis_index("lat") * rows
    for shot in range(shots):
        cell = source[shot]
        source_line = lax.div(cell, cols)
        source_plane = lax.div(source_line, full_rows) - depth_start
        source_row = lax.rem(source_line, full_rows) - row_start + PAD
        spot = (line == source_row) & (column == lax.rem(cell, cols))
        for at in range(-2, planes + 2):
            here = spot & (source_plane == at)
            middle = now_buf[shot, at + 2]
            if -1 <= at < planes + 1:
                lap_out[shot, at + 1] = laplace(
                    lambda k: now_buf[shot, k + 2],
                    at,
                    lambda k: cz[k + 2],
                    lambda k: cx[k + 2],
                    lambda k: cp[k + 2],
                    lambda k: cm[k + 2],
                )
            base_out[shot, at + 2] = (
                2.0 * middle - whole(PREV, shot, at) + jnp.where(here, wavelet[shot, 0], 0.0)
            )
            newest = whole(LAST, shot, at)
            last_out[shot, at + 2] = newest
            if -1 <= at < planes + 1:
                turn_out[shot, at + 1] = jnp.where(here, wavelet[shot, 1], 0.0) - middle
                ahead = 2.0 * newest - dense[shot][2, (at + 1) * wide : (at + 2) * wide]
                if 0 <= at < planes:
                    late_own[shot, at] = ahead - whole(LATE, shot, at)
                else:
                    late_near[shot, int(at >= 0)] = ahead
            if 0 <= at < planes:
                low_out[shot, at] = newest + dense[shot][1, (at + 1) * wide : (at + 2) * wide]


def final_kernel(shape, vels, *refs):
    halo = final_halo(shape, *refs[: 2 + vels])
    dens, ahead, lap_far, late_near, stiff_out = refs[2 + vels :]
    planes = halo.planes
    empty = jnp.zeros((PAD, halo.cols), jnp.float32)

    def whole(which, shot, at):
        return jnp.concatenate([empty, halo.plane((which, shot, at)), empty], axis=0)

    for at in range(-2, planes + 2):
        speed = halo.plane((VEL, 0, at)) * COURANT
        stiff_out[at + 2] = speed * speed * dens[at + 2]
    for shot in range(halo.shots):
        for side, (near, far) in enumerate(((-1, -2), (planes, planes + 1))):
            lap_far[shot, side] = whole(LAP, shot, far)
            late_near[shot, side] = ahead[shot, side] - whole(LATE, shot, near)


def update_kernel(shots, *refs):
    stiff, lap_mid, lap_far, base, turn, late_own, late_near, last, low = refs[:9]
    cz_ref, cx_ref, cp_ref, cm_ref = refs[9:13]
    dense = refs[13 : 13 + shots]
    out, second, scaled, upper, lap_second, scaled_near = refs[13 + shots :]
    planes = low.shape[1]
    wide, _ = low.shape[2:]

    def lap(shot, at):
        if 1 <= at < planes + 3:
            return lap_mid[shot, at - 1]
        return lap_far[shot, int(at > 0)]

    def late(shot, at):
        if 2 <= at < planes + 2:
            return late_own[shot, at - 2]
        return late_near[shot, int(at > 1)]

    cz = lambda k: cz_ref[k]
    cx = lambda k: cx_ref[k]
    cp = lambda k: cp_ref[k]
    cm = lambda k: cm_ref[k]
    for at in range(planes + 4):
        rigid = stiff[at]
        for shot in range(shots):
            second[shot, at] = base[shot, at] + rigid * lap(shot, at)
            scaled[shot, at] = rigid * last[shot, at]
    for at in range(1, planes + 3):
        rigid = stiff[at]
        for shot in range(shots):
            hits = dense[shot][0, (at - 1) * wide : at * wide]
            lap_now = laplace(lambda k: second[shot, k], at, cz, cx, cp, cm)
            third = 2.0 * second[shot, at] + turn[shot, at - 1] + rigid * lap_now
            adj = late(shot, at) + hits * third
            adj = adj + laplace(lambda k: scaled[shot, k], at, cz, cx, cp, cm)
            if 2 <= at < planes + 2:
                upper[shot, at - 1] = adj
            else:
                scaled_near[shot, int(at > 1), PAD : wide - PAD] = (rigid * adj)[PAD : wide - PAD]
            if 2 <= at < planes + 2:
                lap_second[shot, at - 2] = lap_now
    for shot in range(shots):
        for at in range(2, planes + 2):
            scaled[shot, at] = stiff[at] * upper[shot, at - 1]
        for side, at in enumerate((1, planes + 2)):
            scaled[shot, at, PAD : wide - PAD] = scaled_near[shot, side, PAD : wide - PAD]
    for at in range(2, planes + 2):
        total = None
        for shot in range(shots):
            hits = dense[shot][0, (at - 1) * wide : at * wide]
            lower = 2.0 * upper[shot, at - 1] - low[shot, at - 2] + hits * second[shot, at]
            lower = lower + laplace(lambda k: scaled[shot, k], at, cz, cx, cp, cm)
            term = upper[shot, at - 1] * lap_second[shot, at - 2] + lower * lap(shot, at)
            total = term if total is None else total + term
        out[at - 2] = (stiff[at] * total)[PAD : wide - PAD]


def tile_max(value):
    planes, rows, cols = value.shape
    return jnp.max(jnp.abs(value).reshape(planes * rows // 8, 8, cols), axis=0)


def sum_kernel(mine, other, total, edges):
    value = mine[...] + other[...]
    total[...] = value
    first = lax.axis_index("lat") == 0
    planes, rows, _ = value.shape
    for at in range(planes):
        edges[at * PAD : (at + 1) * PAD] = jnp.where(
            first, value[at, rows - PAD :], value[at, :PAD]
        )
    edges[planes * PAD :] = tile_max(value)


def last_sum_kernel(mine, other, total, largest):
    value = mine[...] + other[...]
    total[...] = value
    largest[...] = tile_max(value)


def widen_kernel(total, mine, got, out, to_even, to_odd):
    planes, rows, _ = total.shape
    wide = rows + 2 * PAD
    lat_at = lax.axis_index("lat")
    even = lax.axis_index("depth") % 2 == 0
    for at in range(planes):
        part = got[at * PAD : (at + 1) * PAD]
        out[at * wide : (at + 1) * wide] = with_rows(part, total[at], lat_at)
    low, top = out[:wide], out[(planes - 1) * wide :]
    to_even[:wide] = jnp.where(even, top, low)
    to_odd[:wide] = jnp.where(even, low, top)
    low, top = total[0], total[planes - 1]
    to_even[wide : wide + rows] = jnp.where(even, low, top)
    to_odd[wide : wide + rows] = jnp.where(even, top, low)
    largest = jnp.maximum(mine[planes * PAD :], got[planes * PAD :])
    to_even[wide + rows :] = largest
    to_odd[wide + rows :] = largest


def restiff_kernel(stiff, mine, by_even, by_odd, largest, velocity, stiff_out, vel_out):
    planes, rows, own = velocity.shape
    wide = rows + 2 * PAD
    even = lax.axis_index("depth") % 2 == 0
    shot_at = lax.axis_index("shot")
    cols = mine.shape[1]
    scale = jnp.max(jnp.max(largest[...], axis=1, keepdims=True), axis=0, keepdims=True) + EPSILON
    for at in range(-2, planes + 2):
        if 0 <= at < planes:
            value = mine[at * wide : (at + 1) * wide]
        else:
            a, b = (by_even, by_odd) if at >= planes else (by_odd, by_even)
            if at in (-1, planes):
                value = jnp.where(even, a[:wide], b[:wide])
            else:
                value = jnp.where(even, a[wide : wide + rows], b[wide : wide + rows])
                empty = jnp.zeros((PAD, cols), jnp.float32)
                value = jnp.concatenate([empty, value, empty], axis=0)
        value = value / scale
        stiff_out[at + 2] = stiff[at + 2] * jnp.exp(-2.0 * STEP_SIZE * value)
        if 0 <= at < planes:
            shifted = pltpu.roll(value[PAD : PAD + rows], (cols - shot_at * own) % cols, 1)
            vel_out[at] = velocity[at] * jnp.exp(-STEP_SIZE * shifted[:, :own])


def finish_kernel(total, largest, velocity, vel_out, dir_out, vel_buf, dir_buf, sems):
    planes, _, own = velocity.shape
    shot_at = lax.axis_index("shot")
    cols = total.shape[2]
    scale = jnp.max(jnp.max(largest[...], axis=1, keepdims=True), axis=0, keepdims=True) + EPSILON
    for at in range(planes):
        value = total[at] / scale
        dir_buf[at] = pltpu.roll(value, (cols - shot_at * own) % cols, 1)[:, :own]
    to_dir = pltpu.make_async_copy(dir_buf, dir_out, sems.at[0])
    to_dir.start()
    for at in range(planes):
        vel_buf[at] = velocity[at] * jnp.exp(-STEP_SIZE * dir_buf[at])
    to_vel = pltpu.make_async_copy(vel_buf, vel_out, sems.at[1])
    to_vel.start()
    to_dir.wait()
    to_vel.wait()


def shards(
    fwd_prev,
    fwd_now,
    adj_late,
    adj_last,
    velocity,
    density,
    wavelet,
    source_cell,
    receiver_cell,
    observed,
):
    shots, planes, rows, cols = fwd_now.shape
    depth_count = lax.axis_size("depth")
    shot_count = lax.axis_size("shot")
    lat_count = lax.axis_size("lat")
    if depth_count < 2 or planes != 2 or wavelet.shape[1] != 2 or lat_count != 2:
        raise ValueError("unsupported split")
    depth_at = lax.axis_index("depth")
    lat_at = lax.axis_index("lat")
    evens = even_pairs(depth_count)
    odds = odd_pairs(depth_count)
    swap = [(0, 1), (1, 0)]
    wide = rows + 2 * PAD

    def shot_terms(block):
        if shot_count == 2:
            return block, lax.ppermute(block, "shot", swap)
        return lax.psum(block, "shot"), jnp.zeros_like(block)

    def depth_max(value):
        if depth_count & (depth_count - 1):
            return lax.pmax(value, "depth")
        if depth_count <= 4:
            parts = [
                send(value, "depth", [(i, i ^ k) for i in range(depth_count)])
                for k in range(1, depth_count)
            ]
            for part in parts:
                value = jnp.maximum(value, part)
            return value
        step = 1
        while step < depth_count:
            pairs = [(i, i ^ step) for i in range(depth_count)]
            value = jnp.maximum(value, send(value, "depth", pairs))
            step *= 2
        return value

    hbm = pl.BlockSpec(memory_space=pltpu.HBM)
    spec = pl.BlockSpec(memory_space=pltpu.VMEM)

    def load(kernel, shapes, args, scratch, count):
        return pl.pallas_call(
            kernel,
            out_shape=tuple(pltpu.VMEM(*shape) for shape in shapes),
            in_specs=[hbm] * len(args),
            out_specs=tuple(spec for _ in shapes),
            scratch_shapes=scratch + [pltpu.SemaphoreType.DMA((count,))],
            compiler_params=pltpu.CompilerParams(vmem_limit_bytes=4 << 20),
        )(*[pltpu.with_memory_space_constraint(a, pltpu.HBM) for a in args])

    own_planes = (shots + 1) * planes
    first, first_edges = load(
        first_kernel,
        [((own_planes + 1, rows, cols), jnp.float32), ((own_planes * PAD, cols), jnp.float32)],
        (fwd_now, density, velocity),
        [pltpu.VMEM(velocity.shape, jnp.float32)],
        shots + 2,
    )
    first_odd = send(first, "depth", odds)
    first_even = send(first, "depth", evens)
    first_edges = send(first_edges, "lat", swap)
    second, late, cells, recorded = load(
        second_kernel,
        [
            ((2 * shots * planes, rows, cols), jnp.float32),
            (adj_late.shape, jnp.float32),
            (receiver_cell.shape, receiver_cell.dtype),
            (observed.shape, jnp.float32),
        ],
        (fwd_prev, adj_last, adj_late, receiver_cell, observed),
        [],
        2 * shots + 3,
    )
    second_odd = send(second, "depth", odds)
    second_even = send(second, "depth", evens)

    small = (planes + 1, wide, cols)
    to_even, to_odd, lines, line_edges = on_chip(
        third_kernel,
        [(2 * shots, rows, cols)] * 2 + [(3, rows, cols), (3 * PAD, cols)],
        (first, first_even, first_odd, first_edges, late),
        scratch=[(shots, planes + 2, wide, cols), (planes + 2, wide, cols)] + [small] * 4,
    )
    line_edges = send(line_edges, "lat", swap)
    third_odd = send(to_odd, "depth", odds)
    third_even = send(to_even, "depth", evens)

    (lines,) = on_chip(stretch_kernel, [(3, wide, cols)], (lines, line_edges))
    if shot_count == 2:
        parts = (lines, send(lines, "shot", swap))
    else:
        gathered = lax.all_gather(lines, "shot")
        parts = tuple(gathered[k] for k in range(shot_count))

    full_rows = rows * lat_count
    depth_start = depth_at * planes
    row_start = lat_at * rows

    def place(cells, margin):
        plane_at = cells // (full_rows * cols) - depth_start + margin
        row_at = cells // cols % full_rows - row_start + PAD
        inside = (
            (plane_at >= 0)
            & (plane_at < planes + 2 * margin)
            & (row_at >= 0)
            & (row_at < wide)
        )
        return jnp.where(inside, plane_at * wide + row_at, -1), cells % cols

    row_id, col_id = place(cells, 1)
    spread_shape = (3, (planes + 2) * wide, cols)

    def receivers(shot):
        (out,) = on_chip(
            spread_kernel,
            [spread_shape],
            (row_id[shot : shot + 1], col_id[shot : shot + 1], recorded[shot]),
            flops=14 * spread_shape[1] * cols * row_id.shape[1],
            limit=24,
        )
        return out

    dense = []
    for shot in range(shots):
        dense.append(receivers(shot))
    dense = tuple(dense)
    early = (first, second, late, first_even, first_odd, second_even, second_odd)
    strips = shots * (4 * planes + 12) + planes + 4
    (edges,) = on_chip(early_edge_kernel, [(strips * PAD, cols)], early)
    edges = send(edges, "lat", swap)
    deep = planes + 4
    model = (wide, cols)
    scalars = pl.BlockSpec(memory_space=pltpu.SMEM)
    shapes = [
        (shots, planes + 2) + model,
        (shots, deep) + model,
        (shots, planes + 2) + model,
        (shots, planes) + model,
        (shots, 2) + model,
        (shots, deep) + model,
        (shots, planes) + model,
        (deep,) + model,
        (planes + 3,) + model,
        (planes + 3,) + model,
        (planes + 3,) + model,
        (planes + 3,) + model,
    ]
    vectors = early + (edges,) + dense
    outs = pl.pallas_call(
        functools.partial(early_kernel, full_rows, shots),
        out_shape=tuple(pltpu.VMEM(shape, jnp.float32) for shape in shapes),
        in_specs=[spec] * len(vectors) + [scalars, scalars],
        out_specs=tuple(spec for _ in shapes),
        scratch_shapes=[
            pltpu.VMEM((shots, deep) + model, jnp.float32),
            pltpu.VMEM((deep,) + model, jnp.float32),
        ],
        compiler_params=pltpu.CompilerParams(vmem_limit_bytes=8 << 20),
        name="early",
    )(*[pltpu.with_memory_space_constraint(a, pltpu.VMEM) for a in vectors], source_cell, wavelet)
    lap, base, turn, late_own, ahead, last, low, dens, cz, cx, cp, cm = outs

    final = (third_even, third_odd) + parts
    shape = adj_late.shape
    lap_far, late_near, stiff = on_chip(
        functools.partial(final_kernel, shape, len(parts)),
        [(shots, 2) + model, (shots, 2) + model, (deep,) + model],
        final + (dens, ahead),
    )

    def gradient_of(stiff):
        (out,) = on_chip(
            functools.partial(update_kernel, shots),
            [(planes, rows, cols)],
            (stiff, lap, lap_far, base, turn, late_own, late_near, last, low, cz, cx, cp, cm) + dense,
            scratch=[
                (shots, deep) + model,
                (shots, deep) + model,
                (shots, planes + 2) + model,
                (shots, planes) + model,
                (shots, 2) + model,
            ],
        )
        return out

    own_velocity = velocity
    for update_index in range(ITERS):
        mine, other = shot_terms(gradient_of(stiff))
        if update_index + 1 == ITERS:
            summed, largest = on_chip(
                last_sum_kernel, [(planes, rows, cols), (8, cols)], (mine, other)
            )
            largest = jnp.maximum(largest, lax.ppermute(largest, "lat", swap))
            largest = depth_max(largest)
            shape = velocity.shape
            return pl.pallas_call(
                finish_kernel,
                out_shape=(jax.ShapeDtypeStruct(shape, jnp.float32),) * 2,
                in_specs=[spec] * 3,
                out_specs=(pl.BlockSpec(memory_space=pltpu.HBM),) * 2,
                scratch_shapes=[
                    pltpu.VMEM(shape, jnp.float32),
                    pltpu.VMEM(shape, jnp.float32),
                    pltpu.SemaphoreType.DMA((2,)),
                ],
                compiler_params=pltpu.CompilerParams(vmem_limit_bytes=8 << 20),
                name="finish",
            )(
                *[
                    pltpu.with_memory_space_constraint(a, pltpu.VMEM)
                    for a in (summed, largest, own_velocity)
                ]
            )
        edge_rows = planes * PAD + 8
        summed, tail = on_chip(sum_kernel, [(planes, rows, cols), (edge_rows, cols)], (mine, other))
        got = send(tail, "lat", swap)
        widened, to_even, to_odd = on_chip(
            widen_kernel,
            [(planes * wide, cols)] + [(wide + rows + 8, cols)] * 2,
            (summed, tail, got),
        )
        end = wide + rows
        if depth_count == 4:
            by_odd = send(to_odd, "depth", [(i, i ^ 3) for i in range(4)])
            by_even = send(to_even, "depth", evens)
            further = send(to_even[end:], "depth", [(i, i ^ 2) for i in range(4)])
            largest = jnp.maximum(
                jnp.maximum(to_even[end:], further), jnp.maximum(by_odd[end:], by_even[end:])
            )
        else:
            by_even = send(to_even, "depth", evens)
            by_odd = send(to_odd, "depth", odds)
            largest = depth_max(to_even[end:])
        stiff, own_velocity = on_chip(
            restiff_kernel,
            [stiff.shape, velocity.shape],
            (stiff, widened, by_even, by_odd, largest, own_velocity),
        )


def solution(mesh):
    fields = P(("grp", "shot"), "depth", "lat", None)
    model = P(("grp", "depth"), "lat", "shot")
    placed = (
        fields,
        fields,
        fields,
        fields,
        model,
        P(("grp", "depth"), "lat", None),
        P(("grp", "shot"), None),
        P(("grp", "shot")),
        P(("grp", "shot"), None),
        P(("grp", "shot"), None, None),
    )

    return jax.shard_map(
        shards,
        mesh=mesh,
        in_specs=placed,
        out_specs=(model, model),
        check_vma=False,
    )
```
